32 devices in a mesh: ctx: 8 (over y, x, core), shard: 4 (over z).
Axes of the slice: x: 2, y: 2, z: 4, core: 2. Of those that a mesh axis runs over, the one named last changes fastest.
Arguments:
- inputs: bfloat16 [4, 3072, 768], P('shard', 'ctx'), may hold values from -6 to 6
- out_grad: bfloat16 [4, 3072, 768], P('shard', 'ctx'), may hold values from -6 to 6
- segment_ids: int32 [4, 3072], P('shard'), may hold values from 0 to 12, as said below
- doc_starts: int32 [4, 3072], P('shard'), may hold values from 0 to 3071, as said below
- deal_table: int32 [16], replicated, may hold values from 0 to 15, as said below
- ridge_matrix: float32 [3072, 256], P('ctx'), may hold values from -1.25 to 1.25
- first_gain: float32 [768], replicated, may hold values from 0.5 to 1.5
- first_shift: float32 [768], replicated, may hold values from -1.25 to 1.25
- mixer_in: bfloat16 [768, 2304], P('shard'), may hold values from -0.21875 to 0.21875
- query_bias: float32 [768], replicated, may hold values from -1.25 to 1.25
- value_bias: float32 [768], replicated, may hold values from -1.25 to 1.25
- mixer_out: bfloat16 [768, 768], P('shard'), may hold values from -0.4375 to 0.4375
- out_bias: float32 [768], replicated, may hold values from -1.25 to 1.25
- second_gain: float32 [768], replicated, may hold values from 0.5 to 1.5
- second_shift: float32 [768], replicated, may hold values from -1.25 to 1.25
- up_weight: bfloat16 [768, 3072], P('shard'), may hold values from -0.21875 to 0.21875
- up_bias: float32 [3072], replicated, may hold values from -1.25 to 1.25
- down_weight: bfloat16 [3072, 768], P('shard'), may hold values from -0.109375 to 0.109375
- down_bias: float32 [768], replicated, may hold values from -1.25 to 1.25
- memory_mean: float32 [12], replicated, may hold values from 0.1 to 0.9
- memory_spread: float32 [12], replicated, may hold values from 0.001 to 0.01
Outputs:
- result: float32 [4, 3072, 768], P('shard', 'ctx')
- input_grad: float32 [4, 3072, 768], P('shard', 'ctx')
- mixer_in_grad: float32 [768, 2304], P('shard')
- mixer_out_grad: float32 [768, 768], P('shard')
- up_weight_grad: float32 [768, 3072], P('shard')
- down_weight_grad: float32 [3072, 768], P('shard')
- first_gain_grad: float32 [768], replicated
- first_shift_grad: float32 [768], replicated
- query_bias_grad: float32 [768], replicated
- value_bias_grad: float32 [768], replicated
- out_bias_grad: float32 [768], replicated
- second_gain_grad: float32 [768], replicated
- second_shift_grad: float32 [768], replicated
- up_bias_grad: float32 [3072], replicated
- down_bias_grad: float32 [768], replicated
- memory_mean_grad: float32 [12], replicated
- memory_spread_grad: float32 [12], replicated
The draws below stay inside these ranges and needn't reach their ends.
Inputs may be any that keep to these rules, and one draw needn't show every extreme that they name: segment_ids is 0 at position 0, never falls, and rises by one exactly where a document begins. doc_starts at a position is the first position of its document. `deal_table`: each block number appears once; entries 2i and 2i + 1 sum to 15.
All inputs are finite; a program needn't handle non-finite values.
Results may differ from the reference program's by a relative error of at most 0.02.
Values may be sent and summed in bfloat16 or wider, within the bound.
No kernel may reach another device: no remote copies, remote signals or barrier semaphores. Data moves between devices by JAX's collectives and lax.ppermute only.
A program may use at most 192 MiB of HBM per device.

```python
import math
import jax
import jax.numpy as jnp
from jax import lax

D = 768
H = 12
HD = 64
FF = 3072
NB = 256
SEGL = 16
BL = 192
LEN = 3072
NBLK = 16
SEQS = 4


def document_layout(key):
    base_key = jax.random.fold_in(key, 7)
    key_cuts, key_centers, key_offsets = jax.random.split(base_key, 3)
    spread_count = LEN // 1024 + 1
    spread_cuts = jax.random.randint(key_cuts, (SEQS, spread_count), 1, LEN)
    centers = jax.random.randint(key_centers, (SEQS, 2, 1), 1, LEN)
    offsets = jax.random.randint(key_offsets, (SEQS, 2, 4), 0, 32)
    cluster = jnp.clip(centers + offsets, 1, LEN - 1).reshape(SEQS, 8)
    all_cuts = jnp.concatenate([spread_cuts, cluster], axis=1)
    flags = jnp.zeros((SEQS, LEN), jnp.int32).at[jnp.arange(SEQS)[:, None], all_cuts].set(1)
    segment = jnp.cumsum(flags, axis=1).astype(jnp.int32)
    marked = jnp.where(flags > 0, jnp.arange(LEN).astype(jnp.int32)[None, :], 0)
    starts = lax.cummax(marked, axis=1).astype(jnp.int32)
    return (segment, starts)


def draw_segment_ids(key, part):
    return document_layout(key)[0]


def draw_doc_starts(key, part):
    return document_layout(key)[1]


def draw_deal_table(key, part):
    base_key = jax.random.fold_in(key, 11)
    pair_key, flip_key = jax.random.split(base_key)
    pairs = NBLK // 2
    ordering = jax.random.permutation(pair_key, pairs)
    coins = jax.random.randint(flip_key, (pairs,), 0, 2)
    leading = jnp.where(coins == 1, NBLK - 1 - ordering, ordering)
    trailing = NBLK - 1 - leading
    return jnp.stack([leading, trailing], axis=1).reshape(NBLK).astype(jnp.int32)


def levels(own_key, dims, cuts, smallest, largest):
    def one(position, parts):
        heights = jax.random.uniform(jax.random.fold_in(jax.random.fold_in(own_key, 6), position), (parts,), jnp.float32, smallest / len(cuts), largest / len(cuts))
        return jnp.repeat(jnp.exp(heights), dims[position] // parts).reshape((-1,) + (1,) * (len(dims) - position - 1))

    level = one(*cuts[0])
    for cut in cuts[1:]:
        level = level * one(*cut)
    return level


def gaussian(stream_key, shape, width, most, shards=(), dtype=jnp.bfloat16):
    array = width * jax.random.normal(stream_key, shape, jnp.float32)
    if shards:
        array = array * levels(stream_key, shape, shards, -0.22, 0.18)
    return jnp.clip(array, -most, most).astype(dtype)


def setup_inputs(seed: int = 0) -> dict:
    key_of = jax.random.split(jax.random.key(seed), 22)
    inputs = gaussian(key_of[0], (SEQS, LEN, D), 1.0, 6.0, ((0, 4), (1, 8)))
    out_grad = gaussian(key_of[1], (SEQS, LEN, D), 1.0, 6.0, ((0, 4), (1, 8)))
    segment_ids = draw_segment_ids(jax.random.fold_in(key_of[21], 71), 0)
    doc_starts = draw_doc_starts(jax.random.fold_in(key_of[21], 71), 0)
    deal_table = draw_deal_table(jax.random.fold_in(key_of[21], 71), 0)
    ridge_matrix = gaussian(key_of[5], (LEN, NB), (max(LEN // 128, 1)) ** -0.5, 1.25, ((0, 8),), jnp.float32)
    first_gain = jnp.clip(1.0 + 0.1 * jax.random.normal(key_of[6], (D,), jnp.float32), 0.5, 1.5)
    first_shift = gaussian(key_of[7], (D,), 0.2, 1.25, (), jnp.float32)
    mixer_in = gaussian(key_of[8], (D, 3 * D), D ** -0.5, 0.21875, ((0, 4),))
    query_bias = gaussian(key_of[9], (D,), 0.2, 1.25, (), jnp.float32)
    value_bias = gaussian(key_of[10], (D,), 0.2, 1.25, (), jnp.float32)
    mixer_out = gaussian(key_of[11], (D, D), (D // 4) ** -0.5, 0.4375, ((0, 4),))
    out_bias = gaussian(key_of[12], (D,), 0.2, 1.25, (), jnp.float32)
    second_gain = jnp.clip(1.0 + 0.1 * jax.random.normal(key_of[13], (D,), jnp.float32), 0.5, 1.5)
    second_shift = gaussian(key_of[14], (D,), 0.2, 1.25, (), jnp.float32)
    up_weight = gaussian(key_of[15], (D, FF), D ** -0.5, 0.21875, ((0, 4),))
    up_bias = gaussian(key_of[16], (FF,), 0.2, 1.25, (), jnp.float32)
    down_weight = gaussian(key_of[17], (FF, D), FF ** -0.5, 0.109375, ((0, 4),))
    down_bias = gaussian(key_of[18], (D,), 0.2, 1.25, (), jnp.float32)
    memory_mean = jnp.clip(jax.random.uniform(key_of[19], (H,), jnp.float32, 0.1, 0.9), 0.1, 0.9)
    memory_spread = jnp.clip(jnp.exp(jax.random.uniform(key_of[20], (H,), jnp.float32, math.log(0.001), math.log(0.01))), 0.001, 0.01)
    return dict(inputs=inputs, out_grad=out_grad, segment_ids=segment_ids, doc_starts=doc_starts, deal_table=deal_table, ridge_matrix=ridge_matrix, first_gain=first_gain, first_shift=first_shift, mixer_in=mixer_in, query_bias=query_bias, value_bias=value_bias, mixer_out=mixer_out, out_bias=out_bias, second_gain=second_gain, second_shift=second_shift, up_weight=up_weight, up_bias=up_bias, down_weight=down_weight, down_bias=down_bias, memory_mean=memory_mean, memory_spread=memory_spread)


HIGH = lax.Precision.HIGHEST
EPS = 1e-05

@jax.custom_vjp
def low(v):
    return lax.optimization_barrier(v.astype(jnp.bfloat16)).astype(jnp.float32)

@jax.custom_vjp
def low_back(v):
    return v

def low_keep(v):
    return (low(v), None)

def low_pass(kept, grad):
    return (grad,)

def back_keep(v):
    return (v, None)

def back_low(kept, grad):
    return (low(grad),)
low.defvjp(low_keep, low_pass)
low_back.defvjp(back_keep, back_low)

def layer_norm(values, gain, shift):
    center = values - lax.optimization_barrier(jnp.mean(values, axis=-1, keepdims=True))
    spread = lax.optimization_barrier(jnp.mean(center * center, axis=-1, keepdims=True))
    return center * lax.rsqrt(spread + EPS) * gain + shift

def gelu(values):
    return 0.5 * values * (1.0 + jnp.tanh(0.7978845608028654 * (values + 0.044715 * values * values * values)))

def basis_weights(memory_mean, memory_spread):
    centers = (jnp.arange(NB).astype(jnp.float32) + 0.5) / NB
    widths = memory_spread[:, None] + 1.0 / (NB * NB)
    offset = memory_mean[:, None] - centers[None, :]
    return jnp.exp(-0.5 * offset * offset / widths) * lax.rsqrt(2.0 * math.pi * widths) / NB

def sequence(values, seg, start, pos, ridge, params):
    first_gain, first_shift, mixer_in, query_bias, value_bias, mixer_out, out_bias, second_gain, second_shift, up_weight, up_bias, down_weight, down_bias, memory_mean, memory_spread = params
    scale = HD ** (-0.5)
    qblock = math.gcd(LEN, 512)
    normed = low(layer_norm(values, first_gain, first_shift))
    mixed = jnp.dot(normed, mixer_in, precision=HIGH)
    query = low_back(low(mixed[:, :D] + query_bias))
    keys = low_back(low(mixed[:, D:2 * D]))
    vals = low_back(low(mixed[:, 2 * D:] + value_bias))
    wbasis = basis_weights(memory_mean, memory_spread)
    coef = low_back(low(jnp.dot(ridge, wbasis.T, precision=HIGH)))
    key_heads = keys.reshape(LEN, H, HD)
    val_heads = vals.reshape(LEN, H, HD)
    coef_rows = coef.T
    mem_pos = (pos - start) // SEGL

    def block(items):
        qblk, pblk, sblk, mblk = items
        scores = low_back(jnp.einsum('qhd,khd->hqk', qblk, key_heads, precision=HIGH) * scale)
        same = sblk[:, None] == seg[None, :]
        visible = same & (pos[None, :] <= pblk[:, None])
        probs = jnp.where(visible[None], jnp.exp(scores), 0.0)
        total = lax.optimization_barrier(jnp.sum(probs, axis=-1))
        numer = low_back(jnp.einsum('hqk,khd->qhd', low(probs), val_heads, precision=HIGH))
        attended = numer / total.T[:, :, None]
        earlier = same & (mem_pos[None, :] < mblk[:, None])
        mweights = jnp.where(earlier[None], coef_rows[:, None, :], 0.0)
        memory = low_back(jnp.einsum('hqk,khd->qhd', mweights, val_heads, precision=HIGH))
        return (attended + memory).reshape(qblock, D)
    count = LEN // qblock
    comb = lax.map(jax.checkpoint(block), (query.reshape(count, qblock, H, HD), pos.reshape(count, qblock), seg.reshape(count, qblock), mem_pos.reshape(count, qblock)))
    comb = low(comb.reshape(LEN, D))
    proj = low_back(jnp.dot(comb, mixer_out, precision=HIGH) + out_bias)
    resid = values + proj
    second = low(layer_norm(resid, second_gain, second_shift))
    hidden = low_back(jnp.dot(second, up_weight, precision=HIGH) + up_bias)
    act = low(gelu(hidden))
    down = low_back(jnp.dot(act, down_weight, precision=HIGH) + down_bias)
    return resid + down

def reference(inputs, out_grad, segment_ids, doc_starts, deal_table, ridge_matrix, first_gain, first_shift, mixer_in, query_bias, value_bias, mixer_out, out_bias, second_gain, second_shift, up_weight, up_bias, down_weight, down_bias, memory_mean, memory_spread):
    pos = (deal_table[:, None] * BL + jnp.arange(BL).astype(jnp.int32)[None, :]).reshape(LEN).astype(jnp.int32)
    seg_rows = segment_ids[:, pos]
    start_rows = doc_starts[:, pos]
    params = (first_gain, first_shift, mixer_in.astype(jnp.float32), query_bias, value_bias, mixer_out.astype(jnp.float32), out_bias, second_gain, second_shift, up_weight.astype(jnp.float32), up_bias, down_weight.astype(jnp.float32), down_bias, memory_mean, memory_spread)

    def forward(values, params):

        def one(carry, items):
            rows, seg, start = items
            return (carry, sequence(rows, seg, start, pos, ridge_matrix, params))
        _, outputs = lax.scan(one, jnp.zeros((), jnp.float32), (values, seg_rows, start_rows))
        return outputs
    result, pull = jax.vjp(forward, inputs.astype(jnp.float32), params)
    input_grad, grads = pull(out_grad.astype(jnp.float32))
    g_first_gain, g_first_shift, g_mixer_in, g_query_bias, g_value_bias, g_mixer_out, g_out_bias, g_second_gain, g_second_shift, g_up_weight, g_up_bias, g_down_weight, g_down_bias, g_mean, g_spread = grads
    return (result, input_grad, g_mixer_in, g_mixer_out, g_up_weight, g_down_weight, g_first_gain, g_first_shift, g_query_bias, g_value_bias, g_out_bias, g_second_gain, g_second_shift, g_up_bias, g_down_bias, g_mean, g_spread)
```

```python
import functools
import math

import jax
import jax.numpy as jnp
from jax import lax
from jax.experimental import pallas as pl
from jax.experimental.pallas import tpu as pltpu
from jax.sharding import PartitionSpec as P

D = 768
H = 12
HD = 64
NB = 256
SEGL = 16

HIGH = lax.Precision.HIGHEST
EPS = 1e-05
BF = jnp.bfloat16
F32 = jnp.float32
KT = 256
NN = (((1,), (0,)), ((), ()))
NT = (((1,), (1,)), ((), ()))
TN = (((0,), (0,)), ((), ()))


def mm(a, b, dims=NN):
    return lax.dot_general(a, b, dims, preferred_element_type=F32)


def norm_stats(values):
    center = values - jnp.mean(values, axis=-1, keepdims=True)
    spread = jnp.mean(center * center, axis=-1, keepdims=True)
    recip = lax.rsqrt(spread + EPS)
    return center * recip, recip


def norm_back(upstream, unit, recip, gain):
    scaled = upstream * gain
    return recip * (
        scaled
        - jnp.mean(scaled, axis=-1, keepdims=True)
        - unit * jnp.mean(scaled * unit, axis=-1, keepdims=True)
    )


def basis_weights(memory_mean, memory_spread):
    centers = (jnp.arange(NB).astype(F32) + 0.5) / NB
    widths = memory_spread[:, None] + 1.0 / (NB * NB)
    offset = memory_mean[:, None] - centers[None, :]
    return jnp.exp(-0.5 * offset * offset / widths) * lax.rsqrt(2.0 * math.pi * widths) / NB


def swap(x, axis, count, k):
    return lax.ppermute(x, axis, [(i, i ^ k) for i in range(count)])


def swap_gather(x, axis, count):
    me = lax.axis_index(axis)
    out = jnp.zeros((count,) + x.shape, x.dtype)
    for k in range(count):
        piece = x if k == 0 else swap(x, axis, count, k)
        out = lax.dynamic_update_index_in_dim(out, piece, me ^ k, 0)
    return out


def lane_iota(rows, cols):
    return lax.broadcasted_iota(jnp.int32, (rows, cols), 1)


def row_iota(rows, cols):
    return lax.broadcasted_iota(jnp.int32, (rows, cols), 0)


def head_mask(rows, cols, head):
    lane = lane_iota(rows, cols)
    return (lane >= head * HD) & (lane < (head + 1) * HD)


def load_blocks(geo, bpos, dealt, qkv, others, cexp, q_s, k_s, v_s, c_s, sems):
    blk, lw, own, pad = geo["blk"], geo["lw"], geo["own"], KT
    for ref in (k_s, v_s, c_s):
        ref[0:pad, :] = jnp.zeros((pad, lw), BF)
    copies = [pltpu.make_async_copy(qkv.at[:, pl.ds(0, lw)], q_s, sems.at[0])]
    for n in range(geo["nblk"]):
        source, off = (qkv, lw) if n < own else (others.at[n // own - 1], 0)
        rows = pl.ds((n % own) * blk, blk)
        to = pl.ds(pl.multiple_of(pad + bpos[n] * blk, 64), blk)
        for j, ref in enumerate((k_s, v_s)):
            copies.append(
                pltpu.make_async_copy(
                    source.at[rows, pl.ds(off + j * lw, lw)], ref.at[to], sems.at[1 + 3 * n + j]
                )
            )
        copies.append(
            pltpu.make_async_copy(
                cexp.at[pl.ds(pl.multiple_of(dealt[n] * blk, 64), blk)],
                c_s.at[to],
                sems.at[3 + 3 * n],
            )
        )
    for copy in copies:
        copy.start()
    for copy in copies:
        copy.wait()


def attn_fwd_kernel(geo, bpos, dealt, first, qkv, others, cexp, scol, comb, att, *scratch):
    q_s, k_s, v_s, c_s, acc, mac, sems = scratch
    blk, lw, gw, hpg, own, pad = (geo[k] for k in ("blk", "lw", "gw", "hpg", "own", "pad"))
    load_blocks(geo, bpos, dealt, qkv, others, cexp, q_s, k_s, v_s, c_s, sems)

    @pl.loop(0, geo["seq"] // KT)
    def _(i):
        rows = pl.ds(pl.multiple_of(pad + i * KT, KT), KT)
        c_s[rows, :] = (c_s[rows, :].astype(F32) * v_s[rows, :].astype(F32)).astype(BF)

    @pl.loop(0, own)
    def _(n):
        p = bpos[n]
        end = (p + 1) * blk
        mine = pl.ds(pl.multiple_of(n * blk, blk), blk)
        qb = q_s[mine, :].astype(F32) * (HD**-0.5)
        qm = [jnp.where(head_mask(blk, lw, h), qb, 0.0).astype(BF) for h in range(hpg)]
        part = scol[pl.ds(pl.multiple_of(p * blk, blk), blk), :]
        qstart = jnp.concatenate([part] * (KT // 128), axis=1)
        qpos = p * blk + row_iota(blk, KT)
        qlim = qpos - ((qpos - qstart) & (SEGL - 1))
        acc[...] = jnp.zeros_like(acc)
        mac[...] = jnp.zeros_like(mac)

        @pl.loop(0, (end - first[n] + KT - 1) // KT)
        def _(t):
            base = end - (t + 1) * KT
            rows = pl.ds(pl.multiple_of(pad + base, 64), KT)
            kt, vt, ct = k_s[rows, :], v_s[rows, :], c_s[rows, :]
            kpos = base + lane_iota(blk, KT)
            inside = kpos >= qstart
            visible = inside & (kpos <= qpos)
            earlier = inside & (kpos < qlim)
            for h in range(hpg):
                scores = mm(qm[h], kt, NT)
                probs = jnp.where(visible, jnp.exp(scores), 0.0).astype(BF)
                acc[h] += mm(probs, vt)
            mac[...] += mm(jnp.where(earlier, 1.0, 0.0).astype(BF), ct)

        attended = jnp.zeros((blk, lw), F32)
        for h in range(hpg):
            total = acc[h, :, gw : gw + 1]
            attended = jnp.where(head_mask(blk, lw, h), acc[h] / total, attended)
            attended = jnp.where(lane_iota(blk, lw) == gw + h, total, attended)
        att[mine, :] = attended
        comb[mine, :] = (attended + mac[...])[:, :gw].astype(BF)


def attn_bwd_kernel(geo, bpos, dealt, first, qkv, others, cexp, srow, dcomb, att, dq, dkv, *scratch):
    q_s, k_s, v_s, c_s, dq_a, dk_a, dv_a, r_a, sems = scratch
    blk, lw, gw, hpg, own, pad = (geo[k] for k in ("blk", "lw", "gw", "hpg", "own", "pad"))
    load_blocks(geo, bpos, dealt, qkv, others, cexp, q_s, k_s, v_s, c_s, sems)
    scale = HD**-0.5

    @pl.loop(0, (geo["seq"] + pad) // KT)
    def _(i):
        rows = pl.ds(pl.multiple_of(i * KT, KT), KT)
        for ref in (dk_a, dv_a, r_a):
            ref[rows, :] = jnp.zeros((KT, lw), F32)

    @pl.loop(0, own)
    def _(n):
        p = bpos[n]
        end = (p + 1) * blk
        mine = pl.ds(pl.multiple_of(n * blk, blk), blk)
        qb = q_s[mine, :].astype(F32) * scale
        qm = [jnp.where(head_mask(blk, lw, h), qb, 0.0).astype(BF) for h in range(hpg)]
        grad = jnp.concatenate([dcomb[mine, :], jnp.zeros((blk, lw - gw), BF)], axis=1)
        wide = grad.astype(F32)
        saved = att[mine, :]
        prod = wide * saved
        lane = lane_iota(blk, lw)
        dn = []
        for h in range(hpg):
            recip = 1.0 / saved[:, gw + h : gw + h + 1]
            only = head_mask(blk, lw, h)
            dtot = -jnp.sum(jnp.where(only, prod, 0.0), axis=1, keepdims=True) * recip
            high = dtot.astype(BF).astype(F32)
            aug = jnp.where(only, wide * recip, 0.0)
            aug = jnp.where(lane == gw, high, aug)
            aug = jnp.where(lane == gw + 1, dtot - high, aug)
            dn.append(aug.astype(BF))
        qstart = jnp.broadcast_to(srow[p], (KT, blk))
        qpos = p * blk + lane_iota(KT, blk)
        qlim = qpos - ((qpos - qstart) & (SEGL - 1))
        dq_a[...] = jnp.zeros_like(dq_a)

        @pl.loop(0, (end - first[n] + KT - 1) // KT)
        def _(t):
            base = end - (t + 1) * KT
            rows = pl.ds(pl.multiple_of(pad + base, 64), KT)
            kt, vt = k_s[rows, :], v_s[rows, :]
            kpos = base + row_iota(KT, blk)
            inside = kpos >= qstart
            visible = inside & (kpos <= qpos)
            earlier = inside & (kpos < qlim)
            for h in range(hpg):
                probs = jnp.where(visible, jnp.exp(mm(kt, qm[h], NT)), 0.0)
                dscore = (probs * mm(vt, dn[h], NT)).astype(BF)
                dv_a[rows, :] += mm(probs.astype(BF), dn[h])
                dk_a[rows, :] += mm(dscore, qm[h])
                dq_a[h] += mm(dscore, kt, TN)
            r_a[rows, :] += mm(jnp.where(earlier, 1.0, 0.0).astype(BF), grad)

        dquery = jnp.zeros((blk, lw), F32)
        for h in range(hpg):
            dquery = jnp.where(head_mask(blk, lw, h), dq_a[h] * scale, dquery)
        dq[mine, :] = dquery.astype(BF)

    for n in range(geo["nblk"]):
        rows = pl.ds(pl.multiple_of(pad + bpos[n] * blk, 64), blk)
        out = pl.ds((n % own) * blk, blk)
        reach = r_a[rows, :]
        value = v_s[rows, :].astype(F32)
        lane = lane_iota(blk, lw)
        dval = dv_a[rows, :] + reach * c_s[rows, :].astype(F32)
        dval = jnp.where(lane < gw, dval, 0.0)
        prod = reach * value
        for h in range(hpg):
            part = jnp.sum(jnp.where(head_mask(blk, lw, h), prod, 0.0), axis=1, keepdims=True)
            dval = jnp.where(lane == gw + h, part, dval)
        dkv[n // own, out, 0:lw] = dk_a[rows, :].astype(BF)
        dkv[n // own, out, lw : 2 * lw] = dval.astype(BF)


def ffn_kernel(
    geo, group, comb, wout, x, g, vecs, wup, upb, wdn,
    result, dresid, dcomb, dwup, dwdn, dwout, small, dupb,
    resid_s, unit_s, n2_s, n2t_s, y_s, dn2_s, recip_s,
):
    j = pl.program_id(0)
    groups, gw, tok = geo["groups"], geo["gw"], geo["tok"]

    @pl.when(j == 0)
    def _():
        proj = jnp.zeros((tok, D), F32)
        for k in range(groups):
            proj += mm(comb[k], wout[group[0] ^ k])
        resid = x[...].astype(F32) + proj + vecs[0:1, :]
        unit, recip = norm_stats(resid)
        n2 = (unit * vecs[1:2, :] + vecs[2:3, :]).astype(BF)
        resid_s[...] = resid
        unit_s[...] = unit
        recip_s[...] = jnp.broadcast_to(recip, (tok, 128))
        n2_s[...] = n2
        n2t_s[...] = n2.T
        y_s[...] = jnp.zeros_like(y_s)
        dn2_s[...] = jnp.zeros_like(dn2_s)

    up = wup[0]
    down = wdn[0]
    grad = g[...]
    u = mm(n2_s[...], up) + upb[0]
    sq = u * u
    th = jnp.tanh(0.7978845608028654 * (u + 0.044715 * sq * u))
    half = 0.5 * (1.0 + th)
    act = (u * half).astype(BF)
    slope = half + 0.5 * u * (1.0 - th * th) * (0.7978845608028654 * (1.0 + 3.0 * 0.044715 * sq))
    y_s[...] += mm(act, down)
    dwdn[0] = mm(act, grad, TN).astype(BF)
    dhid = (slope * mm(grad, down, NT)).astype(BF)
    dupb[0] = jnp.sum(dhid.astype(F32), axis=0, keepdims=True)
    dwup[0] = mm(n2t_s[...], dhid).astype(BF)
    dn2_s[...] += mm(dhid, up, NT)

    @pl.when(j == pl.num_programs(0) - 1)
    def _():
        result[...] = resid_s[...] + y_s[...] + vecs[3:4, :]
        wide = g[...].astype(F32)
        dn2 = dn2_s[...]
        unit = unit_s[...]
        dres = wide + norm_back(dn2, unit, recip_s[:, 0:1], vecs[1:2, :])
        dresid[...] = dres
        dproj = dres.astype(BF)
        small[0:1, :] = jnp.sum(dn2 * unit, axis=0, keepdims=True)
        small[1:2, :] = jnp.sum(dn2, axis=0, keepdims=True)
        small[2:3, :] = jnp.sum(dproj.astype(F32), axis=0, keepdims=True)
        small[3:4, :] = jnp.sum(wide, axis=0, keepdims=True)
        small[4:8, :] = jnp.zeros((4, D), F32)
        for k in range(groups):
            dwout[group[0] ^ k] = mm(comb[k], dproj, TN).astype(BF)
            dcomb[k] = mm(dproj, wout[group[0] ^ k], NT).astype(BF)


def tail_kernel(geo, group, recv, win, x, dresid, vecs, grad, small, acc):
    k = pl.program_id(0)

    @pl.when(k == 0)
    def _():
        acc[...] = jnp.zeros_like(acc)

    acc[...] += mm(recv[0], win[...], NT)

    @pl.when(k == pl.num_programs(0) - 1)
    def _():
        unit, recip = norm_stats(x[...].astype(F32))
        dn1 = acc[...]
        grad[...] = dresid[...] + norm_back(dn1, unit, recip, vecs[0:1, :])
        small[0:1, :] = jnp.sum(dn1 * unit, axis=0, keepdims=True)
        small[1:2, :] = jnp.sum(dn1, axis=0, keepdims=True)
        small[2:8, :] = jnp.zeros((6, D), F32)


def full(shape):
    return pl.BlockSpec(shape, lambda *_: (0,) * len(shape))


ANY = pl.BlockSpec(memory_space=pl.ANY)


def call(kernel, geo, scalars, grid, ins, in_specs, outs, out_specs, scratch, flops, moved, exps=0):
    return pl.pallas_call(
        functools.partial(kernel, geo),
        grid_spec=pltpu.PrefetchScalarGridSpec(
            num_scalar_prefetch=len(scalars),
            grid=grid,
            in_specs=in_specs,
            out_specs=out_specs,
            scratch_shapes=scratch,
        ),
        out_shape=[jax.ShapeDtypeStruct(s, t) for s, t in outs],
        compiler_params=pltpu.CompilerParams(vmem_limit_bytes=56 << 20),
        cost_estimate=pl.CostEstimate(flops=flops, bytes_accessed=moved, transcendentals=exps),
    )(*scalars, *ins)


def per_device(
    inputs,
    out_grad,
    segment_ids,
    doc_starts,
    deal_table,
    ridge_matrix,
    first_gain,
    first_shift,
    mixer_in,
    query_bias,
    value_bias,
    mixer_out,
    out_bias,
    second_gain,
    second_shift,
    up_weight,
    up_bias,
    down_weight,
    down_bias,
    memory_mean,
    memory_spread,
):
    tok = inputs.shape[1]
    blk = tok // 2
    nctx, nsh = lax.axis_size("ctx"), lax.axis_size("shard")
    place = lax.axis_index("ctx")
    seq, nblk = tok * nctx, 2 * nctx
    groups = math.gcd(H, nctx)
    splits = nctx // groups
    hpg = H // groups
    gw = hpg * HD
    lw = -(-(gw + hpg) // 128) * 128
    own = 2 * groups
    group, split = place // splits, place % splits
    ff = up_weight.shape[1]
    fb = ff // nctx
    fz = fb // nsh
    rows = D // nsh
    qrows = groups * tok
    geo = dict(
        tok=tok, blk=blk, seq=seq, nblk=nblk, groups=groups, hpg=hpg, gw=gw, lw=lw, own=own, pad=KT
    )
    x = inputs[0]
    upstream = out_grad[0]

    unit, _ = norm_stats(x.astype(F32))
    first_b = (unit * first_gain + first_shift).astype(BF)
    pieces = [first_b] + [swap(first_b, "ctx", nctx, k * splits) for k in range(1, groups)]

    w_parts = mixer_in.reshape(rows, 3, groups, gw)
    w_mine = lax.dynamic_index_in_dim(w_parts, group, 2, keepdims=False)
    w_mine = jnp.pad(w_mine, ((0, 0), (0, 0), (0, lw - gw))).reshape(rows, 3 * lw)
    w_group = swap_gather(w_mine, "shard", nsh).reshape(D, 3 * lw)

    up_mine = lax.dynamic_index_in_dim(
        up_weight.reshape(rows, nsh, nctx, fz), place, 2, keepdims=False
    ).reshape(rows, fb)
    down_mine = lax.dynamic_index_in_dim(down_weight.reshape(nctx, fz, D), place, 0, keepdims=False)
    w_out = swap_gather(mixer_out, "shard", nsh).reshape(groups, gw, D)
    up_z = swap_gather(up_mine, "shard", nsh).reshape(D, fb)
    down_z = swap_gather(down_mine, "shard", nsh).reshape(fb, D)
    w_up = lax.all_gather(up_z, "ctx", axis=0)
    w_down = lax.all_gather(down_z, "ctx", axis=0)
    in_pad = jnp.pad(
        w_parts.transpose(0, 2, 1, 3), ((0, 0), (0, 0), (0, 0), (0, lw - gw))
    ).reshape(rows, groups * 3 * lw)
    sub = rows // nctx
    in_mine = lax.dynamic_slice_in_dim(in_pad, place * sub, sub)
    w_in = lax.all_gather(in_mine, ("shard", "ctx"), axis=0, tiled=True)

    coef = jnp.dot(
        ridge_matrix,
        basis_weights(memory_mean, memory_spread).T,
        precision=HIGH,
        preferred_element_type=F32,
    ).astype(BF)
    coef_all = lax.all_gather(coef, "ctx", axis=0, tiled=True)
    lanes = jnp.arange(lw)
    spread = (lanes[None, :] // HD + group * hpg == jnp.arange(H)[:, None]) & (lanes[None, :] < gw)
    cexp = jnp.dot(coef_all, spread.astype(BF), preferred_element_type=F32).astype(BF)

    offsets = jnp.arange(groups)[None, :] * splits + jnp.arange(splits)[:, None]
    dealt = (2 * (place ^ offsets)[:, :, None] + jnp.arange(2)).reshape(nblk).astype(jnp.int32)
    pick = dealt[:, None] == jnp.arange(nblk)[None, :]
    bpos = jnp.sum(jnp.where(pick, deal_table[None, :], 0), axis=1).astype(jnp.int32)
    starts = doc_starts[0].astype(jnp.int32)
    lead = starts.reshape(nblk, blk)[:, 0]
    first = jnp.sum(
        jnp.where(bpos[:own, None] == jnp.arange(nblk)[None, :], lead[None, :], 0), axis=1
    ).astype(jnp.int32)
    scol = jnp.broadcast_to(starts[:, None], (seq, 128))
    srow = starts.reshape(nblk, 1, blk)

    lane_pad = lambda v: jnp.pad(
        lax.dynamic_slice_in_dim(v, group * gw, gw), (0, lw - gw)
    )
    ones = ((lanes >= gw) & (lanes < gw + 2)).astype(F32)
    bias = jnp.concatenate(
        [lane_pad(query_bias), jnp.zeros((lw,), F32), lane_pad(value_bias) + ones]
    )
    first_cat = jnp.concatenate(pieces, axis=0)
    qkv = (jnp.dot(first_cat, w_group, preferred_element_type=F32) + bias).astype(BF)
    kv = qkv[:, lw:]
    others = jnp.stack([swap(kv, "ctx", nctx, m) for m in range(1, splits)])

    vm = pltpu.VMEM
    blocks = [
        vm((qrows, lw), BF),
        vm((seq + KT, lw), BF),
        vm((seq + KT, lw), BF),
        vm((seq + KT, lw), BF),
    ]
    sems = pltpu.SemaphoreType.DMA((1 + 3 * nblk,))
    tiles = qrows * seq // 2
    moved = (3 * qrows + 3 * seq) * lw * 2
    comb, att = call(
        attn_fwd_kernel, geo, (bpos, dealt, first), (1,),
        (qkv, others, cexp, scol),
        [ANY, ANY, ANY, full((seq, 128))],
        [((qrows, gw), BF), ((qrows, lw), F32)],
        [full((qrows, gw)), full((qrows, lw))],
        blocks + [vm((hpg, blk, lw), F32), vm((blk, lw), F32), sems],
        tiles * lw * 2 * (2 * hpg + 1), moved, tiles * hpg,
    )
    comb = comb.reshape(groups, tok, gw)
    combs = jnp.stack(
        [comb[k] if k == 0 else swap(comb[k], "ctx", nctx, k * splits) for k in range(groups)]
    )

    vecs = jnp.concatenate(
        [jnp.stack([out_bias, second_gain, second_shift, down_bias]), jnp.zeros((4, D), F32)]
    )
    up_b = up_bias.reshape(nsh, nctx, fz).transpose(1, 0, 2).reshape(nctx, 1, fb)
    gidx = group.astype(jnp.int32).reshape(1)
    step = lambda shape: pl.BlockSpec((1,) + shape, lambda j, *_: (j, 0, 0))
    result, dresid, dcomb, dwup, dwdn, dwout, small2, dupb = call(
        ffn_kernel, geo, (gidx,), (nctx,),
        (combs, w_out, x, upstream, vecs, w_up, up_b, w_down),
        [full((groups, tok, gw)), full((groups, gw, D)), full((tok, D)), full((tok, D)),
         full((8, D)), step((D, fb)), step((1, fb)), step((fb, D))],
        [((tok, D), F32), ((tok, D), F32), ((groups, tok, gw), BF), ((nctx, D, fb), BF),
         ((nctx, fb, D), BF), ((groups, gw, D), BF), ((8, D), F32), ((nctx, 1, fb), F32)],
        [full((tok, D)), full((tok, D)), full((groups, tok, gw)), step((D, fb)),
         step((fb, D)), full((groups, gw, D)), full((8, D)), step((1, fb))],
        [vm((tok, D), F32), vm((tok, D), F32), vm((tok, D), BF), vm((D, tok), BF),
         vm((tok, D), F32), vm((tok, D), F32), vm((tok, 128), F32)],
        tok * D * (6 * ff + 3 * D) * 2, 8 * D * ff, tok * ff,
    )

    dcombs = jnp.concatenate(
        [dcomb[k] if k == 0 else swap(dcomb[k], "ctx", nctx, k * splits) for k in range(groups)]
    )
    wide = vm((seq + KT, lw), F32)
    dq, dkv = call(
        attn_bwd_kernel, geo, (bpos, dealt, first), (1,),
        (qkv, others, cexp, srow, dcombs, att),
        [ANY, ANY, ANY, full((nblk, 1, blk)), full((qrows, gw)), full((qrows, lw))],
        [((qrows, lw), BF), ((splits, qrows, 2 * lw), BF)],
        [full((qrows, lw)), full((splits, qrows, 2 * lw))],
        blocks + [vm((hpg, blk, lw), F32), wide, wide, wide, sems],
        tiles * lw * 2 * (5 * hpg + 1), moved, tiles * hpg,
    )
    dkv_sum = dkv[0].astype(F32)
    for m in range(1, splits):
        dkv_sum = dkv_sum + swap(dkv[m], "ctx", nctx, m).astype(F32)
    dqkv = jnp.concatenate([dq, dkv_sum.astype(BF)], axis=1)
    dpieces = dqkv.reshape(groups, tok, 3 * lw)
    recv = jnp.stack(
        [dpieces[k] if k == 0 else swap(dpieces[k], "ctx", nctx, k * splits) for k in range(groups)]
    )

    wg = jnp.einsum("td,te->de", first_cat, dqkv, preferred_element_type=F32).astype(BF)
    wg = wg.reshape(nsh, splits, rows // splits, 3 * lw)
    mine = lambda m: lax.dynamic_index_in_dim(wg, split ^ m, 1, keepdims=False)
    wsum = mine(0).astype(F32)
    for m in range(1, splits):
        wsum = wsum + swap(mine(m), "ctx", nctx, m).astype(F32)
    wsum = wsum.astype(BF)
    zplace = lax.axis_index("shard")
    zpart = lambda k: lax.dynamic_index_in_dim(wsum, zplace ^ k, 0, keepdims=False)
    zsum = zpart(0).astype(F32)
    for k in range(1, nsh):
        zsum = zsum + swap(zpart(k), "shard", nsh, k).astype(F32)
    zsum = zsum.astype(BF).reshape(rows // splits, 3, lw)[:, :, :gw]
    in_g = lax.all_gather(zsum, "ctx", axis=0)
    in_g = in_g.reshape(groups, splits, rows // splits, 3, gw).transpose(1, 2, 3, 0, 4)
    in_g = in_g.reshape(rows, 3 * D).astype(F32)

    vec1 = jnp.concatenate([first_gain[None], jnp.zeros((7, D), F32)])
    input_grad, small1 = call(
        tail_kernel, geo, (gidx,), (groups,),
        (recv, w_in, x, dresid, vec1),
        [step((tok, 3 * lw)), pl.BlockSpec((D, 3 * lw), lambda k, grp: (0, grp[0] ^ k)),
         full((tok, D)), full((tok, D)), full((8, D))],
        [((tok, D), F32), ((8, D), F32)],
        [full((tok, D)), full((8, D))],
        [vm((tok, D), F32)],
        tok * D * 3 * D * 2, 10 * D * D,
    )

    up_r = lax.psum_scatter(dwup, "ctx", scatter_dimension=0, tiled=False)
    down_r = lax.psum_scatter(dwdn, "ctx", scatter_dimension=0, tiled=False)
    up_r = lax.psum_scatter(up_r, "shard", scatter_dimension=0, tiled=True)
    down_r = lax.psum_scatter(down_r, "shard", scatter_dimension=0, tiled=True)
    up_g = lax.all_gather(up_r, "ctx", axis=0)
    down_g = lax.all_gather(down_r, "ctx", axis=0, tiled=True).astype(F32)
    up_g = up_g.reshape(nctx, rows, nsh, fz).transpose(1, 2, 0, 3).reshape(rows, ff).astype(F32)
    out_r = lax.psum_scatter(dwout.reshape(D, D), "shard", scatter_dimension=0, tiled=True)
    out_g = lax.psum(out_r, "ctx").astype(F32)

    colsum = jnp.sum(dqkv.astype(F32), axis=0).reshape(3, lw)[:, :gw]
    here = (jnp.arange(groups) == group).astype(F32)[:, None]
    query_b_g = (here * colsum[0][None]).reshape(D)
    value_b_g = (here * colsum[2][None]).reshape(D)
    up_b_g = dupb.reshape(nctx, nsh, fz).transpose(1, 0, 2).reshape(ff)
    dcoef = recv[:, :, 2 * lw + gw : 2 * lw + gw + hpg].astype(F32)
    parts = jnp.einsum("ktc,tj->kcj", dcoef, ridge_matrix, precision=HIGH)
    order = (jnp.arange(groups)[:, None] ^ group) == jnp.arange(groups)[None, :]
    dbasis = jnp.sum(jnp.where(order[:, :, None, None], parts[None], 0.0), axis=1).reshape(H, NB)
    _, basis_pull = jax.vjp(basis_weights, memory_mean, memory_spread)
    mean_g, spread_g = basis_pull(dbasis)
    small = lax.psum(
        (
            small1[0], small1[1], query_b_g, value_b_g, small2[2], small2[0], small2[1],
            up_b_g, small2[3], mean_g, spread_g,
        ),
        ("ctx", "shard"),
    )
    return (result[None], input_grad[None], in_g, out_g, up_g, down_g) + tuple(small)


def solution(mesh):
    rows, split = P("shard", None), P("shard", "ctx", None)
    none = P()
    return jax.shard_map(
        per_device,
        mesh=mesh,
        in_specs=(
            split, split, rows, rows, none, P("ctx", None), none, none, rows, none, none, rows,
            none, none, none, rows, none, rows, none, none, none,
        ),
        out_specs=(split, split, rows, rows, rows, rows) + (none,) * 11,
        check_vma=False,
    )
```

```python
import functools
import math

import jax
import jax.numpy as jnp
from jax import lax
from jax.experimental import pallas as pl
from jax.experimental.pallas import tpu as pltpu
from jax.sharding import PartitionSpec as P

D = 768
H = 12
HD = 64
NB = 256
SEGL = 16

HIGH = lax.Precision.HIGHEST
EPS = 1e-05
BF = jnp.bfloat16
F32 = jnp.float32
KT = 256
NN = (((1,), (0,)), ((), ()))
NT = (((1,), (1,)), ((), ()))
TN = (((0,), (0,)), ((), ()))


def mm(a, b, dims=NN):
    return lax.dot_general(a, b, dims, preferred_element_type=F32)


def norm_stats(values):
    center = values - jnp.mean(values, axis=-1, keepdims=True)
    spread = jnp.mean(center * center, axis=-1, keepdims=True)
    recip = lax.rsqrt(spread + EPS)
    return center * recip, recip


def norm_back(upstream, unit, recip, gain):
    scaled = upstream * gain
    return recip * (
        scaled
        - jnp.mean(scaled, axis=-1, keepdims=True)
        - unit * jnp.mean(scaled * unit, axis=-1, keepdims=True)
    )


def basis_weights(memory_mean, memory_spread):
    centers = (jnp.arange(NB).astype(F32) + 0.5) / NB
    widths = memory_spread[:, None] + 1.0 / (NB * NB)
    offset = memory_mean[:, None] - centers[None, :]
    return jnp.exp(-0.5 * offset * offset / widths) * lax.rsqrt(2.0 * math.pi * widths) / NB


def swap(x, axis, count, k):
    return lax.ppermute(x, axis, [(i, i ^ k) for i in range(count)])


def swap_gather(x, axis, count):
    me = lax.axis_index(axis)
    out = jnp.zeros((count,) + x.shape, x.dtype)
    for k in range(count):
        piece = x if k == 0 else swap(x, axis, count, k)
        out = lax.dynamic_update_index_in_dim(out, piece, me ^ k, 0)
    return out


def butterfly(x, sizes):
    for axis, count in sizes:
        k = 1
        while k < count:
            x = x + swap(x, axis, count, k)
            k *= 2
    return x


def lane_iota(rows, cols):
    return lax.broadcasted_iota(jnp.int32, (rows, cols), 1)


def row_iota(rows, cols):
    return lax.broadcasted_iota(jnp.int32, (rows, cols), 0)


def head_mask(rows, cols, head):
    lane = lane_iota(rows, cols)
    return (lane >= head * HD) & (lane < (head + 1) * HD)


def load_blocks(geo, bpos, dealt, kv, others, cexp, k_s, v_s, c_s, sems):
    blk, lw, own, pad = geo["blk"], geo["lw"], geo["own"], KT
    for ref in (k_s, v_s, c_s):
        ref[0:pad, :] = jnp.zeros((pad, lw), BF)
    copies = []
    for n in range(geo["nblk"]):
        source = kv if n < own else others[n // own - 1]
        rows = pl.ds((n % own) * blk, blk)
        to = pl.ds(pl.multiple_of(pad + bpos[n] * blk, 64), blk)
        for j, ref in enumerate((k_s, v_s)):
            copies.append(
                pltpu.make_async_copy(
                    source.at[rows, pl.ds(j * lw, lw)], ref.at[to], sems.at[3 * n + j]
                )
            )
        copies.append(
            pltpu.make_async_copy(
                cexp.at[pl.ds(pl.multiple_of(dealt[n] * blk, 64), blk)],
                c_s.at[to],
                sems.at[3 * n + 2],
            )
        )
    for copy in copies:
        copy.start()
    for copy in copies:
        copy.wait()


def attn_fwd_kernel(geo, bpos, dealt, first, *refs):
    splits, groups = geo["splits"], geo["groups"]
    q_s, kv, others, (cexp, scol) = refs[0], refs[1], refs[2 : splits + 1], refs[splits + 1 : splits + 3]
    combs, att = refs[splits + 3 : splits + 3 + groups], refs[splits + 3 + groups]
    k_s, v_s, c_s, comb_s, acc, mac, sems = refs[splits + 4 + groups :]
    blk, lw, gw, hpg, own, pad = (geo[k] for k in ("blk", "lw", "gw", "hpg", "own", "pad"))
    load_blocks(geo, bpos, dealt, kv, others, cexp, k_s, v_s, c_s, sems)

    @pl.loop(0, geo["seq"] // KT)
    def _(i):
        rows = pl.ds(pl.multiple_of(pad + i * KT, KT), KT)
        c_s[rows, :] = (c_s[rows, :].astype(F32) * v_s[rows, :].astype(F32)).astype(BF)

    @pl.loop(0, own)
    def _(n):
        p = bpos[n]
        end = (p + 1) * blk
        mine = pl.ds(pl.multiple_of(n * blk, blk), blk)
        qb = q_s[mine, :].astype(F32) * (HD**-0.5)
        qm = [jnp.where(head_mask(blk, lw, h), qb, 0.0).astype(BF) for h in range(hpg)]
        part = scol[pl.ds(pl.multiple_of(p * blk, blk), blk), :]
        qstart = jnp.concatenate([part] * (KT // 128), axis=1)
        qpos = p * blk + row_iota(blk, KT)
        qlim = qpos - ((qpos - qstart) & (SEGL - 1))
        acc[...] = jnp.zeros_like(acc)
        mac[...] = jnp.zeros_like(mac)

        @pl.loop(0, (end - first[n] + KT - 1) // KT)
        def _(t):
            base = end - (t + 1) * KT
            rows = pl.ds(pl.multiple_of(pad + base, 64), KT)
            kt, vt, ct = k_s[rows, :], v_s[rows, :], c_s[rows, :]
            kpos = base + lane_iota(blk, KT)
            inside = kpos >= qstart
            visible = inside & (kpos <= qpos)
            earlier = inside & (kpos < qlim)
            for h in range(hpg):
                scores = mm(qm[h], kt, NT)
                probs = jnp.where(visible, jnp.exp(scores), 0.0).astype(BF)
                acc[h] += mm(probs, vt)
            mac[...] += mm(jnp.where(earlier, 1.0, 0.0).astype(BF), ct)

        attended = jnp.zeros((blk, lw), F32)
        for h in range(hpg):
            total = acc[h, :, gw : gw + 1]
            attended = jnp.where(head_mask(blk, lw, h), acc[h] / total, attended)
            attended = jnp.where(lane_iota(blk, lw) == gw + h, total, attended)
        att[mine, :] = attended
        comb_s[mine, :] = (attended + mac[...]).astype(BF)

    for k in range(groups):
        combs[k][...] = comb_s[2 * k * blk : 2 * (k + 1) * blk, :gw]


def attn_bwd_kernel(geo, bpos, dealt, first, *refs):
    splits, groups, nblk = geo["splits"], geo["groups"], geo["nblk"]
    q_s, kv, others, (cexp, srow) = refs[0], refs[1], refs[2 : splits + 1], refs[splits + 1 : splits + 3]
    dcombs, att = refs[splits + 3 : splits + 3 + groups], refs[splits + 3 + groups]
    dq, dkvs = refs[splits + 4 + groups], refs[splits + 5 + groups : 2 * splits + 5 + groups]
    k_s, v_s, c_s, g_s, dq_a, dk_a, dv_a, r_a, sems = refs[2 * splits + 5 + groups :]
    blk, lw, gw, hpg, own, pad = (geo[k] for k in ("blk", "lw", "gw", "hpg", "own", "pad"))
    load_blocks(geo, bpos, dealt, kv, others, cexp, k_s, v_s, c_s, sems)
    scale = HD**-0.5
    for k in range(groups):
        rows = slice(2 * k * blk, 2 * (k + 1) * blk)
        g_s[rows, :] = jnp.concatenate([dcombs[k][...], jnp.zeros((2 * blk, lw - gw), BF)], axis=1)

    @pl.loop(0, (geo["seq"] + pad) // KT)
    def _(i):
        rows = pl.ds(pl.multiple_of(i * KT, KT), KT)
        for ref in (dk_a, dv_a, r_a):
            ref[rows, :] = jnp.zeros((KT, lw), F32)

    @pl.loop(0, own)
    def _(n):
        p = bpos[n]
        end = (p + 1) * blk
        mine = pl.ds(pl.multiple_of(n * blk, blk), blk)
        qb = q_s[mine, :].astype(F32) * scale
        qm = [jnp.where(head_mask(blk, lw, h), qb, 0.0).astype(BF) for h in range(hpg)]
        grad = g_s[mine, :]
        wide = grad.astype(F32)
        saved = att[mine, :]
        prod = wide * saved
        lane = lane_iota(blk, lw)
        dn = []
        for h in range(hpg):
            recip = 1.0 / saved[:, gw + h : gw + h + 1]
            only = head_mask(blk, lw, h)
            dtot = -jnp.sum(jnp.where(only, prod, 0.0), axis=1, keepdims=True) * recip
            high = dtot.astype(BF).astype(F32)
            aug = jnp.where(only, wide * recip, 0.0)
            aug = jnp.where(lane == gw, high, aug)
            aug = jnp.where(lane == gw + 1, dtot - high, aug)
            dn.append(aug.astype(BF))
        qstart = jnp.broadcast_to(srow[p], (KT, blk))
        qpos = p * blk + lane_iota(KT, blk)
        qlim = qpos - ((qpos - qstart) & (SEGL - 1))
        dq_a[...] = jnp.zeros_like(dq_a)

        @pl.loop(0, (end - first[n] + KT - 1) // KT)
        def _(t):
            base = end - (t + 1) * KT
            rows = pl.ds(pl.multiple_of(pad + base, 64), KT)
            kt, vt = k_s[rows, :], v_s[rows, :]
            kpos = base + row_iota(KT, blk)
            inside = kpos >= qstart
            visible = inside & (kpos <= qpos)
            earlier = inside & (kpos < qlim)
            for h in range(hpg):
                probs = jnp.where(visible, jnp.exp(mm(kt, qm[h], NT)), 0.0)
                dscore = (probs * mm(vt, dn[h], NT)).astype(BF)
                dv_a[rows, :] += mm(probs.astype(BF), dn[h])
                dk_a[rows, :] += mm(dscore, qm[h])
                dq_a[h] += mm(dscore, kt, TN)
            r_a[rows, :] += mm(jnp.where(earlier, 1.0, 0.0).astype(BF), grad)

        dquery = jnp.zeros((blk, lw), F32)
        for h in range(hpg):
            dquery = jnp.where(head_mask(blk, lw, h), dq_a[h] * scale, dquery)
        dq[mine, :] = dquery.astype(BF)

    for n in range(nblk):
        rows = pl.ds(pl.multiple_of(pad + bpos[n] * blk, 64), blk)
        out = slice((n % own) * blk, (n % own + 1) * blk)
        reach = r_a[rows, :]
        value = v_s[rows, :].astype(F32)
        lane = lane_iota(blk, lw)
        dval = dv_a[rows, :] + reach * c_s[rows, :].astype(F32)
        dval = jnp.where(lane < gw, dval, 0.0)
        prod = reach * value
        for h in range(hpg):
            part = jnp.sum(jnp.where(head_mask(blk, lw, h), prod, 0.0), axis=1, keepdims=True)
            dval = jnp.where(lane == gw + h, part, dval)
        dkvs[n // own][out, 0:lw] = dk_a[rows, :].astype(BF)
        dkvs[n // own][out, lw : 2 * lw] = dval.astype(BF)


def qkv_kernel(geo, *refs):
    groups, tok, lw = geo["groups"], geo["tok"], geo["lw"]
    pieces, w, bias, q, kv = refs[:groups], *refs[groups:]
    for k in range(groups):
        rows = slice(k * tok, (k + 1) * tok)
        out = (mm(pieces[k][...], w[...]) + bias[0:1, :]).astype(BF)
        q[rows, :] = out[:, :lw]
        kv[rows, :] = out[:, lw:]


def ffn_kernel(geo, group, *refs):
    groups, gw, tok, nsh, fz, fza, fb = (
        geo[k] for k in ("groups", "gw", "tok", "nsh", "fz", "fza", "fb")
    )
    combs = refs[:groups]
    wout, x, g, vecs, mup, mdn, upb = refs[groups : groups + 7]
    result, dresid = refs[groups + 7 : groups + 9]
    dcombs = refs[groups + 9 : 2 * groups + 9]
    dm, dwout, small, dupb = refs[2 * groups + 9 : 2 * groups + 13]
    resid_s, unit_s, n2_s, n2t_s, y_s, dn2_s, recip_s, up_s, dn_s = refs[2 * groups + 13 :]
    j = pl.program_id(0)
    rows = D // nsh

    @pl.when(j == 0)
    def _():
        proj = jnp.zeros((tok, D), F32)
        for k in range(groups):
            proj += mm(combs[k][...], wout[group[0] ^ k])
        resid = x[...].astype(F32) + proj + vecs[0:1, :]
        unit, recip = norm_stats(resid)
        n2 = (unit * vecs[1:2, :] + vecs[2:3, :]).astype(BF)
        resid_s[...] = resid
        unit_s[...] = unit
        recip_s[...] = jnp.broadcast_to(recip, (tok, 128))
        n2_s[...] = n2
        n2t_s[...] = n2.T
        y_s[...] = jnp.zeros_like(y_s)
        dn2_s[...] = jnp.zeros_like(dn2_s)

    for z in range(nsh):
        for q in range(D // fb):
            at = z * rows + q * fz
            up_s[at : at + fz, :] = mup[z, 0, 0:fz, q * fb : (q + 1) * fb].astype(up_s.dtype)
        dn_s[z * fz : (z + 1) * fz, :] = mdn[z, 0, 0:fz, :].astype(dn_s.dtype)
    up = up_s[...].astype(BF)
    down = dn_s[...].astype(BF)
    grad = g[...]
    u = mm(n2_s[...], up) + upb[0]
    sq = u * u
    th = jnp.tanh(0.7978845608028654 * (u + 0.044715 * sq * u))
    half = 0.5 * (1.0 + th)
    act = (u * half).astype(BF)
    slope = half + 0.5 * u * (1.0 - th * th) * (0.7978845608028654 * (1.0 + 3.0 * 0.044715 * sq))
    y_s[...] += mm(act, down)
    dwdn = mm(act, grad, TN)
    dhid = (slope * mm(grad, down, NT)).astype(BF)
    dupb[0] = jnp.sum(dhid.astype(F32), axis=0, keepdims=True)
    dwup = mm(n2t_s[...], dhid)
    for z in range(nsh):
        for q in range(D // fb):
            at = z * rows + q * fz
            dm[0, z, 0:fz, q * fb : (q + 1) * fb] = dwup[at : at + fz, :].astype(BF)
        dm[0, z, fza : fza + fz, :] = dwdn[z * fz : (z + 1) * fz, :].astype(BF)
    dn2_s[...] += mm(dhid, up, NT)

    @pl.when(j == pl.num_programs(0) - 1)
    def _():
        result[...] = resid_s[...] + y_s[...] + vecs[3:4, :]
        wide = g[...].astype(F32)
        dn2 = dn2_s[...]
        unit = unit_s[...]
        dres = wide + norm_back(dn2, unit, recip_s[:, 0:1], vecs[1:2, :])
        dresid[...] = dres
        dproj = dres.astype(BF)
        small[0:1, :] = jnp.sum(dn2 * unit, axis=0, keepdims=True)
        small[1:2, :] = jnp.sum(dn2, axis=0, keepdims=True)
        small[2:3, :] = jnp.sum(dproj.astype(F32), axis=0, keepdims=True)
        small[3:4, :] = jnp.sum(wide, axis=0, keepdims=True)
        small[4:8, :] = jnp.zeros((4, D), F32)
        for k in range(groups):
            dwout[group[0] ^ k] = mm(combs[k][...], dproj, TN).astype(BF)
            dcombs[k][...] = mm(dproj, wout[group[0] ^ k], NT).astype(BF)


def dn1_kernel(geo, *refs):
    splits, groups, tok, lw = geo["splits"], geo["groups"], geo["tok"], geo["lw"]
    dq, dkv, others, w = refs[0], refs[1], refs[2 : splits + 1], refs[splits + 1]
    dqkv, colsum = refs[splits + 2], refs[splits + 3]
    parts, coefs = refs[splits + 4 : splits + 4 + groups], refs[splits + 4 + groups :]
    total = jnp.zeros((1, 3 * lw), F32)
    for k in range(groups):
        rows = slice(k * tok, (k + 1) * tok)
        both = dkv[rows, :].astype(F32)
        for ref in others:
            both += ref[rows, :].astype(F32)
        dqkv[rows, 0:lw] = dq[rows, :]
        dqkv[rows, lw : 3 * lw] = both.astype(BF)
        piece = dqkv[rows, :]
        parts[k][...] = mm(piece, w[...], NT).astype(BF)
        coefs[k][...] = piece[:, 3 * lw - 128 :]
        total += jnp.sum(piece.astype(F32), axis=0, keepdims=True)
    colsum[...] = jnp.broadcast_to(total, colsum.shape)


def wgrad_kernel(geo, *refs):
    groups, tok, lw = geo["groups"], geo["tok"], geo["lw"]
    pieces, dqkv, out = refs[:groups], refs[groups], refs[groups + 1]
    acc = jnp.zeros((D, 3 * lw), F32)
    for k in range(groups):
        acc += mm(pieces[k][...], dqkv[k * tok : (k + 1) * tok, :], TN)
    out[...] = acc.astype(BF)


def tail_kernel(geo, *refs):
    groups = geo["groups"]
    parts = refs[:groups]
    x, dresid, vecs, grad, small = refs[groups:]
    dn1 = jnp.zeros((geo["tok"], D), F32)
    for ref in parts:
        dn1 += ref[...].astype(F32)
    unit, recip = norm_stats(x[...].astype(F32))
    grad[...] = dresid[...] + norm_back(dn1, unit, recip, vecs[0:1, :])
    small[0:1, :] = jnp.sum(dn1 * unit, axis=0, keepdims=True)
    small[1:2, :] = jnp.sum(dn1, axis=0, keepdims=True)
    small[2:8, :] = jnp.zeros((6, D), F32)


def finish_kernel(geo, up, down, up_g, down_g):
    nctx, nsh, fz, fb = (geo[k] for k in ("nctx", "nsh", "fz", "fb"))
    wide = geo["ff"] // nsh
    for i in range(nctx):
        for q in range(D // fb):
            part = up[i, 0:fz, q * fb : (q + 1) * fb].astype(F32)
            for z in range(nsh):
                at = z * wide + i * fz
                up_g[q * fz : (q + 1) * fz, at : at + fz] = part[:, z * fz : (z + 1) * fz]
        down_g[i * fz : (i + 1) * fz, :] = down[i, 0:fz, :].astype(F32)


def full(shape):
    return pl.BlockSpec(shape, lambda *_: (0,) * len(shape))


ANY = pl.BlockSpec(memory_space=pl.ANY)


def call(kernel, geo, scalars, grid, ins, in_specs, outs, out_specs, scratch, flops, moved, exps=0):
    return pl.pallas_call(
        functools.partial(kernel, geo),
        grid_spec=pltpu.PrefetchScalarGridSpec(
            num_scalar_prefetch=len(scalars),
            grid=grid,
            in_specs=in_specs,
            out_specs=out_specs,
            scratch_shapes=scratch,
        ),
        out_shape=[jax.ShapeDtypeStruct(s, t) for s, t in outs],
        compiler_params=pltpu.CompilerParams(vmem_limit_bytes=56 << 20),
        cost_estimate=pl.CostEstimate(flops=flops, bytes_accessed=moved, transcendentals=exps),
    )(*scalars, *ins)


def per_device(
    inputs,
    out_grad,
    segment_ids,
    doc_starts,
    deal_table,
    ridge_matrix,
    first_gain,
    first_shift,
    mixer_in,
    query_bias,
    value_bias,
    mixer_out,
    out_bias,
    second_gain,
    second_shift,
    up_weight,
    up_bias,
    down_weight,
    down_bias,
    memory_mean,
    memory_spread,
):
    tok = inputs.shape[1]
    blk = tok // 2
    nctx, nsh = lax.axis_size("ctx"), lax.axis_size("shard")
    place = lax.axis_index("ctx")
    seq, nblk = tok * nctx, 2 * nctx
    groups = math.gcd(H, nctx)
    splits = nctx // groups
    hpg = H // groups
    gw = hpg * HD
    lw = -(-(gw + hpg) // 128) * 128
    own = 2 * groups
    group, split = place // splits, place % splits
    ff = up_weight.shape[1]
    fb = ff // nctx
    fz = fb // nsh
    rows = D // nsh
    qrows = groups * tok
    sub = rows // nctx
    fza = -(-fz // 16) * 16
    pr = 2 * fza + sub
    geo = dict(
        tok=tok, blk=blk, seq=seq, nblk=nblk, groups=groups, splits=splits, hpg=hpg, gw=gw, lw=lw,
        own=own, pad=KT, nctx=nctx, nsh=nsh, ff=ff, fb=fb, fz=fz, fza=fza,
    )
    x = inputs[0]
    upstream = out_grad[0]
    peers = range(groups)
    across = lambda v, k: v if k == 0 else swap(v, "ctx", nctx, k * splits)
    inside = lambda v, m: swap(v, "ctx", nctx, m)

    unit, _ = norm_stats(x.astype(F32))
    first_b = (unit * first_gain + first_shift).astype(BF)
    pieces = [across(first_b, k) for k in peers]

    stack = D // fb
    up_mine = lax.dynamic_index_in_dim(
        up_weight.reshape(rows, nsh, nctx, fz), place, 2, keepdims=False
    )
    up_mine = up_mine.reshape(stack, fz, fb).transpose(1, 0, 2).reshape(fz, D)
    down_mine = lax.dynamic_index_in_dim(down_weight.reshape(nctx, fz, D), place, 0, keepdims=False)
    out_mine = lax.dynamic_index_in_dim(mixer_out.reshape(nctx, sub, D), place, 0, keepdims=False)
    fill = ((0, fza - fz), (0, 0))
    m_mine = jnp.concatenate([jnp.pad(up_mine, fill), jnp.pad(down_mine, fill), out_mine])
    m_all = lax.all_gather(m_mine, ("shard", "ctx"), axis=0).reshape(nsh, nctx, pr, D)
    w_out = m_all[:, :, 2 * fza :, :].reshape(groups, gw, D)

    part = rows // splits
    w_part = lax.dynamic_slice_in_dim(mixer_in, split * part, part).reshape(part, 3, groups, gw)
    w_mine = lax.dynamic_index_in_dim(w_part, group, 2, keepdims=False)
    w_mine = jnp.pad(w_mine, ((0, 0), (0, 0), (0, lw - gw))).reshape(part, 3 * lw)
    w_z = swap_gather(w_mine, "shard", nsh)
    w_group = jnp.zeros((nsh, splits, part, 3 * lw), BF)
    for m in range(splits):
        w_group = lax.dynamic_update_index_in_dim(
            w_group, w_z if m == 0 else inside(w_z, m), split ^ m, 1
        )
    w_group = w_group.reshape(D, 3 * lw)

    coef = jnp.dot(
        ridge_matrix,
        basis_weights(memory_mean, memory_spread).T,
        precision=HIGH,
        preferred_element_type=F32,
    ).astype(BF)
    coef_all = lax.all_gather(coef, "ctx", axis=0, tiled=True)
    lanes = jnp.arange(lw)
    spread = (lanes[None, :] // HD + group * hpg == jnp.arange(H)[:, None]) & (lanes[None, :] < gw)
    cexp = jnp.dot(coef_all, spread.astype(BF), preferred_element_type=F32).astype(BF)

    offsets = jnp.arange(groups)[None, :] * splits + jnp.arange(splits)[:, None]
    dealt = (2 * (place ^ offsets)[:, :, None] + jnp.arange(2)).reshape(nblk).astype(jnp.int32)
    pick = dealt[:, None] == jnp.arange(nblk)[None, :]
    bpos = jnp.sum(jnp.where(pick, deal_table[None, :], 0), axis=1).astype(jnp.int32)
    starts = doc_starts[0].astype(jnp.int32)
    lead = starts.reshape(nblk, blk)[:, 0]
    first = jnp.sum(
        jnp.where(bpos[:own, None] == jnp.arange(nblk)[None, :], lead[None, :], 0), axis=1
    ).astype(jnp.int32)
    scol = jnp.broadcast_to(starts[:, None], (seq, 128))
    srow = starts.reshape(nblk, 1, blk)

    lane_pad = lambda v: jnp.pad(lax.dynamic_slice_in_dim(v, group * gw, gw), (0, lw - gw))
    ones = ((lanes >= gw) & (lanes < gw + 2)).astype(F32)
    bias = jnp.concatenate(
        [lane_pad(query_bias), jnp.zeros((lw,), F32), lane_pad(value_bias) + ones]
    )
    bias = jnp.broadcast_to(bias[None], (8, 3 * lw))
    vm = pltpu.VMEM
    q, kv = call(
        qkv_kernel, geo, (), (1,), (*pieces, w_group, bias),
        [full((tok, D))] * groups + [full((D, 3 * lw)), full((8, 3 * lw))],
        [((qrows, lw), BF), ((qrows, 2 * lw), BF)],
        [full((qrows, lw)), full((qrows, 2 * lw))],
        [], qrows * D * 6 * lw, qrows * D * 4,
    )
    others = [inside(kv, m) for m in range(1, splits)]

    wide = (seq + KT, lw)
    blocks = [vm(wide, BF)] * 3
    sems = pltpu.SemaphoreType.DMA((3 * nblk,))
    tiles = qrows * seq // 2
    moved = (3 * qrows + 3 * seq) * lw * 2
    *combs, att = call(
        attn_fwd_kernel, geo, (bpos, dealt, first), (1,),
        (q, kv, *others, cexp, scol),
        [full((qrows, lw))] + [ANY] * (splits + 1) + [full((seq, 128))],
        [((tok, gw), BF)] * groups + [((qrows, lw), F32)],
        [full((tok, gw))] * groups + [full((qrows, lw))],
        blocks + [vm((qrows, lw), BF), vm((hpg, blk, lw), F32), vm((blk, lw), F32), sems],
        tiles * lw * 2 * (2 * hpg + 1), moved, tiles * hpg,
    )
    combs = [across(combs[k], k) for k in peers]

    vecs = jnp.concatenate(
        [jnp.stack([out_bias, second_gain, second_shift, down_bias]), jnp.zeros((4, D), F32)]
    )
    up_b = up_bias.reshape(nsh, nctx, fz).transpose(1, 0, 2).reshape(nctx, 1, fb)
    gidx = group.astype(jnp.int32).reshape(1)
    mblock = lambda r: pl.BlockSpec((nsh, 1, fza, D), lambda j, *_: (0, j, r, 0))
    wtype = BF if fz % 16 == 0 else F32
    result, dresid, *rest = call(
        ffn_kernel, geo, (gidx,), (nctx,),
        (*combs, w_out, x, upstream, vecs, m_all, m_all, up_b),
        [full((tok, gw))] * groups
        + [full((groups, gw, D)), full((tok, D)), full((tok, D)), full((8, D)),
           mblock(0), mblock(1), pl.BlockSpec((1, 1, fb), lambda j, *_: (j, 0, 0))],
        [((tok, D), F32), ((tok, D), F32)] + [((tok, gw), BF)] * groups
        + [((nctx, nsh, pr, D), BF), ((groups, gw, D), BF), ((8, D), F32), ((nctx, 1, fb), F32)],
        [full((tok, D)), full((tok, D))] + [full((tok, gw))] * groups
        + [pl.BlockSpec((1, nsh, 2 * fza, D), lambda j, *_: (j, 0, 0, 0)), full((groups, gw, D)),
           full((8, D)), pl.BlockSpec((1, 1, fb), lambda j, *_: (j, 0, 0))],
        [vm((tok, D), F32), vm((tok, D), F32), vm((tok, D), BF), vm((D, tok), BF),
         vm((tok, D), F32), vm((tok, D), F32), vm((tok, 128), F32), vm((D, fb), wtype),
         vm((fb, D), wtype)],
        tok * D * (6 * ff + 3 * D) * 2, 8 * D * ff, tok * ff,
    )
    dcombs, (dm, dwout, small2, dupb) = rest[:groups], rest[groups:]
    dwout = dwout.reshape(nsh, nctx, sub, D).transpose(1, 0, 2, 3)
    dm = lax.dynamic_update_slice(dm, dwout, (0, 0, 2 * fza, 0))
    dm_sum = lax.psum_scatter(dm, "ctx", scatter_dimension=0, tiled=False)

    dcombs = [across(dcombs[k], k) for k in peers]
    dq, *dkvs = call(
        attn_bwd_kernel, geo, (bpos, dealt, first), (1,),
        (q, kv, *others, cexp, srow, *dcombs, att),
        [full((qrows, lw))] + [ANY] * (splits + 1) + [full((nblk, 1, blk))]
        + [full((tok, gw))] * groups + [full((qrows, lw))],
        [((qrows, lw), BF)] + [((qrows, 2 * lw), BF)] * splits,
        [full((qrows, lw))] + [full((qrows, 2 * lw))] * splits,
        blocks + [vm((qrows, lw), BF), vm((hpg, blk, lw), F32), vm(wide, F32), vm(wide, F32),
                  vm(wide, F32), sems],
        tiles * lw * 2 * (5 * hpg + 1), moved, tiles * hpg,
    )
    dkvs = [dkvs[0]] + [inside(dkvs[m], m) for m in range(1, splits)]
    dqkv, colsum, *rest = call(
        dn1_kernel, geo, (), (1,), (dq, *dkvs, w_group),
        [full((qrows, lw))] + [full((qrows, 2 * lw))] * splits + [full((D, 3 * lw))],
        [((qrows, 3 * lw), BF), ((8, 3 * lw), F32)] + [((tok, D), BF)] * groups
        + [((tok, 128), BF)] * groups,
        [full((qrows, 3 * lw)), full((8, 3 * lw))] + [full((tok, D))] * groups
        + [full((tok, 128))] * groups,
        [], qrows * D * 6 * lw, qrows * D * 6,
    )
    parts = [across(rest[k], k) for k in peers]
    dcoef = jnp.stack([across(rest[groups + k], k) for k in peers])

    (wg,) = call(
        wgrad_kernel, geo, (), (1,), (*pieces, dqkv),
        [full((tok, D))] * groups + [full((qrows, 3 * lw))],
        [((D, 3 * lw), BF)], [full((D, 3 * lw))],
        [], qrows * D * 6 * lw, qrows * D * 4,
    )
    wg = wg.reshape(nsh, splits, part, 3 * lw)
    mine = lambda m: lax.dynamic_index_in_dim(wg, split ^ m, 1, keepdims=False)
    wsum = mine(0).astype(F32)
    for m in range(1, splits):
        wsum = wsum + inside(mine(m), m).astype(F32)
    wsum = wsum.astype(BF)
    zplace = lax.axis_index("shard")

    def zreduce(v):
        pick = lambda k: lax.dynamic_index_in_dim(v, zplace ^ k, 0, keepdims=False)
        total = pick(0).astype(F32)
        for k in range(1, nsh):
            total = total + swap(pick(k), "shard", nsh, k).astype(F32)
        return total.astype(BF)

    zsum = zreduce(wsum).reshape(part, 3, lw)[:, :, :gw]
    in_g = lax.all_gather(zsum, "ctx", axis=0)
    in_g = in_g.reshape(groups, splits, part, 3, gw).transpose(1, 2, 3, 0, 4)
    in_g = in_g.reshape(rows, 3 * D).astype(F32)

    vec1 = jnp.concatenate([first_gain[None], jnp.zeros((7, D), F32)])
    input_grad, small1 = call(
        tail_kernel, geo, (), (1,), (*parts, x, dresid, vec1),
        [full((tok, D))] * (groups + 2) + [full((8, D))],
        [((tok, D), F32), ((8, D), F32)],
        [full((tok, D)), full((8, D))],
        [], tok * D * 20, tok * D * 20,
    )

    dm_sum, wg, *parts = lax.optimization_barrier((dm_sum, wg, *parts))
    m_g = lax.all_gather(zreduce(dm_sum), "ctx", axis=0)
    out_g = m_g[:, 2 * fza :, :].reshape(rows, D).astype(F32)
    gblock = lambda r: pl.BlockSpec((nctx, fza, D), lambda j, *_: (0, r, 0))
    up_g, down_g = call(
        finish_kernel, geo, (), (1,), (m_g, m_g), [gblock(0), gblock(1)],
        [((rows, ff), F32), ((ff // nsh, D), F32)],
        [full((rows, ff)), full((ff // nsh, D))],
        [], 1000, rows * ff * 12,
    )

    colsum = colsum[0].reshape(3, lw)[:, :gw]
    here = (jnp.arange(groups) == group).astype(F32)[:, None]
    query_b_g = (here * colsum[0][None]).reshape(D)
    value_b_g = (here * colsum[2][None]).reshape(D)
    up_b_g = dupb.reshape(nctx, nsh, fz).transpose(1, 0, 2).reshape(ff)
    off = 128 - (lw - gw)
    dcoef = dcoef[:, :, off : off + hpg].astype(F32)
    dparts = jnp.einsum("ktc,tj->kcj", dcoef, ridge_matrix, precision=HIGH)
    order = (jnp.arange(groups)[:, None] ^ group) == jnp.arange(groups)[None, :]
    dbasis = jnp.sum(jnp.where(order[:, :, None, None], dparts[None], 0.0), axis=1).reshape(H, NB)
    _, basis_pull = jax.vjp(basis_weights, memory_mean, memory_spread)
    mean_g, spread_g = basis_pull(dbasis)
    axes = (("ctx", nctx), ("shard", nsh))
    early = jnp.concatenate([small2[:4].reshape(-1), up_b_g]).reshape(-1, 128)
    early = butterfly(early, axes).reshape(-1)
    late = jnp.concatenate(
        [small1[:2].reshape(-1), query_b_g, value_b_g, jnp.pad(mean_g, (0, 128 - H)),
         jnp.pad(spread_g, (0, 128 - H))]
    ).reshape(-1, 128)
    late = butterfly(late, axes).reshape(-1)
    ev = [early[i * D : (i + 1) * D] for i in range(4)]
    lv = [late[i * D : (i + 1) * D] for i in range(4)]
    small = (
        lv[0], lv[1], lv[2], lv[3], ev[2], ev[0], ev[1], early[4 * D :], ev[3],
        late[4 * D : 4 * D + H], late[4 * D + 128 : 4 * D + 128 + H],
    )
    return (result[None], input_grad[None], in_g, out_g, up_g, down_g) + small


def solution(mesh):
    rows, split = P("shard", None), P("shard", "ctx", None)
    none = P()
    return jax.shard_map(
        per_device,
        mesh=mesh,
        in_specs=(
            split, split, rows, rows, none, P("ctx", None), none, none, rows, none, none, rows,
            none, none, none, rows, none, rows, none, none, none,
        ),
        out_specs=(split, split, rows, rows, rows, rows) + (none,) * 11,
        check_vma=False,
    )
```

```python
import functools
import math

import jax
import jax.numpy as jnp
from jax import lax
from jax.experimental import pallas as pl
from jax.experimental.pallas import tpu as pltpu
from jax.sharding import PartitionSpec as P

D = 768
H = 12
HD = 64
NB = 256
SEGL = 16

HIGH = lax.Precision.HIGHEST
EPS = 1e-05
BF = jnp.bfloat16
F32 = jnp.float32
KT = 256
FB = 256
NN = (((1,), (0,)), ((), ()))
NT = (((1,), (1,)), ((), ()))
TN = (((0,), (0,)), ((), ()))


def mm(a, b, dims=NN):
    return lax.dot_general(a, b, dims, preferred_element_type=F32)


def norm_stats(values):
    center = values - jnp.mean(values, axis=-1, keepdims=True)
    spread = jnp.mean(center * center, axis=-1, keepdims=True)
    recip = lax.rsqrt(spread + EPS)
    return center * recip, recip


def norm_back(upstream, unit, recip, gain):
    scaled = upstream * gain
    return recip * (
        scaled
        - jnp.mean(scaled, axis=-1, keepdims=True)
        - unit * jnp.mean(scaled * unit, axis=-1, keepdims=True)
    )


def swap(x, axis, count, k):
    return lax.ppermute(x, axis, [(i, i ^ k) for i in range(count)])


def swap_gather(x, axis, count):
    me = lax.axis_index(axis)
    out = jnp.zeros((count,) + x.shape, x.dtype)
    for k in range(count):
        piece = x if k == 0 else swap(x, axis, count, k)
        out = lax.dynamic_update_index_in_dim(out, piece, me ^ k, 0)
    return out


def lane_iota(rows, cols):
    return lax.broadcasted_iota(jnp.int32, (rows, cols), 1)


def row_iota(rows, cols):
    return lax.broadcasted_iota(jnp.int32, (rows, cols), 0)


def head_mask(rows, cols, head):
    lane = lane_iota(rows, cols)
    return (lane >= head * HD) & (lane < (head + 1) * HD)


HP = 16
VR = 32


def pack(value):
    cut = value.shape[0] * 3 // 4
    last = [value[cut:, h * HD : (h + 1) * HD] for h in range(3)]
    return jnp.concatenate([value[:cut, :], jnp.concatenate(last, axis=0)], axis=1)


def unpack(value):
    each, gw = value.shape[0] // 3, 3 * HD
    last = [value[h * each : (h + 1) * each, gw:] for h in range(3)]
    return jnp.concatenate([value[:, :gw], jnp.concatenate(last, axis=1)], axis=0)


def coef_spread(lw, gw, hpg):
    row, lane = row_iota(lw, lw), lane_iota(lw, lw)
    hit = (row >= gw) & (row < gw + hpg) & (lane < gw)
    hit = hit & (lane >= (row - gw) * HD) & (lane < (row - gw + 1) * HD)
    return jnp.where(hit, 1.0, 0.0).astype(BF)


def block_at(geo, deal, place, n):
    own, splits = geo["own"], geo["splits"]
    device = place[0] ^ (((n % own) // 2) * splits + n // own)
    return deal[2 * device + n % 2]


def starts_of(ref, p, blk):
    at = pl.multiple_of((p * blk) // 128 * 128, 128)
    window = ref[:, pl.ds(at, blk + 64)]
    return jnp.where((p * blk) % 128 == 0, window[:, :blk], window[:, 64:])


def load_blocks(geo, deal, place, kv, others, k_s, v_s, sems):
    blk, lw, own, pad = geo["blk"], geo["lw"], geo["own"], KT
    for ref in (k_s, v_s):
        ref[0:pad, :] = jnp.zeros((pad, lw), BF)
    copies = []
    for n in range(geo["nblk"]):
        source = kv if n < own else others[n // own - 1]
        rows = pl.ds((n % own) * blk, blk)
        to = pl.ds(pl.multiple_of(pad + block_at(geo, deal, place, n) * blk, 64), blk)
        for j, ref in enumerate((k_s, v_s)):
            copies.append(
                pltpu.make_async_copy(
                    source.at[rows, pl.ds(j * lw, lw)], ref.at[to], sems.at[2 * n + j]
                )
            )
    for copy in copies:
        copy.start()
    for copy in copies:
        copy.wait()


def row(ref):
    return ref[...].reshape(1, ref.shape[0])


def column(values):
    at = row_iota(HP, H) == lane_iota(HP, H)
    return jnp.sum(jnp.where(at, values, 0.0), axis=1, keepdims=True)


def basis_rows(mean, spread):
    centers = (lane_iota(HP, NB).astype(F32) + 0.5) / NB
    widths = spread + 1.0 / (NB * NB)
    offset = mean - centers
    weights = jnp.exp(-0.5 * offset * offset / widths) * lax.rsqrt(2.0 * math.pi * widths) / NB
    ratio = offset / widths
    return weights, -weights * ratio, 0.5 * weights * (ratio * ratio - 1.0 / widths)


def prep_kernel(geo, x, gain, shift, ridge, mean, spread, out):
    tok = geo["tok"]
    unit, _ = norm_stats(x[...].astype(F32))
    out[0:tok, :] = (unit * row(gain) + row(shift)).astype(BF)
    out[tok : tok + 2 * HP, :] = jnp.zeros((2 * HP, D), BF)
    used = row_iota(HP, 1) < H
    spreads = jnp.where(used, column(row(spread)), 0.01)
    for i, basis in enumerate(basis_rows(column(row(mean)), spreads)):
        rows = lax.dot_general(basis, ridge[...], NT, precision=HIGH, preferred_element_type=F32)
        at, lanes = tok + HP * (i // 2), tok * (i % 2)
        out[at : at + HP, lanes : lanes + tok] = rows.astype(BF)


def qkv_kernel(geo, group, *refs):
    groups, tok, lw, gw, hpg = (geo[k] for k in ("groups", "tok", "lw", "gw", "hpg"))
    pieces, (w, qbias, vbias, q, kv) = refs[:groups], refs[groups:]
    head = row_iota(HP, lw) - group[0] * hpg
    place = jnp.where((head >= 0) & (head < hpg) & (lane_iota(HP, lw) == gw + head), 1.0, 0.0)
    place = place.astype(BF)
    lane = lane_iota(1, lw)
    ones = jnp.where((lane >= gw) & (lane < gw + 2), 1.0, 0.0)
    biases = []
    for ref in (qbias, vbias):
        wide = row(ref)
        mine = jnp.zeros((1, gw), F32)
        for g in range(groups):
            mine = jnp.where(group[0] == g, wide[:, g * gw : (g + 1) * gw], mine)
        biases.append(jnp.concatenate([mine, jnp.zeros((1, lw - gw), F32)], axis=1))
    bias = jnp.concatenate([biases[0], jnp.zeros((1, lw), F32), biases[1] + ones], axis=1)
    for k in range(groups):
        rows = slice(k * tok, (k + 1) * tok)
        out = mm(pieces[k][0:tok, :], w[...]) + bias
        q[rows, :] = out[:, :lw].astype(BF)
        coef = mm(pieces[k][tok : tok + HP, 0:tok], place, TN)
        kv[rows, 0:lw] = (out[:, lw : 2 * lw] + coef).astype(BF)
        kv[rows, lw : 2 * lw] = out[:, 2 * lw :].astype(BF)


def attn_fwd_kernel(geo, deal, starts, place, *refs):
    splits, groups = geo["splits"], geo["groups"]
    q_s, kv, others, srow = refs[0], refs[1], refs[2 : splits + 1], refs[splits + 1]
    comb, att = refs[splits + 2 : splits + 4]
    k_s, v_s, c_s, comb_s, acc, mac, sems = refs[splits + 4 :]
    blk, lw, gw, hpg, own, pad = (geo[k] for k in ("blk", "lw", "gw", "hpg", "own", "pad"))
    load_blocks(geo, deal, place, kv, others, k_s, v_s, sems)
    group = place[0] // splits
    spread = coef_spread(lw, gw, hpg)

    @pl.loop(0, (geo["seq"] + pad) // KT)
    def _(i):
        rows = pl.ds(pl.multiple_of(i * KT, KT), KT)
        c_s[rows, :] = (mm(k_s[rows, :], spread) * v_s[rows, :].astype(F32)).astype(BF)

    @pl.loop(0, own)
    def _(n):
        p = block_at(geo, deal, place, n)
        end = (p + 1) * blk
        mine = pl.ds(pl.multiple_of(n * blk, blk), blk)
        qb = q_s[mine, :].astype(F32) * (HD**-0.5)
        qm = [jnp.where(head_mask(blk, lw, h), qb, 0.0).astype(BF) for h in range(hpg)]
        qstart = jnp.broadcast_to(starts_of(srow, p, blk), (KT, blk)).T
        qpos = p * blk + row_iota(blk, KT)
        qlim = qpos - ((qpos - qstart) & (SEGL - 1))
        acc[...] = jnp.zeros_like(acc)
        mac[...] = jnp.zeros_like(mac)

        @pl.loop(0, (end - starts[0, p * blk] + KT - 1) // KT)
        def _(t):
            base = end - (t + 1) * KT
            rows = pl.ds(pl.multiple_of(pad + base, 64), KT)
            kt, vt, ct = k_s[rows, :], v_s[rows, :], c_s[rows, :]
            kpos = base + lane_iota(blk, KT)
            inside = kpos >= qstart
            visible = inside & (kpos <= qpos)
            earlier = inside & (kpos < qlim)
            for h in range(hpg):
                scores = mm(qm[h], kt, NT)
                probs = jnp.where(visible, jnp.exp(scores), 0.0).astype(BF)
                acc[h] += mm(probs, vt)
            mac[...] += mm(jnp.where(earlier, 1.0, 0.0).astype(BF), ct)

        attended = jnp.zeros((blk, lw), F32)
        for h in range(hpg):
            total = acc[h, :, gw : gw + 1]
            attended = jnp.where(head_mask(blk, lw, h), acc[h] * (1.0 / total), attended)
            attended = jnp.where(lane_iota(blk, lw) == gw + h, total, attended)
        att[mine, :] = attended
        comb_s[mine, :] = (attended + mac[...]).astype(BF)

    for k in range(groups):
        comb[group ^ k] = pack(comb_s[2 * k * blk : 2 * (k + 1) * blk, :gw])


def attn_bwd_kernel(geo, deal, starts, place, *refs):
    splits, groups, nblk = geo["splits"], geo["groups"], geo["nblk"]
    q_s, kv, others, srow = refs[0], refs[1], refs[2 : splits + 1], refs[splits + 1]
    dcombs = refs[splits + 2 : splits + 2 + groups]
    att, dq, dkvs = refs[splits + 2 + groups : splits + 5 + groups]
    k_s, v_s, g_s, dq_a, dk_a, dv_a, r_a, sems = refs[splits + 5 + groups :]
    blk, lw, gw, hpg, own, pad = (geo[k] for k in ("blk", "lw", "gw", "hpg", "own", "pad"))
    load_blocks(geo, deal, place, kv, others, k_s, v_s, sems)
    split = place[0] % splits
    scale = HD**-0.5
    for k in range(groups):
        rows = slice(2 * k * blk, 2 * (k + 1) * blk)
        g_s[rows, :] = jnp.concatenate([unpack(dcombs[k][...]), jnp.zeros((2 * blk, lw - gw), BF)], axis=1)

    @pl.loop(0, (geo["seq"] + pad) // KT)
    def _(i):
        rows = pl.ds(pl.multiple_of(i * KT, KT), KT)
        for ref in (dk_a, dv_a, r_a):
            ref[rows, :] = jnp.zeros((KT, lw), F32)

    @pl.loop(0, own)
    def _(n):
        p = block_at(geo, deal, place, n)
        end = (p + 1) * blk
        mine = pl.ds(pl.multiple_of(n * blk, blk), blk)
        qb = q_s[mine, :].astype(F32) * scale
        qm = [jnp.where(head_mask(blk, lw, h), qb, 0.0).astype(BF) for h in range(hpg)]
        grad = g_s[mine, :]
        wide = grad.astype(F32)
        saved = att[mine, :]
        prod = wide * saved
        lane = lane_iota(blk, lw)
        dn = []
        for h in range(hpg):
            recip = 1.0 / saved[:, gw + h : gw + h + 1]
            only = head_mask(blk, lw, h)
            dtot = -jnp.sum(jnp.where(only, prod, 0.0), axis=1, keepdims=True) * recip
            high = dtot.astype(BF).astype(F32)
            aug = jnp.where(only, wide * recip, 0.0)
            aug = jnp.where(lane == gw, high, aug)
            aug = jnp.where(lane == gw + 1, dtot - high, aug)
            dn.append(aug.astype(BF))
        qstart = jnp.broadcast_to(starts_of(srow, p, blk), (KT, blk))
        qpos = p * blk + lane_iota(KT, blk)
        qlim = qpos - ((qpos - qstart) & (SEGL - 1))
        dq_a[...] = jnp.zeros_like(dq_a)

        @pl.loop(0, (end - starts[0, p * blk] + KT - 1) // KT)
        def _(t):
            base = end - (t + 1) * KT
            rows = pl.ds(pl.multiple_of(pad + base, 64), KT)
            kt, vt = k_s[rows, :], v_s[rows, :]
            kpos = base + row_iota(KT, blk)
            inside = kpos >= qstart
            visible = inside & (kpos <= qpos)
            earlier = inside & (kpos < qlim)
            for h in range(hpg):
                probs = jnp.where(visible, jnp.exp(mm(kt, qm[h], NT)), 0.0)
                dscore = (probs * mm(vt, dn[h], NT)).astype(BF)
                dv_a[rows, :] += mm(probs.astype(BF), dn[h])
                dk_a[rows, :] += mm(dscore, qm[h])
                dq_a[h] += mm(dscore, kt, TN)
            r_a[rows, :] += mm(jnp.where(earlier, 1.0, 0.0).astype(BF), grad)

        dquery = jnp.zeros((blk, lw), F32)
        for h in range(hpg):
            dquery = jnp.where(head_mask(blk, lw, h), dq_a[h] * scale, dquery)
        dq[mine, :] = dquery.astype(BF)

    spread = coef_spread(lw, gw, hpg)
    for n in range(nblk):
        rows = pl.ds(pl.multiple_of(pad + block_at(geo, deal, place, n) * blk, 64), blk)
        out = slice((n % own) * blk, (n % own + 1) * blk)
        reach = r_a[rows, :]
        value = v_s[rows, :].astype(F32)
        lane = lane_iota(blk, lw)
        dval = dv_a[rows, :] + reach * mm(k_s[rows, :], spread)
        dval = jnp.where(lane < gw, dval, 0.0)
        prod = reach * value
        for h in range(hpg):
            part = jnp.sum(jnp.where(head_mask(blk, lw, h), prod, 0.0), axis=1, keepdims=True)
            dval = jnp.where(lane == gw + h, part, dval)
        dkvs[split ^ (n // own), out, 0:lw] = dk_a[rows, :].astype(BF)
        dkvs[split ^ (n // own), out, lw : 2 * lw] = dval.astype(BF)


def proj_kernel(geo, comb, wout, x, bias, gain, shift, resid, n2):
    total = x[...].astype(F32) + row(bias)
    for g in range(geo["groups"]):
        total += mm(unpack(comb[g]), wout[g])
    resid[...] = total
    unit, _ = norm_stats(total)
    n2[...] = (unit * row(gain) + row(shift)).astype(BF)


def ffn_kernel(geo, group, n2, g, wup, wdn, upb, y, dn2, act, dhid):
    tok, fg, groups, nsh = geo["tok"], geo["fg"], geo["groups"], geo["nsh"]
    wide, each, mine = row(upb), fg // nsh, []
    for z in range(nsh):
        value = jnp.zeros((1, each), F32)
        for k in range(groups):
            at = (z * groups + k) * each
            value = jnp.where(group[0] == k, wide[:, at : at + each], value)
        mine.append(value)
    bias = jnp.concatenate(mine, axis=1)
    ysum = jnp.zeros((tok, D), F32)
    dsum = jnp.zeros((tok, D), F32)
    for b in range(0, fg, FB):
        cols = slice(b, b + FB)
        u = mm(n2[...], wup[:, cols]) + bias[:, cols]
        sq = u * u
        th = jnp.tanh(0.7978845608028654 * (u + 0.044715 * sq * u))
        half = 0.5 * (1.0 + th)
        a = (u * half).astype(BF)
        slope = half + 0.5 * u * (1.0 - th * th) * (0.7978845608028654 * (1.0 + 0.134145 * sq))
        d = (slope * mm(g[...], wdn[cols, :], NT)).astype(BF)
        act[:, cols] = a
        dhid[:, cols] = d
        ysum += mm(a, wdn[cols, :])
        dsum += mm(d, wup[:, cols], NT)
    y[...] = ysum.astype(BF)
    dn2[...] = dsum.astype(BF)


def ffn_grad_kernel(geo, split, *refs):
    groups, splits, nsh, part, parta, tok, fg = (
        geo[k] for k in ("groups", "splits", "nsh", "part", "parta", "tok", "fg")
    )
    n2s, dhids, acts, gs = (refs[i * groups : (i + 1) * groups] for i in range(4))
    outs, dupb, acc = refs[4 * groups : 4 * groups + splits], refs[-2], refs[-1]
    total = jnp.zeros((1, fg), F32)
    for ref in dhids:
        total += jnp.sum(ref[...].astype(F32), axis=0, keepdims=True)
    dupb[...] = jnp.broadcast_to(total, dupb.shape)
    for at, left, right in ((0, n2s, dhids), (parta, acts, gs)):
        flip = jnp.concatenate([ref[...].T for ref in left], axis=1)
        for b in range(0, fg, FB):
            side = jnp.concatenate([ref[:, b : b + FB] for ref in right])
            acc[:, b : b + FB] = mm(flip, side)
        for m in range(splits):
            for z in range(nsh):
                rows = (z * splits + (split[0] ^ m)) * part
                rows = pl.ds(pl.multiple_of(rows, 8), part)
                outs[m][z, at : at + part, :] = acc[rows, :].astype(BF)


def post_kernel(geo, group, *refs):
    groups = geo["groups"]
    dn2s, (wout, resid, g, gain) = refs[:groups], refs[groups : groups + 4]
    dresid, dproj, small = refs[groups + 4 : groups + 7]
    dcombs = refs[groups + 7 :]
    unit, recip = norm_stats(resid[...])
    dn2 = dn2s[0][...].astype(F32)
    for ref in dn2s[1:]:
        dn2 += ref[...].astype(F32)
    wide = g[...].astype(F32)
    dres = wide + norm_back(dn2, unit, recip, row(gain))
    dresid[...] = dres
    low = dres.astype(BF)
    dproj[...] = low
    for k in range(groups):
        dcombs[k][...] = pack(mm(low, wout[group[0] ^ k], NT).astype(BF))
    small[0:1, :] = jnp.sum(low.astype(F32), axis=0, keepdims=True)
    small[1:2, :] = jnp.sum(dn2 * unit, axis=0, keepdims=True)
    small[2:3, :] = jnp.sum(dn2, axis=0, keepdims=True)
    small[3:4, :] = jnp.sum(wide, axis=0, keepdims=True)
    small[4:8, :] = jnp.zeros((4, D), F32)


def out_grad_kernel(geo, comb, dproj, out):
    for g in range(geo["groups"]):
        out[g] = mm(unpack(comb[g]), dproj[...], TN).astype(BF)


def result_kernel(geo, *refs):
    groups = geo["groups"]
    ys, (resid, bias, out) = refs[:groups], refs[groups:]
    total = resid[...] + row(bias)
    for ref in ys:
        total += ref[...].astype(F32)
    out[...] = total


def dn1_kernel(geo, dq, dkvs, w, dqkv, *parts):
    splits, groups, tok, lw = (geo[k] for k in ("splits", "groups", "tok", "lw"))
    for k in range(groups):
        rows = slice(k * tok, (k + 1) * tok)
        both = dkvs[0, rows, :].astype(F32)
        for m in range(1, splits):
            both += dkvs[m, rows, :].astype(F32)
        dqkv[rows, 0:lw] = dq[rows, :]
        dqkv[rows, lw : 3 * lw] = both.astype(BF)
        parts[k][...] = mm(dqkv[rows, :], w[...], NT).astype(BF)


def wgrad_kernel(geo, group, split, *refs):
    groups, splits, nsh, part, tok, lw, gw, hpg = (
        geo[k] for k in ("groups", "splits", "nsh", "part", "tok", "lw", "gw", "hpg")
    )
    pieces, parts, dqkv = refs[:groups], refs[groups : 2 * groups], refs[2 * groups]
    outs, (vec, acc) = refs[2 * groups + 1 : -2], refs[-2:]
    flip = jnp.concatenate([ref[0:tok, :].T for ref in pieces], axis=1)
    for b in range(0, 3 * lw, lw):
        acc[:, b : b + lw] = mm(flip, dqkv[:, b : b + lw])
    for m in range(splits):
        for z in range(nsh):
            rows = pl.ds(pl.multiple_of((z * splits + (split[0] ^ m)) * part, 8), part)
            for t in range(3):
                value = pack(acc[rows, t * lw : t * lw + gw])
                outs[m][z, :, t * lw : (t + 1) * lw] = value.astype(BF)
    plain = jnp.zeros((1, D), F32)
    cross = jnp.zeros((1, D), F32)
    means = jnp.zeros((HP, 128), F32)
    spreads = jnp.zeros((HP, 128), F32)
    for k in range(groups):
        dn1 = parts[k][...].astype(F32)
        plain += jnp.sum(dn1, axis=0, keepdims=True)
        cross += jnp.sum(dn1 * pieces[k][0:tok, :].astype(F32), axis=0, keepdims=True)
        dcoef = dqkv[k * tok : (k + 1) * tok, 3 * lw - 128 :]
        means += mm(pieces[k][tok : tok + HP, tok : 2 * tok], dcoef)
        spreads += mm(pieces[k][tok + HP : tok + 2 * HP, 0:tok], dcoef)
    total = jnp.sum(dqkv[...].astype(F32), axis=0, keepdims=True)
    vec[0:1, :] = cross
    vec[1:2, :] = plain
    head = row_iota(HP, 128) - group[0] * hpg
    hit = (head >= 0) & (head < hpg) & (lane_iota(HP, 128) == 128 - (lw - gw) + head)
    across = row_iota(HP, D) == lane_iota(HP, D)
    for i, value in enumerate((means, spreads)):
        value = jnp.sum(jnp.where(hit, value, 0.0), axis=1, keepdims=True)
        value = jnp.sum(jnp.where(across, value, 0.0), axis=0, keepdims=True)
        vec[4 + i : 5 + i, :] = value
    for i, t in enumerate((0, 2)):
        mine = total[:, t * lw : t * lw + gw]
        for g in range(groups):
            vec[2 + i : 3 + i, g * gw : (g + 1) * gw] = jnp.where(group[0] == g, mine, 0.0)
    vec[6:8, :] = jnp.zeros((2, D), F32)


def tail_kernel(geo, *refs):
    groups = geo["groups"]
    parts = refs[:groups]
    x, dresid, gain, grad = refs[groups:]
    dn1 = parts[0][...].astype(F32)
    for ref in parts[1:]:
        dn1 += ref[...].astype(F32)
    unit, recip = norm_stats(x[...].astype(F32))
    grad[...] = dresid[...] + norm_back(dn1, unit, recip, row(gain))


def finish_kernel(geo, ups, downs, up_g, down_g):
    groups, splits, nsh, part, fg, rows = (
        geo[k] for k in ("groups", "splits", "nsh", "part", "fg", "rows")
    )
    each = fg // nsh
    for i in range(groups * splits):
        g, c = i // splits, i % splits
        value = ups[i, 0:part, :].astype(F32)
        for z in range(nsh):
            at = z * groups * each + g * each
            up_g[c * part : (c + 1) * part, at : at + each] = value[:, z * each : (z + 1) * each]
        at = g * each + c * part
        down_g[at : at + part, :] = downs[i, 0:part, :].astype(F32)


def zsum_kernel(geo, *refs):
    parts, out = refs[:-1], refs[-1]
    total = parts[0][...].astype(F32)
    for ref in parts[1:]:
        total += ref[...].astype(F32)
    out[...] = total.astype(BF)


def finish_in_kernel(geo, place, *refs):
    groups, splits, part, gw, lw = (geo[k] for k in ("groups", "splits", "part", "gw", "lw"))
    near, far, (gain, shift) = refs[:groups], refs[groups : groups + splits - 1], refs[-14:-12]
    outs = refs[-12:]
    in_g, out_g = outs[:2]
    group, split = place[0] // splits, place[0] % splits
    prow = part * 3 // 4
    total = jnp.zeros((HP, D), F32)
    for k in range(groups):
        for m in range(splits):
            value = (near[k][...] if m == 0 else far[m - 1][k]).astype(F32)
            total += value[0:HP, :]
            out_g[place[0] ^ (k * splits + m)] = value[HP + prow :, :]
            rows = pl.ds(pl.multiple_of((split ^ m) * part, 8), part)
            wide = [unpack(value[HP : HP + prow, t * lw : (t + 1) * lw]) for t in range(3)]
            for g in range(groups):

                @pl.when((group ^ k) == g)
                def _():
                    for t in range(3):
                        in_g[rows, t * D + g * gw : t * D + (g + 1) * gw] = wide[t]

    flat = lambda i, n=D: total[i : i + 1, 0:n].reshape(n)
    outs[2][...] = ((total[0:1, :] - row(shift) * total[1:2, :]) / row(gain)).reshape(D)
    for ref, i in zip(outs[3:10], (1, 2, 3, 6, 7, 8, 9)):
        ref[...] = flat(i)
    outs[10][...] = total[4:6, 0:128]
    outs[11][...] = total[10:14, :]


def full(shape):
    return pl.BlockSpec(shape, lambda *_: (0,) * len(shape))


ANY = pl.BlockSpec(memory_space=pl.ANY)


def call(kernel, geo, scalars, grid, ins, in_specs, outs, out_specs, scratch, flops, moved, exps=0):
    return pl.pallas_call(
        functools.partial(kernel, geo),
        grid_spec=pltpu.PrefetchScalarGridSpec(
            num_scalar_prefetch=len(scalars),
            grid=grid,
            in_specs=in_specs,
            out_specs=out_specs,
            scratch_shapes=scratch,
        ),
        out_shape=[jax.ShapeDtypeStruct(s, t) for s, t in outs],
        compiler_params=pltpu.CompilerParams(vmem_limit_bytes=56 << 20),
        cost_estimate=pl.CostEstimate(flops=1000, bytes_accessed=1000, transcendentals=0),
    )(*scalars, *ins)


def per_device(
    inputs,
    out_grad,
    segment_ids,
    doc_starts,
    deal_table,
    ridge_matrix,
    first_gain,
    first_shift,
    mixer_in,
    query_bias,
    value_bias,
    mixer_out,
    out_bias,
    second_gain,
    second_shift,
    up_weight,
    up_bias,
    down_weight,
    down_bias,
    memory_mean,
    memory_spread,
):
    tok = inputs.shape[1]
    blk = tok // 2
    nctx, nsh = lax.axis_size("ctx"), lax.axis_size("shard")
    place = lax.axis_index("ctx").astype(jnp.int32)
    seq, nblk = tok * nctx, 2 * nctx
    groups = math.gcd(H, nctx)
    splits = nctx // groups
    hpg = H // groups
    gw = hpg * HD
    lw = -(-(gw + hpg) // 128) * 128
    own = 2 * groups
    group, split = place // splits, place % splits
    ff = up_weight.shape[1]
    fg = ff // groups
    each = fg // nsh
    rows = D // nsh
    part = rows // splits
    parta = -(-part // 16) * 16
    sub = rows // nctx
    qrows = groups * tok
    geo = dict(
        tok=tok, blk=blk, seq=seq, nblk=nblk, groups=groups, splits=splits, hpg=hpg, gw=gw, lw=lw,
        own=own, pad=KT, nctx=nctx, nsh=nsh, fg=fg, rows=rows, part=part, parta=parta,
    )
    x = inputs[0]
    upstream = out_grad[0]
    peers = range(groups)
    across = lambda v, k: v if k == 0 else swap(v, "ctx", nctx, k * splits)
    inside = lambda v, m: swap(v, "ctx", nctx, m)
    gidx, sidx = group.reshape(1), split.reshape(1)
    vm = pltpu.VMEM
    zero = lambda n: jnp.zeros((n, D), F32)
    vrow = full((D,))
    tokd, square = full((tok, D)), full((D, D))

    prow = tok + 2 * HP
    (payload,) = call(
        prep_kernel, geo, (), (1,),
        (x, first_gain, first_shift, ridge_matrix, memory_mean, memory_spread),
        [tokd, vrow, vrow, full((tok, NB)), full((H,)), full((H,))],
        [((prow, D), BF)], [full((prow, D))], [], tok * D * 10, tok * D * 6,
    )
    pieces = [across(payload, k) for k in peers]

    def between(v, axis):
        shape = v.shape[:axis] + (splits,) + v.shape[axis:]
        out = jnp.zeros(shape, v.dtype)
        for m in range(splits):
            piece = v if m == 0 else inside(v, m)
            out = lax.dynamic_update_index_in_dim(out, piece, split ^ m, axis)
        return out

    w_mine = jnp.concatenate(
        [
            jnp.pad(
                lax.dynamic_slice_in_dim(mixer_in, t * D + group * gw, gw, 1),
                ((0, 0), (0, lw - gw)),
            )
            for t in range(3)
        ],
        axis=1,
    )
    w_mine, _ = lax.optimization_barrier((w_mine, payload))
    w_group = swap_gather(w_mine, "shard", nsh).reshape(D, 3 * lw)

    up_rows = lax.dynamic_slice_in_dim(up_weight, split * part, part)
    up_mine = jnp.concatenate(
        [
            lax.dynamic_slice_in_dim(up_rows, z * (ff // nsh) + group * each, each, 1)
            for z in range(nsh)
        ],
        axis=1,
    )
    down_mine = lax.dynamic_slice_in_dim(down_weight, group * each + split * part, part)
    out_mine = lax.dynamic_slice_in_dim(mixer_out, split * part, part)
    trio = jnp.stack([up_mine, down_mine, out_mine])
    trio, _ = lax.optimization_barrier((trio, (w_group, pieces)))
    trio = lax.all_gather(trio, "shard", axis=1)

    pidx = place.reshape(1)
    tables = (deal_table, doc_starts, pidx)

    q, kv = call(
        qkv_kernel, geo, (gidx,), (1,), (*pieces, w_group, query_bias, value_bias),
        [full((prow, D))] * groups + [full((D, 3 * lw)), vrow, vrow],
        [((qrows, lw), BF), ((qrows, 2 * lw), BF)],
        [full((qrows, lw)), full((qrows, 2 * lw))],
        [], qrows * D * 6 * lw, qrows * D * 4,
    )
    others = [inside(kv, m) for m in range(1, splits)]
    upstream_later, _ = lax.optimization_barrier((upstream, q))
    planes = [[g * splits + c for g in peers] for c in range(splits)]
    gs = [upstream if k == 0 else across(upstream_later, k) for k in peers]

    wide = (seq + KT, lw)
    sems = pltpu.SemaphoreType.DMA((2 * nblk,))
    tiles = qrows * seq // 2
    moved = (3 * qrows + 3 * seq) * lw * 2
    comb, att = call(
        attn_fwd_kernel, geo, tables, (1,),
        (q, kv, *others, doc_starts),
        [full((qrows, lw))] + [ANY] * splits + [full((1, seq))],
        [((groups, tok * 3 // 4, 256), BF), ((qrows, lw), F32)],
        [full((groups, tok * 3 // 4, 256)), full((qrows, lw))],
        [vm(wide, BF)] * 3
        + [vm((qrows, lw), BF), vm((hpg, blk, lw), F32), vm((blk, lw), F32), sems],
        tiles * lw * 2 * (2 * hpg + 1), moved, tiles * hpg,
    )
    comb, gs, trio = lax.optimization_barrier((comb, gs, trio))
    w_up, w_down, w_out = between(trio, 2).reshape(3, D, D)
    w_out = w_out.reshape(groups, gw, D)
    trade = lambda v: lax.all_to_all(v, "ctx", 0, 0, axis_index_groups=planes, tiled=True)
    comb = trade(comb)

    resid, n2 = call(
        proj_kernel, geo, (), (1,), (comb, w_out, x, out_bias, second_gain, second_shift),
        [full((groups, tok * 3 // 4, 256)), full((groups, gw, D)), tokd, vrow, vrow, vrow],
        [((tok, D), F32), ((tok, D), BF)], [tokd, tokd],
        [], tok * D * D * 2, tok * D * 12,
    )
    n2s = [across(n2, k) for k in peers]
    ys, dn2s, acts, dhids = [], [], [], []
    for k in peers:
        outs = call(
            ffn_kernel, geo, (gidx,), (1,), (n2s[k], gs[k], w_up, w_down, up_bias),
            [tokd, tokd, square, square, full((ff,))],
            [((tok, D), BF)] * 4, [tokd] * 4,
            [], tok * D * fg * 8, tok * D * 12 + D * fg * 4, tok * fg,
        )
        ys.append(outs[0])
        dn2s.append(across(outs[1], k))
        acts.append(outs[2])
        dhids.append(outs[3])
    dresid, dproj, small2, *dcombs = call(
        post_kernel, geo, (gidx,), (1,), (*dn2s, w_out, resid, upstream, second_gain),
        [tokd] * groups + [full((groups, gw, D)), tokd, tokd, vrow],
        [((tok, D), F32), ((tok, D), BF), ((8, D), F32)]
        + [((tok * 3 // 4, 256), BF)] * groups,
        [tokd, tokd, full((8, D))] + [full((tok * 3 // 4, 256))] * groups,
        [], tok * D * D * 2, tok * D * 20,
    )
    dcombs = [across(dcombs[k], k) for k in peers]
    *dms, dupb = call(
        ffn_grad_kernel, geo, (sidx,), (1,), (*n2s, *dhids, *acts, *gs),
        [tokd] * (4 * groups),
        [((nsh, 2 * parta, D), BF)] * splits + [((8, fg), F32)],
        [full((nsh, 2 * parta, D))] * splits + [full((8, fg))],
        [vm((D, D), F32)], qrows * D * fg * 4, qrows * D * 8,
    )
    (dwout,) = call(
        out_grad_kernel, geo, (), (1,), (comb, dproj),
        [full((groups, tok * 3 // 4, 256)), tokd],
        [((groups, gw, D), BF)], [full((groups, gw, D))],
        [], tok * D * D * 2, tok * D * 6,
    )
    dms, dwout, dcombs = lax.optimization_barrier((dms, dwout, dcombs))
    dwout = dwout.reshape(nsh, nctx, sub, D).transpose(1, 0, 2, 3)
    dwout = lax.psum_scatter(dwout, "ctx", scatter_dimension=0, tiled=False)
    dm = dms[0].astype(F32)
    for m in range(1, splits):
        dm = dm + inside(dms[m], m).astype(F32)
    dm = lax.psum_scatter(dm.astype(BF), "shard", scatter_dimension=0, tiled=False)

    dq, dkvs = call(
        attn_bwd_kernel, geo, tables, (1,),
        (q, kv, *others, doc_starts, *dcombs, att),
        [full((qrows, lw))] + [ANY] * splits + [full((1, seq))]
        + [full((tok * 3 // 4, 256))] * groups + [full((qrows, lw))],
        [((qrows, lw), BF), ((splits, qrows, 2 * lw), BF)],
        [full((qrows, lw)), full((splits, qrows, 2 * lw))],
        [vm(wide, BF)] * 2
        + [vm((qrows, lw), BF), vm((hpg, blk, lw), F32), vm(wide, F32), vm(wide, F32),
           vm(wide, F32), sems],
        tiles * lw * 2 * (5 * hpg + 1), moved, tiles * hpg,
    )
    teams = [[g * splits + c for c in range(splits)] for g in peers]
    dkvs = lax.all_to_all(dkvs, "ctx", 0, 0, axis_index_groups=teams, tiled=True)
    ys_later, _ = lax.optimization_barrier((ys, dcombs))
    ys = [across(ys_later[k], k) for k in peers]
    dkvs, ys, dm = lax.optimization_barrier((dkvs, ys, dm))
    m_g = lax.all_gather(dm, "ctx", axis=0)
    (result,) = call(
        result_kernel, geo, (), (1,), (*ys, resid, down_bias),
        [tokd] * (groups + 1) + [vrow], [((tok, D), F32)], [tokd],
        [], tok * D * 8, tok * D * 16,
    )
    dqkv, *parts = call(
        dn1_kernel, geo, (), (1,), (dq, dkvs, w_group),
        [full((qrows, lw)), full((splits, qrows, 2 * lw)), full((D, 3 * lw))],
        [((qrows, 3 * lw), BF)] + [((tok, D), BF)] * groups,
        [full((qrows, 3 * lw))] + [tokd] * groups,
        [], qrows * D * 6 * lw, qrows * D * 8,
    )
    mine = parts
    parts = [across(parts[k], k) for k in peers]

    prow = part * 3 // 4
    *wgs, vec1 = call(
        wgrad_kernel, geo, (gidx, sidx), (1,), (*pieces, *mine, dqkv),
        [full((tok + 2 * HP, D))] * groups + [tokd] * groups + [full((qrows, 3 * lw))],
        [((nsh, prow, 3 * lw), BF)] * splits + [((8, D), F32)],
        [full((nsh, prow, 3 * lw))] * splits + [full((8, D))],
        [vm((D, 3 * lw), F32)], qrows * D * 6 * lw, qrows * D * 4,
    )
    wsum = wgs[0].astype(F32)
    for m in range(1, splits):
        wsum = wsum + inside(wgs[m], m).astype(F32)
    here = jnp.arange(groups) == group
    up_vec = jnp.where(here[None, :, None], dupb[0].reshape(nsh, 1, each), 0.0).reshape(-1, D)
    vec = jnp.concatenate([vec1[:6], small2[:4], up_vec, zero(2)]).astype(BF)
    late = jnp.concatenate(
        [jnp.broadcast_to(vec[None], (nsh, HP, D)), wsum.astype(BF), dwout], axis=1
    )
    lrow = HP + prow + sub
    zplace = lax.axis_index("shard")
    pick = lambda k: lax.dynamic_index_in_dim(late, zplace ^ k, 0, keepdims=False)
    zs = [pick(k) if k == 0 else swap(pick(k), "shard", nsh, k) for k in range(nsh)]
    (zsum,) = call(
        zsum_kernel, geo, (), (1,), tuple(zs), [full((lrow, D))] * nsh,
        [((lrow, D), BF)], [full((lrow, D))], [], 1000, 1000,
    )
    zsum, parts, result = lax.optimization_barrier((zsum, parts, result))
    near = [across(zsum, k) for k in peers]
    (input_grad,) = call(
        tail_kernel, geo, (), (1,), (*parts, x, dresid, first_gain),
        [tokd] * (groups + 2) + [vrow], [((tok, D), F32)], [tokd],
        [], tok * D * 20, tok * D * 20,
    )
    gblock = lambda r: pl.BlockSpec((nctx, parta, D), lambda j, *_: (0, r, 0))
    up_g, down_g = call(
        finish_kernel, geo, (), (1,), (m_g, m_g), [gblock(0), gblock(1)],
        [((rows, ff), F32), ((ff // nsh, D), F32)],
        [full((rows, ff)), full((ff // nsh, D))],
        [], 1000, rows * ff * 12,
    )
    near, input_grad, up_g = lax.optimization_barrier((near, input_grad, up_g))
    stacked = jnp.stack(near)
    far = [inside(stacked, m) for m in range(1, splits)]
    in_g, out_g, gain_g, shift_g, qb_g, vb_g, ob_g, gain2_g, shift2_g, db_g, pair_g, ub_g = call(
        finish_in_kernel, geo, (pidx,), (1,),
        (*near, *far, first_gain, first_shift),
        [full((lrow, D))] * groups + [full((groups, lrow, D))] * (splits - 1) + [vrow] * 2,
        [((rows, 3 * D), F32), ((nctx, sub, D), F32)] + [((D,), F32)] * 8
        + [((2, 128), F32), ((4, D), F32)],
        [full((rows, 3 * D)), full((nctx, sub, D))] + [vrow] * 8
        + [full((2, 128)), full((4, D))],
        [], 1000, rows * D * 20,
    )
    out_g = out_g.reshape(rows, D)
    small = (
        gain_g, shift_g, qb_g, vb_g, ob_g, gain2_g, shift2_g, ub_g.reshape(ff), db_g,
        pair_g[0, :H], pair_g[1, :H],
    )
    return (result[None], input_grad[None], in_g, out_g, up_g, down_g) + small


def solution(mesh):
    rows, split = P("shard", None), P("shard", "ctx", None)
    none = P()
    return jax.shard_map(
        per_device,
        mesh=mesh,
        in_specs=(
            split, split, rows, rows, none, P("ctx", None), none, none, rows, none, none, rows,
            none, none, none, rows, none, rows, none, none, none,
        ),
        out_specs=(split, split, rows, rows, rows, rows) + (none,) * 11,
        check_vma=False,
    )
```

```python
import functools
import math

import jax
import jax.numpy as jnp
from jax import lax
from jax.experimental import pallas as pl
from jax.experimental.pallas import tpu as pltpu
from jax.sharding import PartitionSpec as P

D = 768
H = 12
HD = 64
NB = 256
SEGL = 16

HIGH = lax.Precision.HIGHEST
EPS = 1e-05
BF = jnp.bfloat16
F32 = jnp.float32
KT = 256
FB = 256
NN = (((1,), (0,)), ((), ()))
NT = (((1,), (1,)), ((), ()))
TN = (((0,), (0,)), ((), ()))


def mm(a, b, dims=NN):
    return lax.dot_general(a, b, dims, preferred_element_type=F32)


def norm_stats(values):
    center = values - jnp.mean(values, axis=-1, keepdims=True)
    spread = jnp.mean(center * center, axis=-1, keepdims=True)
    recip = lax.rsqrt(spread + EPS)
    return center * recip, recip


def norm_back(upstream, unit, recip, gain):
    scaled = upstream * gain
    return recip * (
        scaled
        - jnp.mean(scaled, axis=-1, keepdims=True)
        - unit * jnp.mean(scaled * unit, axis=-1, keepdims=True)
    )


def swap(x, axis, count, k):
    return lax.ppermute(x, axis, [(i, i ^ k) for i in range(count)])


def swap_pieces(x, axis, count):
    out = [x]
    for k in range(1, count):
        if k > 2:
            x, _ = lax.optimization_barrier((x, out[-1]))
        out.append(swap(x, axis, count, k))
    return out


def lane_iota(rows, cols):
    return lax.broadcasted_iota(jnp.int32, (rows, cols), 1)


def row_iota(rows, cols):
    return lax.broadcasted_iota(jnp.int32, (rows, cols), 0)


def head_mask(rows, cols, head):
    lane = lane_iota(rows, cols)
    return (lane >= head * HD) & (lane < (head + 1) * HD)


HP = 16
VR = 32


def pack(value):
    cut = value.shape[0] * 3 // 4
    last = [value[cut:, h * HD : (h + 1) * HD] for h in range(3)]
    return jnp.concatenate([value[:cut, :], jnp.concatenate(last, axis=0)], axis=1)


def unpack(value):
    each, gw = value.shape[0] // 3, 3 * HD
    last = [value[h * each : (h + 1) * each, gw:] for h in range(3)]
    return jnp.concatenate([value[:, :gw], jnp.concatenate(last, axis=1)], axis=0)


def coef_spread(lw, gw, hpg):
    row, lane = row_iota(lw, lw), lane_iota(lw, lw)
    hit = (row >= gw) & (row < gw + hpg) & (lane < gw)
    hit = hit & (lane >= (row - gw) * HD) & (lane < (row - gw + 1) * HD)
    return jnp.where(hit, 1.0, 0.0).astype(BF)


def block_at(geo, deal, place, n):
    own, splits = geo["own"], geo["splits"]
    device = place[0] ^ (((n % own) // 2) * splits + n // own)
    return deal[2 * device + n % 2]


def starts_of(ref, p, blk):
    at = pl.multiple_of((p * blk) // 128 * 128, 128)
    window = ref[:, pl.ds(at, blk + 64)]
    return jnp.where((p * blk) % 128 == 0, window[:, :blk], window[:, 64:])


def fetch(pairs, sems, first=0):
    copies = [pltpu.make_async_copy(a, b, sems.at[first + i]) for i, (a, b) in enumerate(pairs)]
    for copy in copies:
        copy.start()
    return copies


def load_blocks(geo, deal, place, kv, others, k_s, v_s, sems):
    blk, lw, own, pad = geo["blk"], geo["lw"], geo["own"], KT
    for ref in (k_s, v_s):
        ref[0:pad, :] = jnp.zeros((pad, lw), BF)
    copies = []
    for n in range(geo["nblk"]):
        source = kv if n < own else others[n // own - 1]
        rows = pl.ds((n % own) * blk, blk)
        to = pl.ds(pl.multiple_of(pad + block_at(geo, deal, place, n) * blk, 64), blk)
        for j, ref in enumerate((k_s, v_s)):
            copies.append(
                pltpu.make_async_copy(
                    source.at[rows, pl.ds(j * lw, lw)], ref.at[to], sems.at[2 * n + j]
                )
            )
    for copy in copies:
        copy.start()
    return copies


def row(ref):
    return ref[...].reshape(1, ref.shape[0])


def column(values):
    at = row_iota(HP, H) == lane_iota(HP, H)
    return jnp.sum(jnp.where(at, values, 0.0), axis=1, keepdims=True)


def basis_rows(mean, spread):
    centers = (lane_iota(HP, NB).astype(F32) + 0.5) / NB
    widths = spread + 1.0 / (NB * NB)
    offset = mean - centers
    weights = jnp.exp(-0.5 * offset * offset / widths) * lax.rsqrt(2.0 * math.pi * widths) / NB
    ratio = offset / widths
    return weights, -weights * ratio, 0.5 * weights * (ratio * ratio - 1.0 / widths)


def prep_kernel(geo, x, gain, shift, ridge, mean, spread, out):
    tok = geo["tok"]
    unit, _ = norm_stats(x[...].astype(F32))
    out[0:tok, :] = (unit * row(gain) + row(shift)).astype(BF)
    out[tok : tok + 2 * HP, :] = jnp.zeros((2 * HP, D), BF)
    used = row_iota(HP, 1) < H
    spreads = jnp.where(used, column(row(spread)), 0.01)
    for i, basis in enumerate(basis_rows(column(row(mean)), spreads)):
        rows = lax.dot_general(basis, ridge[...], NT, precision=HIGH, preferred_element_type=F32)
        at, lanes = tok + HP * (i // 2), tok * (i % 2)
        out[at : at + HP, lanes : lanes + tok] = rows.astype(BF)


def qkv_kernel(geo, here, *refs):
    groups, nsh, rows, tok, lw, gw, hpg, fg = (
        geo[k] for k in ("groups", "nsh", "rows", "tok", "lw", "gw", "hpg", "fg")
    )
    pieces, parts = refs[:groups], refs[groups : groups + nsh]
    qbias, vbias, upb = refs[groups + nsh : groups + nsh + 3]
    vectors = refs[groups + nsh + 3 : -5]
    q, kv, w, vecs, ups = refs[-5:]
    group = here[0]
    for k in range(nsh):
        w[pl.ds(pl.multiple_of((here[2] ^ k) * rows, 16), rows), :] = parts[k][...]
    for i, ref in enumerate(vectors):
        vecs[i : i + 1, :] = row(ref)
    wide, each, mine = row(upb), fg // nsh, []
    for z in range(nsh):
        value = jnp.zeros((1, each), F32)
        for k in range(groups):
            at = (z * groups + k) * each
            value = jnp.where(group == k, wide[:, at : at + each], value)
        mine.append(value)
    ups[...] = jnp.broadcast_to(jnp.concatenate(mine, axis=1), ups.shape)
    head = row_iota(HP, lw) - group * hpg
    place = jnp.where((head >= 0) & (head < hpg) & (lane_iota(HP, lw) == gw + head), 1.0, 0.0)
    place = place.astype(BF)
    lane = lane_iota(1, lw)
    ones = jnp.where((lane >= gw) & (lane < gw + hpg), 1.0, 0.0)
    biases = []
    for ref in (qbias, vbias):
        wide = row(ref)
        mine = jnp.zeros((1, gw), F32)
        for g in range(groups):
            mine = jnp.where(group == g, wide[:, g * gw : (g + 1) * gw], mine)
        biases.append(jnp.concatenate([mine, jnp.zeros((1, lw - gw), F32)], axis=1))
    bias = jnp.concatenate([biases[0], jnp.zeros((1, lw), F32), biases[1] + ones], axis=1)
    for k in range(groups):
        rows = slice(k * tok, (k + 1) * tok)
        out = mm(pieces[k][0:tok, :], w[...]) + bias
        q[rows, :] = out[:, :lw].astype(BF)
        coef = mm(pieces[k][tok : tok + HP, 0:tok], place, TN)
        kv[rows, 0:lw] = (out[:, lw : 2 * lw] + coef).astype(BF)
        kv[rows, lw : 2 * lw] = out[:, 2 * lw :].astype(BF)


def attn_fwd_kernel(geo, deal, starts, place, *refs):
    splits, groups = geo["splits"], geo["groups"]
    q_s, kv, others, srow = refs[0], refs[1], refs[2 : splits + 1], refs[splits + 1]
    comb, att = refs[splits + 2 : splits + 4]
    k_s, v_s, c_s, comb_s, acc, mac, sems = refs[splits + 4 :]
    blk, lw, gw, hpg, own, pad = (geo[k] for k in ("blk", "lw", "gw", "hpg", "own", "pad"))
    for copy in load_blocks(geo, deal, place, kv, others, k_s, v_s, sems):
        copy.wait()
    group = place[0] // splits
    spread = coef_spread(lw, gw, hpg)
    zero = jnp.zeros((), BF)

    @pl.loop(0, (geo["seq"] + pad) // KT)
    def _(i):
        rows = pl.ds(pl.multiple_of(i * KT, KT), KT)
        c_s[rows, :] = (mm(k_s[rows, :], spread) * v_s[rows, :].astype(F32)).astype(BF)

    @pl.loop(0, own)
    def _(n):
        p = block_at(geo, deal, place, n)
        end = (p + 1) * blk
        mine = pl.ds(pl.multiple_of(n * blk, blk), blk)
        qb = q_s[mine, :].astype(F32) * (HD**-0.5)
        qm = [jnp.where(head_mask(blk, lw, h), qb, 0.0).astype(BF) for h in range(hpg)]
        qstart = jnp.broadcast_to(starts_of(srow, p, blk), (KT, blk)).T
        qpos = p * blk + row_iota(blk, KT)
        qlim = qpos - ((qpos - qstart) & (SEGL - 1))
        acc[...] = jnp.zeros_like(acc)
        mac[...] = jnp.zeros_like(mac)

        @pl.loop(0, (end - starts[0, p * blk] + KT - 1) // KT)
        def _(t):
            base = end - (t + 1) * KT
            rows = pl.ds(pl.multiple_of(pad + base, 64), KT)
            kt, vt, ct = k_s[rows, :], v_s[rows, :], c_s[rows, :]
            kpos = base + lane_iota(blk, KT)
            inside = kpos >= qstart
            visible = inside & (kpos <= qpos)
            earlier = inside & (kpos < qlim)
            numer = jnp.zeros((blk, lw), F32)
            for h in range(hpg):
                scores = mm(qm[h], kt, NT)
                probs = jnp.where(visible, jnp.exp(scores), 0.0).astype(BF)
                mine = head_mask(KT, lw, h) | (lane_iota(KT, lw) == gw + h)
                numer += mm(probs, jnp.where(mine, vt, zero))
            acc[...] += numer
            mac[...] += mm(jnp.where(earlier, 1.0, 0.0).astype(BF), ct)

        attended = acc[...]
        scale = jnp.ones((blk, lw), F32)
        for h in range(hpg):
            recip = 1.0 / acc[:, gw + h : gw + h + 1]
            scale = jnp.where(head_mask(blk, lw, h), recip, scale)
        attended = attended * scale
        att[mine, :] = attended
        comb_s[mine, :] = (attended + mac[...]).astype(BF)

    for k in range(groups):
        comb[group ^ k] = pack(comb_s[2 * k * blk : 2 * (k + 1) * blk, :gw])


def attn_bwd_kernel(geo, deal, starts, place, *refs):
    splits, groups, nblk = geo["splits"], geo["groups"], geo["nblk"]
    q_h, kv, others, srow = refs[0], refs[1], refs[2 : splits + 1], refs[splits + 1]
    dcombs = refs[splits + 2 : splits + 2 + groups]
    att_h, dq_h = refs[splits + 2 + groups : splits + 4 + groups]
    dkvs_h = refs[splits + 4 + groups : 2 * splits + 4 + groups]
    k_s, v_s, g_s, dq_a, dk_a, dv_a, r_a, q_s, att, dc_s, dq, dkvs, sems, out_sems = refs[
        2 * splits + 4 + groups :
    ]
    copies = [(q_h, q_s), (att_h, att)] + [(dcombs[k], dc_s.at[k]) for k in range(groups)]
    copies = fetch(copies, sems, 2 * nblk)
    zero = jnp.zeros((), BF)
    blk, lw, gw, hpg, own, pad = (geo[k] for k in ("blk", "lw", "gw", "hpg", "own", "pad"))
    copies += load_blocks(geo, deal, place, kv, others, k_s, v_s, sems)
    scale = HD**-0.5
    @pl.loop(0, (geo["seq"] + pad) // KT)
    def _(i):
        rows = pl.ds(pl.multiple_of(i * KT, KT), KT)
        for ref in (dk_a, dv_a, r_a):
            ref[rows, :] = jnp.zeros((KT, lw), F32)

    for copy in copies:
        copy.wait()
    for k in range(groups):
        rows = slice(2 * k * blk, 2 * (k + 1) * blk)
        g_s[rows, :] = jnp.concatenate([unpack(dc_s[k]), jnp.zeros((2 * blk, lw - gw), BF)], axis=1)

    @pl.loop(0, own)
    def _(n):
        p = block_at(geo, deal, place, n)
        end = (p + 1) * blk
        mine = pl.ds(pl.multiple_of(n * blk, blk), blk)
        qb = q_s[mine, :].astype(F32) * scale
        qm = [jnp.where(head_mask(blk, lw, h), qb, 0.0).astype(BF) for h in range(hpg)]
        grad = g_s[mine, :]
        wide = grad.astype(F32)
        saved = att[mine, :]
        prod = wide * saved
        lane = lane_iota(blk, lw)
        dn = []
        for h in range(hpg):
            recip = 1.0 / saved[:, gw + h : gw + h + 1]
            only = head_mask(blk, lw, h)
            dtot = -jnp.sum(jnp.where(only, prod, 0.0), axis=1, keepdims=True) * recip
            high = dtot.astype(BF).astype(F32)
            aug = jnp.where(only, wide * recip, 0.0)
            aug = jnp.where(lane == gw, high, aug)
            aug = jnp.where(lane == gw + 1, dtot - high, aug)
            dn.append(aug.astype(BF))
        qstart = jnp.broadcast_to(starts_of(srow, p, blk), (KT, blk))
        qpos = p * blk + lane_iota(KT, blk)
        qlim = qpos - ((qpos - qstart) & (SEGL - 1))
        dq_a[...] = jnp.zeros_like(dq_a)

        @pl.loop(0, (end - starts[0, p * blk] + KT - 1) // KT)
        def _(t):
            base = end - (t + 1) * KT
            rows = pl.ds(pl.multiple_of(pad + base, 64), KT)
            kt, vt = k_s[rows, :], v_s[rows, :]
            kpos = base + row_iota(KT, blk)
            inside = kpos >= qstart
            visible = inside & (kpos <= qpos)
            earlier = inside & (kpos < qlim)
            dval = jnp.zeros((KT, lw), F32)
            dkey = jnp.zeros((KT, lw), F32)
            dque = jnp.zeros((blk, lw), F32)
            for h in range(hpg):
                probs = jnp.where(visible, jnp.exp(mm(kt, qm[h], NT)), 0.0)
                dscore = (probs * mm(vt, dn[h], NT)).astype(BF)
                dval += mm(probs.astype(BF), dn[h])
                dkey += mm(dscore, qm[h])
                dque += mm(dscore, jnp.where(head_mask(KT, lw, h), kt, zero), TN)
            dv_a[rows, :] += dval
            dk_a[rows, :] += dkey
            dq_a[...] += dque
            r_a[rows, :] += mm(jnp.where(earlier, 1.0, 0.0).astype(BF), grad)

        dq[mine, :] = (dq_a[...] * scale).astype(BF)

    copies = fetch([(dq, dq_h)], out_sems, splits)
    spread = coef_spread(lw, gw, hpg)
    for m in reversed(range(splits)):

        @pl.loop(0, own)
        def _(i):
            at = block_at(geo, deal, place, m * own + i) * blk
            rows = pl.ds(pl.multiple_of(pad + at, 64), blk)
            out = pl.ds(pl.multiple_of(i * blk, blk), blk)
            reach = r_a[rows, :]
            value = v_s[rows, :].astype(F32)
            lane = lane_iota(blk, lw)
            dval = dv_a[rows, :] + reach * mm(k_s[rows, :], spread)
            dval = jnp.where(lane < gw, dval, 0.0)
            prod = reach * value
            for h in range(hpg):
                only = head_mask(blk, lw, h)
                part = jnp.sum(jnp.where(only, prod, 0.0), axis=1, keepdims=True)
                dval = jnp.where(lane == gw + h, part, dval)
            dkvs[m, out, 0:lw] = dk_a[rows, :].astype(BF)
            dkvs[m, out, lw : 2 * lw] = dval.astype(BF)

        copies += fetch([(dkvs.at[m], dkvs_h[m])], out_sems, m)

    for copy in copies:
        copy.wait()


def assemble_kernel(geo, split, *refs):
    splits, nsh = geo["splits"], geo["nsh"]
    for m in range(splits):
        for i in range(3):
            for z in range(nsh):
                refs[splits + i][z, split[0] ^ m] = refs[m][i, z]


def proj_kernel(geo, comb, wout, x, vecs, resid, n2):
    total = x[...].astype(F32) + vecs[0:1, :]
    for g in range(geo["groups"]):
        total += mm(unpack(comb[g]), wout[g])
    resid[...] = total
    unit, _ = norm_stats(total)
    n2[...] = (unit * vecs[1:2, :] + vecs[2:3, :]).astype(BF)


def ffn_kernel(geo, n2, g, wup, wdn, bias, y, dn2, act, dhid, ysum, dsum):
    fg = geo["fg"]
    ysum[...] = jnp.zeros_like(ysum)
    dsum[...] = jnp.zeros_like(dsum)

    @pl.loop(0, fg // FB)
    def _(b):
        cols = pl.ds(pl.multiple_of(b * FB, FB), FB)
        u = mm(n2[...], wup[:, cols]) + bias[0:1, cols]
        sq = u * u
        th = jnp.tanh(0.7978845608028654 * (u + 0.044715 * sq * u))
        half = 0.5 * (1.0 + th)
        a = (u * half).astype(BF)
        slope = half + 0.5 * u * (1.0 - th * th) * (0.7978845608028654 * (1.0 + 0.134145 * sq))
        d = (slope * mm(g[...], wdn[cols, :], NT)).astype(BF)
        act[:, cols] = a
        dhid[:, cols] = d
        ysum[...] += mm(a, wdn[cols, :])
        dsum[...] += mm(d, wup[:, cols], NT)

    y[...] = ysum[...].astype(BF)
    dn2[...] = dsum[...].astype(BF)


def ffn_grad_kernel(geo, split, *refs):
    groups, splits, nsh, part, parta, tok, fg = (
        geo[k] for k in ("groups", "splits", "nsh", "part", "parta", "tok", "fg")
    )
    n2s, dhids, acts, gs = (refs[i * groups : (i + 1) * groups] for i in range(4))
    outs, dupb, acc = refs[4 * groups : 4 * groups + splits], refs[-2], refs[-1]
    total = jnp.zeros((1, fg), F32)
    for ref in dhids:
        total += jnp.sum(ref[...].astype(F32), axis=0, keepdims=True)
    dupb[...] = jnp.broadcast_to(total, dupb.shape)
    for at, left, right in ((0, n2s, dhids), (parta, acts, gs)):
        flip = jnp.concatenate([ref[...].T for ref in left], axis=1)
        for b in range(0, fg, FB):
            side = jnp.concatenate([ref[:, b : b + FB] for ref in right])
            acc[:, b : b + FB] = mm(flip, side)
        for m in range(splits):
            for z in range(nsh):
                rows = (z * splits + (split[0] ^ m)) * part
                rows = pl.ds(pl.multiple_of(rows, 8), part)
                outs[m][z, at : at + part, :] = acc[rows, :].astype(BF)


def post_kernel(geo, group, *refs):
    groups = geo["groups"]
    dn2s, (wout, resid, g, vecs) = refs[:groups], refs[groups : groups + 4]
    dresid, dproj, small = refs[groups + 4 : groups + 7]
    dcombs = refs[groups + 7 :]
    unit, recip = norm_stats(resid[...])
    dn2 = dn2s[0][...].astype(F32)
    for ref in dn2s[1:]:
        dn2 += ref[...].astype(F32)
    wide = g[...].astype(F32)
    dres = wide + norm_back(dn2, unit, recip, vecs[1:2, :])
    dresid[...] = dres
    low = dres.astype(BF)
    dproj[...] = low
    for k in range(groups):
        dcombs[k][...] = pack(mm(low, wout[group[0] ^ k], NT).astype(BF))
    small[0:1, :] = jnp.sum(low.astype(F32), axis=0, keepdims=True)
    small[1:2, :] = jnp.sum(dn2 * unit, axis=0, keepdims=True)
    small[2:3, :] = jnp.sum(dn2, axis=0, keepdims=True)
    small[3:4, :] = jnp.sum(wide, axis=0, keepdims=True)
    small[4:8, :] = jnp.zeros((4, D), F32)


def out_grad_kernel(geo, here, comb, dproj, *outs):
    splits, nsh, gw = geo["splits"], geo["nsh"], geo["gw"]
    rows, sub = D // nsh, D // nsh // geo["nctx"]
    for g in range(geo["groups"]):
        value = mm(unpack(comb[g]), dproj[...], TN)
        for r in range(0, gw, sub):
            z, i = (g * gw + r) // rows, (g * gw + r) % rows // sub
            piece = value[r : r + sub, :].astype(BF)
            for m in range(splits):

                @pl.when(((i % splits) ^ here[1]) == m)
                def _():
                    outs[m][(i // splits) ^ here[0], z] = piece


def extend_kernel(geo, *refs):
    groups, splits, nsh, tok = (geo[k] for k in ("groups", "splits", "nsh", "tok"))
    ys, grads, outs = refs[: groups - 1], refs[groups - 1 : groups - 1 + splits], refs[-groups:]
    for k in range(groups):
        total = grads[0][k].astype(F32)
        for ref in grads[1:]:
            total += ref[k].astype(F32)
        total = total.reshape(nsh * total.shape[1], D).astype(BF)
        if k == 0:
            outs[0][...] = total
        else:
            outs[k][0:tok, :] = ys[k - 1][...]
            outs[k][tok:, :] = total


def sum_kernel(geo, *refs):
    total = refs[0][...].astype(F32)
    for ref in refs[1:-1]:
        total += ref[...].astype(F32)
    refs[-1][...] = total.astype(BF)


def stack_kernel(geo, *refs):
    for k, ref in enumerate(refs[:-1]):
        refs[-1][k] = ref[...]


def late_kernel(geo, here, *refs):
    splits, groups, nsh, fg = (geo[k] for k in ("splits", "groups", "nsh", "fg"))
    sub = D // nsh // geo["nctx"]
    wgs, exts = refs[:splits], refs[splits : splits + groups]
    vec1, small2, dupb = refs[splits + groups : splits + groups + 3]
    outs, (dwout, vec) = refs[splits + groups + 3 : -2], refs[-2:]
    total = exts[0][...].astype(F32)
    for ref in exts[1:]:
        total += ref[geo["tok"] :, :].astype(F32)
    for z in range(nsh):
        dwout[z] = total[z * sub : (z + 1) * sub, :]
    vec[0:6, :] = vec1[0:6, :]
    vec[6:10, :] = small2[0:4, :]
    each, spans = fg // nsh, []
    for z in range(nsh):
        for g in range(groups):
            value = dupb[0:1, z * each : (z + 1) * each]
            spans.append(jnp.where(here[0] == g, value, 0.0))
    per = D // each
    for i in range(len(spans) // per):
        vec[10 + i : 11 + i, :] = jnp.concatenate(spans[i * per : (i + 1) * per], axis=1)
    vec[14:16, :] = jnp.zeros((2, D), F32)
    for k in range(nsh):
        z = here[2] ^ k
        total = wgs[0][z].astype(F32)
        for ref in wgs[1:]:
            total += ref[z].astype(F32)
        outs[k][...] = jnp.concatenate([vec[...], total, dwout[z]], axis=0).astype(BF)


def result_kernel(geo, *refs):
    groups = geo["groups"]
    ys, (resid, vecs, out) = refs[:groups], refs[groups:]
    total = resid[...] + vecs[3:4, :]
    for ref in ys:
        total += ref[0 : geo["tok"], :].astype(F32)
    out[...] = total


def dn1_kernel(geo, dq, *refs):
    splits, groups, tok, lw = (geo[k] for k in ("splits", "groups", "tok", "lw"))
    dkvs, (w, dqkv), parts = refs[:splits], refs[splits : splits + 2], refs[splits + 2 :]
    for k in range(groups):
        rows = slice(k * tok, (k + 1) * tok)
        both = dkvs[0][rows, :].astype(F32)
        for ref in dkvs[1:]:
            both += ref[rows, :].astype(F32)
        dqkv[rows, 0:lw] = dq[rows, :]
        dqkv[rows, lw : 3 * lw] = both.astype(BF)
        parts[k][...] = mm(dqkv[rows, :], w[...], NT).astype(BF)


def wgrad_kernel(geo, group, split, *refs):
    groups, splits, nsh, part, tok, lw, gw, hpg = (
        geo[k] for k in ("groups", "splits", "nsh", "part", "tok", "lw", "gw", "hpg")
    )
    pieces, parts, dqkv = refs[:groups], refs[groups : 2 * groups], refs[2 * groups]
    outs, (vec, acc) = refs[2 * groups + 1 : -2], refs[-2:]
    flip = jnp.concatenate([ref[0:tok, :].T for ref in pieces], axis=1)
    for b in range(0, 3 * lw, lw):
        acc[:, b : b + lw] = mm(flip, dqkv[:, b : b + lw])
    for m in range(splits):
        for z in range(nsh):
            rows = pl.ds(pl.multiple_of((z * splits + (split[0] ^ m)) * part, 8), part)
            for t in range(3):
                value = pack(acc[rows, t * lw : t * lw + gw])
                outs[m][z, :, t * lw : (t + 1) * lw] = value.astype(BF)
    plain = jnp.zeros((1, D), F32)
    cross = jnp.zeros((1, D), F32)
    means = jnp.zeros((HP, 128), F32)
    spreads = jnp.zeros((HP, 128), F32)
    for k in range(groups):
        dn1 = parts[k][...].astype(F32)
        plain += jnp.sum(dn1, axis=0, keepdims=True)
        cross += jnp.sum(dn1 * pieces[k][0:tok, :].astype(F32), axis=0, keepdims=True)
        dcoef = dqkv[k * tok : (k + 1) * tok, 3 * lw - 128 :]
        means += mm(pieces[k][tok : tok + HP, tok : 2 * tok], dcoef)
        spreads += mm(pieces[k][tok + HP : tok + 2 * HP, 0:tok], dcoef)
    total = jnp.sum(dqkv[...].astype(F32), axis=0, keepdims=True)
    vec[0:1, :] = cross
    vec[1:2, :] = plain
    head = row_iota(HP, 128) - group[0] * hpg
    hit = (head >= 0) & (head < hpg) & (lane_iota(HP, 128) == 128 - (lw - gw) + head)
    across = row_iota(HP, D) == lane_iota(HP, D)
    for i, value in enumerate((means, spreads)):
        value = jnp.sum(jnp.where(hit, value, 0.0), axis=1, keepdims=True)
        value = jnp.sum(jnp.where(across, value, 0.0), axis=0, keepdims=True)
        vec[4 + i : 5 + i, :] = value
    for i, t in enumerate((0, 2)):
        mine = total[:, t * lw : t * lw + gw]
        for g in range(groups):
            vec[2 + i : 3 + i, g * gw : (g + 1) * gw] = jnp.where(group[0] == g, mine, 0.0)
    vec[6:8, :] = jnp.zeros((2, D), F32)


def tail_kernel(geo, *refs):
    groups = geo["groups"]
    parts = refs[:groups]
    x, dresid, vecs, grad = refs[groups:]
    dn1 = parts[0][...].astype(F32)
    for ref in parts[1:]:
        dn1 += ref[...].astype(F32)
    unit, recip = norm_stats(x[...].astype(F32))
    grad[...] = dresid[...] + norm_back(dn1, unit, recip, vecs[4:5, :])


def finish_kernel(geo, ups, downs, up_g, down_g):
    groups, splits, nsh, part, fg, rows = (
        geo[k] for k in ("groups", "splits", "nsh", "part", "fg", "rows")
    )
    each = fg // nsh
    for i in range(groups * splits):
        g, c = i // splits, i % splits
        value = ups[i, 0:part, :].astype(F32)
        for z in range(nsh):
            at = z * groups * each + g * each
            up_g[c * part : (c + 1) * part, at : at + each] = value[:, z * each : (z + 1) * each]
        at = g * each + c * part
        down_g[at : at + part, :] = downs[i, 0:part, :].astype(F32)


def finish_in_kernel(geo, place, *refs):
    groups, splits, part, gw, lw = (geo[k] for k in ("groups", "splits", "part", "gw", "lw"))
    near, far, vecs = refs[:groups], refs[groups : groups + splits - 1], refs[-14]
    outs = refs[-13:]
    in_g, out_g = outs[:2]
    group, split = place[0] // splits, place[0] % splits
    prow = part * 3 // 4
    total = jnp.zeros((HP, D), F32)
    for k in range(groups):
        for m in range(splits):
            value = (near[k][...] if m == 0 else far[m - 1][k]).astype(F32)
            total += value[0:HP, :]
            out_g[place[0] ^ (k * splits + m)] = value[HP + prow :, :]
            rows = pl.ds(pl.multiple_of((split ^ m) * part, 8), part)
            wide = [unpack(value[HP : HP + prow, t * lw : (t + 1) * lw]) for t in range(3)]
            for g in range(groups):

                @pl.when((group ^ k) == g)
                def _():
                    for t in range(3):
                        in_g[rows, t * D + g * gw : t * D + (g + 1) * gw] = wide[t]

    flat = lambda i, n=D: total[i : i + 1, 0:n].reshape(n)
    outs[2][...] = ((total[0:1, :] - vecs[5:6, :] * total[1:2, :]) / vecs[4:5, :]).reshape(D)
    for ref, i in zip(outs[3:10], (1, 2, 3, 6, 7, 8, 9)):
        ref[...] = flat(i)
    outs[10][...] = flat(4, H)
    outs[11][...] = flat(5, H)
    for i in range(4):
        outs[12][i * D : (i + 1) * D] = flat(10 + i)


def full(shape):
    return pl.BlockSpec(shape, lambda *_: (0,) * len(shape))


ANY = pl.BlockSpec(memory_space=pl.ANY)
DMA = pltpu.SemaphoreType.DMA


def call(kernel, geo, scalars, grid, ins, in_specs, outs, out_specs, scratch, flops, moved, exps=0, limit=12):
    return pl.pallas_call(
        functools.partial(kernel, geo),
        grid_spec=pltpu.PrefetchScalarGridSpec(
            num_scalar_prefetch=len(scalars),
            grid=grid,
            in_specs=in_specs,
            out_specs=out_specs,
            scratch_shapes=scratch,
        ),
        out_shape=[jax.ShapeDtypeStruct(s, t) for s, t in outs],
        compiler_params=pltpu.CompilerParams(vmem_limit_bytes=limit << 20),
        cost_estimate=pl.CostEstimate(flops=1000, bytes_accessed=1000, transcendentals=0),
    )(*scalars, *ins)


def per_device(
    inputs,
    out_grad,
    segment_ids,
    doc_starts,
    deal_table,
    ridge_matrix,
    first_gain,
    first_shift,
    mixer_in,
    query_bias,
    value_bias,
    mixer_out,
    out_bias,
    second_gain,
    second_shift,
    up_weight,
    up_bias,
    down_weight,
    down_bias,
    memory_mean,
    memory_spread,
):
    tok = inputs.shape[1]
    blk = tok // 2
    nctx, nsh = lax.axis_size("ctx"), lax.axis_size("shard")
    place = lax.axis_index("ctx").astype(jnp.int32)
    seq, nblk = tok * nctx, 2 * nctx
    groups = math.gcd(H, nctx)
    splits = nctx // groups
    hpg = H // groups
    gw = hpg * HD
    lw = -(-(gw + hpg) // 128) * 128
    own = 2 * groups
    group, split = place // splits, place % splits
    ff = up_weight.shape[1]
    fg = ff // groups
    each = fg // nsh
    rows = D // nsh
    part = rows // splits
    parta = -(-part // 16) * 16
    sub = rows // nctx
    qrows = groups * tok
    geo = dict(
        tok=tok, blk=blk, seq=seq, nblk=nblk, groups=groups, splits=splits, hpg=hpg, gw=gw, lw=lw,
        own=own, pad=KT, nctx=nctx, nsh=nsh, fg=fg, rows=rows, part=part, parta=parta,
    )
    x = inputs[0]
    upstream = out_grad[0]
    peers = range(groups)
    across = lambda v, k: v if k == 0 else swap(v, "ctx", nctx, k * splits)
    inside = lambda v, m: swap(v, "ctx", nctx, m)
    gidx, sidx = group.reshape(1), split.reshape(1)
    vm = pltpu.VMEM
    zero = lambda n: jnp.zeros((n, D), F32)
    vrow = full((D,))
    tokd, square = full((tok, D)), full((D, D))

    prow = tok + 2 * HP
    (payload,) = call(
        prep_kernel, geo, (), (1,),
        (x, first_gain, first_shift, ridge_matrix, memory_mean, memory_spread),
        [tokd, vrow, vrow, full((tok, NB)), full((H,)), full((H,))],
        [((prow, D), BF)], [full((prow, D))], [], tok * D * 10, tok * D * 6,
    )
    pieces = [across(payload, k) for k in peers]

    w_mine = jnp.concatenate(
        [
            jnp.pad(
                lax.dynamic_slice_in_dim(mixer_in, t * D + group * gw, gw, 1),
                ((0, 0), (0, lw - gw)),
            )
            for t in range(3)
        ],
        axis=1,
    )
    w_mine, _ = lax.optimization_barrier((w_mine, payload))
    w_parts = swap_pieces(w_mine, "shard", nsh)

    up_rows = lax.dynamic_slice_in_dim(up_weight, split * part, part)
    up_mine = jnp.concatenate(
        [
            lax.dynamic_slice_in_dim(up_rows, z * (ff // nsh) + group * each, each, 1)
            for z in range(nsh)
        ],
        axis=1,
    )
    down_mine = lax.dynamic_slice_in_dim(down_weight, group * each + split * part, part)
    out_mine = lax.dynamic_slice_in_dim(mixer_out, split * part, part)
    trio = jnp.stack([up_mine, down_mine, out_mine])
    trio, _ = lax.optimization_barrier((trio, (w_parts, pieces)))
    trio = lax.all_gather(trio, "shard", axis=1)

    pidx = place.reshape(1)
    tables = (deal_table, doc_starts, pidx)

    vectors = (out_bias, second_gain, second_shift, down_bias, first_gain, first_shift)
    here = jnp.stack([group, split, lax.axis_index("shard").astype(jnp.int32)])
    vrows = full((8, D))
    q, kv, w_group, vecs, up_b = call(
        qkv_kernel, geo, (here,), (1,),
        (*pieces, *w_parts, query_bias, value_bias, up_bias, *vectors),
        [full((prow, D))] * groups + [full((rows, 3 * lw))] * nsh + [vrow] * 2 + [full((ff,))]
        + [vrow] * len(vectors),
        [((qrows, lw), BF), ((qrows, 2 * lw), BF), ((D, 3 * lw), BF), ((8, D), F32),
         ((8, fg), F32)],
        [full((qrows, lw)), full((qrows, 2 * lw)), full((D, 3 * lw)), vrows, full((8, fg))],
        [], qrows * D * 6 * lw, qrows * D * 4, 0, 16,
    )
    others = [inside(kv, m) for m in range(1, splits)]
    upstream_later, _ = lax.optimization_barrier((upstream, q))
    planes = [[g * splits + c for g in peers] for c in range(splits)]
    gs = [upstream if k == 0 else across(upstream_later, k) for k in peers]

    wide = (seq + KT, lw)
    sems = pltpu.SemaphoreType.DMA((2 * nblk,))
    tiles = qrows * seq // 2
    moved = (3 * qrows + 3 * seq) * lw * 2
    comb, att = call(
        attn_fwd_kernel, geo, tables, (1,),
        (q, kv, *others, doc_starts),
        [full((qrows, lw))] + [ANY] * splits + [full((1, seq))],
        [((groups, tok * 3 // 4, 256), BF), ((qrows, lw), F32)],
        [full((groups, tok * 3 // 4, 256)), full((qrows, lw))],
        [vm(wide, BF)] * 3
        + [vm((qrows, lw), BF), vm((blk, lw), F32), vm((blk, lw), F32), sems],
        tiles * lw * 2 * (2 * hpg + 1), moved, tiles * hpg, 6 + seq // 512,
    )
    comb, gs, trio = lax.optimization_barrier((comb, gs, trio))
    trios = [trio if m == 0 else inside(trio, m) for m in range(splits)]
    w_up, w_down, w_out = call(
        assemble_kernel, geo, (sidx,), (1,), trios, [full((3, nsh, part, D))] * splits,
        [((nsh, splits, part, D), BF)] * 3, [full((nsh, splits, part, D))] * 3,
        [], 1000, 1000, 0, 16,
    )
    w_up, w_down, w_out = (w.reshape(D, D) for w in (w_up, w_down, w_out))
    w_out = w_out.reshape(groups, gw, D)
    trade = lambda v: lax.all_to_all(v, "ctx", 0, 0, axis_index_groups=planes, tiled=True)
    comb = trade(comb)

    resid, n2 = call(
        proj_kernel, geo, (), (1,), (comb, w_out, x, vecs),
        [full((groups, tok * 3 // 4, 256)), full((groups, gw, D)), tokd, vrows],
        [((tok, D), F32), ((tok, D), BF)], [tokd, tokd],
        [], tok * D * D * 2, tok * D * 12,
    )
    ys, dn2s, acts, dhids = [], [], [], []
    n2s = [n2]
    for k in peers:
        if k == 1:
            n2s += [across(n2, m) for m in range(1, groups - 1)]
            n2_last, *n2s = lax.optimization_barrier((n2, *n2s, ys[0]))[:-1]
            n2s.append(across(n2_last, groups - 1))
        outs = call(
            ffn_kernel, geo, (), (1,), (n2s[k], gs[k], w_up, w_down, up_b),
            [tokd, tokd, square, square, full((8, fg))],
            [((tok, D), BF)] * 4, [tokd] * 4,
            [vm((tok, D), F32), vm((tok, D), F32)], tok * D * fg * 8, tok * D * 12 + D * fg * 4, tok * fg,
        )
        ys.append(outs[0])
        dn2s.append(across(outs[1], k))
        acts.append(outs[2])
        dhids.append(outs[3])
    dresid, dproj, small2, *dcombs = call(
        post_kernel, geo, (gidx,), (1,), (*dn2s, w_out, resid, upstream, vecs),
        [tokd] * groups + [full((groups, gw, D)), tokd, tokd, vrows],
        [((tok, D), F32), ((tok, D), BF), ((8, D), F32)]
        + [((tok * 3 // 4, 256), BF)] * groups,
        [tokd, tokd, full((8, D))] + [full((tok * 3 // 4, 256))] * groups,
        [], tok * D * D * 2, tok * D * 20,
    )
    dcombs = [across(dcombs[k], k) for k in peers]
    *dms, dupb = call(
        ffn_grad_kernel, geo, (sidx,), (1,), (*n2s, *dhids, *acts, *gs),
        [tokd] * (4 * groups),
        [((nsh, 2 * parta, D), BF)] * splits + [((8, fg), F32)],
        [full((nsh, 2 * parta, D))] * splits + [full((8, fg))],
        [vm((D, D), F32)], qrows * D * fg * 4, qrows * D * 8,
    )
    dwouts = call(
        out_grad_kernel, geo, (here,), (1,), (comb, dproj),
        [full((groups, tok * 3 // 4, 256)), tokd],
        [((groups, nsh, sub, D), BF)] * splits, [full((groups, nsh, sub, D))] * splits,
        [], tok * D * D * 2, tok * D * 6,
    )
    dwouts = [dwouts[0]] + [inside(dwouts[m], m) for m in range(1, splits)]
    dms = [dms[0]] + [inside(dms[m], m) for m in range(1, splits)]
    (dm,) = call(
        sum_kernel, geo, (), (1,), dms, [full((nsh, 2 * parta, D))] * splits,
        [((nsh, 2 * parta, D), BF)], [full((nsh, 2 * parta, D))], [], 1000, 1000,
    )
    dm, dwouts, dcombs = lax.optimization_barrier((dm, dwouts, dcombs))
    erow = tok + nsh * sub
    exts = call(
        extend_kernel, geo, (), (1,), (*ys[1:], *dwouts),
        [tokd] * (groups - 1) + [full((groups, nsh, sub, D))] * splits,
        [((nsh * sub, D), BF)] + [((erow, D), BF)] * (groups - 1),
        [full((nsh * sub, D))] + [full((erow, D))] * (groups - 1),
        [], 1000, 1000,
    )
    dms, _ = lax.optimization_barrier((dms, dproj))
    dm = lax.psum_scatter(dm, "shard", scatter_dimension=0, tiled=False)

    dq, *dkvs = call(
        attn_bwd_kernel, geo, tables, (1,),
        (q, kv, *others, doc_starts, *dcombs, att),
        [ANY] * (splits + 1) + [full((1, seq))] + [ANY] * (groups + 1),
        [((qrows, lw), BF)] + [((qrows, 2 * lw), BF)] * splits,
        [ANY] * (splits + 1),
        [vm(wide, BF)] * 2
        + [vm((qrows, lw), BF), vm((blk, lw), F32), vm(wide, F32), vm(wide, F32),
           vm(wide, F32), vm((qrows, lw), BF), vm((qrows, lw), F32),
           vm((groups, tok * 3 // 4, 256), BF), vm((qrows, lw), BF),
           vm((splits, qrows, 2 * lw), BF), DMA((2 * nblk + 2 + groups,)), DMA((splits + 1,))],
        tiles * lw * 2 * (5 * hpg + 1), moved, tiles * hpg, 60,
    )
    later, _ = lax.optimization_barrier((exts, dcombs))
    exts = [across(later[k], k) for k in peers]
    dkvs, exts, dm = lax.optimization_barrier((dkvs, exts, dm))
    dkvs = [dkvs[0]] + [inside(dkvs[m], m) for m in range(1, splits)]
    m_g = lax.all_gather(dm, "ctx", axis=0)
    (result,) = call(
        result_kernel, geo, (), (1,), (ys[0], *exts[1:], resid, vecs),
        [tokd] + [full((erow, D))] * (groups - 1) + [tokd, vrows], [((tok, D), F32)], [tokd],
        [], tok * D * 8, tok * D * 16,
    )
    dqkv, *parts = call(
        dn1_kernel, geo, (), (1,), (dq, *dkvs, w_group),
        [full((qrows, lw))] + [full((qrows, 2 * lw))] * splits + [full((D, 3 * lw))],
        [((qrows, 3 * lw), BF)] + [((tok, D), BF)] * groups,
        [full((qrows, 3 * lw))] + [tokd] * groups,
        [], qrows * D * 6 * lw, qrows * D * 8, 0, 60,
    )
    mine = parts
    parts = [across(parts[k], k) for k in peers]

    prow = part * 3 // 4
    *wgs, vec1 = call(
        wgrad_kernel, geo, (gidx, sidx), (1,), (*pieces, *mine, dqkv),
        [full((tok + 2 * HP, D))] * groups + [tokd] * groups + [full((qrows, 3 * lw))],
        [((nsh, prow, 3 * lw), BF)] * splits + [((8, D), F32)],
        [full((nsh, prow, 3 * lw))] * splits + [full((8, D))],
        [vm((D, 3 * lw), F32)], qrows * D * 6 * lw, qrows * D * 4,
    )
    wgs = [wgs[0]] + [inside(wgs[m], m) for m in range(1, splits)]
    lrow = HP + prow + sub
    lates = call(
        late_kernel, geo, (here,), (1,), (*wgs, *exts, vec1, small2, dupb),
        [full((nsh, prow, 3 * lw))] * splits + [full((nsh * sub, D))]
        + [full((erow, D))] * (groups - 1) + [full((8, D)), full((8, D)), full((8, fg))],
        [((lrow, D), BF)] * nsh, [full((lrow, D))] * nsh,
        [vm((nsh, sub, D), F32), vm((HP, D), F32)], 1000, 1000,
    )
    zs = [lates[k] if k == 0 else swap(lates[k], "shard", nsh, k) for k in range(nsh)]
    (zsum,) = call(
        sum_kernel, geo, (), (1,), zs, [full((lrow, D))] * nsh,
        [((lrow, D), BF)], [full((lrow, D))], [], 1000, 1000,
    )
    zsum, parts, result = lax.optimization_barrier((zsum, parts, result))
    near = [across(zsum, k) for k in peers]
    (input_grad,) = call(
        tail_kernel, geo, (), (1,), (*parts, x, dresid, vecs),
        [tokd] * (groups + 2) + [vrows], [((tok, D), F32)], [tokd],
        [], tok * D * 20, tok * D * 20,
    )
    gblock = lambda r: pl.BlockSpec((nctx, parta, D), lambda j, *_: (0, r, 0))
    up_g, down_g = call(
        finish_kernel, geo, (), (1,), (m_g, m_g), [gblock(0), gblock(1)],
        [((rows, ff), F32), ((ff // nsh, D), F32)],
        [full((rows, ff)), full((ff // nsh, D))],
        [], 1000, rows * ff * 12,
    )
    near, input_grad = lax.optimization_barrier((near, input_grad))
    (stacked,) = call(
        stack_kernel, geo, (), (1,), near, [full((lrow, D))] * groups,
        [((groups, lrow, D), BF)], [full((groups, lrow, D))], [], 1000, 1000,
    )
    far = [inside(stacked, m) for m in range(1, splits)]
    in_g, out_g, gain_g, shift_g, qb_g, vb_g, ob_g, gain2_g, shift2_g, db_g, mean_g, spread_g, ub_g = call(
        finish_in_kernel, geo, (pidx,), (1,),
        (*near, *far, vecs),
        [full((lrow, D))] * groups + [full((groups, lrow, D))] * (splits - 1) + [vrows],
        [((rows, 3 * D), F32), ((nctx, sub, D), F32)] + [((D,), F32)] * 8
        + [((H,), F32)] * 2 + [((ff,), F32)],
        [full((rows, 3 * D)), full((nctx, sub, D))] + [vrow] * 8 + [full((H,))] * 2
        + [full((ff,))],
        [], 1000, rows * D * 20,
    )
    out_g = out_g.reshape(rows, D)
    small = (
        gain_g, shift_g, qb_g, vb_g, ob_g, gain2_g, shift2_g, ub_g, db_g, mean_g, spread_g
    )
    return (result[None], input_grad[None], in_g, out_g, up_g, down_g) + small


def solution(mesh):
    rows, split = P("shard", None), P("shard", "ctx", None)
    none = P()
    return jax.shard_map(
        per_device,
        mesh=mesh,
        in_specs=(
            split, split, rows, rows, none, P("ctx", None), none, none, rows, none, none, rows,
            none, none, none, rows, none, rows, none, none, none,
        ),
        out_specs=(split, split, rows, rows, rows, rows) + (none,) * 11,
        check_vma=False,
    )
```

```python
import functools
import math

import jax
import jax.numpy as jnp
from jax import lax
from jax.experimental import pallas as pl
from jax.experimental.pallas import tpu as pltpu
from jax.sharding import PartitionSpec as P

D = 768
H = 12
HD = 64
NB = 256
SEGL = 16

HIGH = lax.Precision.HIGHEST
EPS = 1e-05
BF = jnp.bfloat16
F32 = jnp.float32
KT = 256
FB = 256
NN = (((1,), (0,)), ((), ()))
NT = (((1,), (1,)), ((), ()))
TN = (((0,), (0,)), ((), ()))


def mm(a, b, dims=NN):
    return lax.dot_general(a, b, dims, preferred_element_type=F32)


def norm_stats(values):
    center = values - jnp.mean(values, axis=-1, keepdims=True)
    spread = jnp.mean(center * center, axis=-1, keepdims=True)
    recip = lax.rsqrt(spread + EPS)
    return center * recip, recip


def norm_back(upstream, unit, recip, gain):
    scaled = upstream * gain
    return recip * (
        scaled
        - jnp.mean(scaled, axis=-1, keepdims=True)
        - unit * jnp.mean(scaled * unit, axis=-1, keepdims=True)
    )


def swap(x, axis, count, k):
    return lax.ppermute(x, axis, [(i, i ^ k) for i in range(count)])


def swap_pieces(x, axis, count):
    out = [x]
    for k in range(1, count):
        if k > 2:
            x, _ = lax.optimization_barrier((x, out[-1]))
        out.append(swap(x, axis, count, k))
    return out


def lane_iota(rows, cols):
    return lax.broadcasted_iota(jnp.int32, (rows, cols), 1)


def row_iota(rows, cols):
    return lax.broadcasted_iota(jnp.int32, (rows, cols), 0)


def head_mask(rows, cols, head):
    lane = lane_iota(rows, cols)
    return (lane >= head * HD) & (lane < (head + 1) * HD)


HP = 16
VR = 32


def pack(value):
    cut = value.shape[0] * 3 // 4
    last = [value[cut:, h * HD : (h + 1) * HD] for h in range(3)]
    return jnp.concatenate([value[:cut, :], jnp.concatenate(last, axis=0)], axis=1)


def unpack(value):
    each, gw = value.shape[0] // 3, 3 * HD
    last = [value[h * each : (h + 1) * each, gw:] for h in range(3)]
    return jnp.concatenate([value[:, :gw], jnp.concatenate(last, axis=1)], axis=0)


def coef_spread(lw, gw, hpg):
    row, lane = row_iota(lw, lw), lane_iota(lw, lw)
    hit = (row >= gw) & (row < gw + hpg) & (lane < gw)
    hit = hit & (lane >= (row - gw) * HD) & (lane < (row - gw + 1) * HD)
    return jnp.where(hit, 1.0, 0.0).astype(BF)


def block_at(geo, deal, place, n):
    own, splits = geo["own"], geo["splits"]
    device = place[0] ^ (((n % own) // 2) * splits + n // own)
    return deal[2 * device + n % 2]


def starts_of(ref, p, blk):
    at = pl.multiple_of((p * blk) // 128 * 128, 128)
    window = ref[:, pl.ds(at, blk + 64)]
    return jnp.where((p * blk) % 128 == 0, window[:, :blk], window[:, 64:])


def own_lanes(stacked, blk, lw, hpg):
    out = jnp.zeros((blk, lw), F32)
    for h in range(hpg):
        out = jnp.where(head_mask(blk, lw, h), stacked[h * blk : (h + 1) * blk], out)
    return out


def fetch(pairs, sems, first=0):
    copies = [pltpu.make_async_copy(a, b, sems.at[first + i]) for i, (a, b) in enumerate(pairs)]
    for copy in copies:
        copy.start()
    return copies


def load_blocks(geo, deal, place, kv, others, k_s, v_s, sems):
    blk, lw, own, pad = geo["blk"], geo["lw"], geo["own"], KT
    for ref in (k_s, v_s):
        ref[0:pad, :] = jnp.zeros((pad, lw), BF)
    copies = []
    for n in range(geo["nblk"]):
        source = kv if n < own else others[n // own - 1]
        rows = pl.ds((n % own) * blk, blk)
        to = pl.ds(pl.multiple_of(pad + block_at(geo, deal, place, n) * blk, 64), blk)
        for j, ref in enumerate((k_s, v_s)):
            copies.append(
                pltpu.make_async_copy(
                    source.at[rows, pl.ds(j * lw, lw)], ref.at[to], sems.at[2 * n + j]
                )
            )
    for copy in copies:
        copy.start()
    return copies


def row(ref):
    return ref[...].reshape(1, ref.shape[0])


def column(values):
    at = row_iota(HP, H) == lane_iota(HP, H)
    return jnp.sum(jnp.where(at, values, 0.0), axis=1, keepdims=True)


def basis_rows(mean, spread):
    centers = (lane_iota(HP, NB).astype(F32) + 0.5) / NB
    widths = spread + 1.0 / (NB * NB)
    offset = mean - centers
    weights = jnp.exp(-0.5 * offset * offset / widths) * lax.rsqrt(2.0 * math.pi * widths) / NB
    ratio = offset / widths
    return weights, -weights * ratio, 0.5 * weights * (ratio * ratio - 1.0 / widths)


def prep_kernel(geo, x, gain, shift, ridge, mean, spread, out):
    tok = geo["tok"]
    unit, _ = norm_stats(x[...].astype(F32))
    out[0:tok, :] = (unit * row(gain) + row(shift)).astype(BF)
    out[tok : tok + 2 * HP, :] = jnp.zeros((2 * HP, D), BF)
    used = row_iota(HP, 1) < H
    spreads = jnp.where(used, column(row(spread)), 0.01)
    for i, basis in enumerate(basis_rows(column(row(mean)), spreads)):
        rows = lax.dot_general(basis, ridge[...], NT, precision=HIGH, preferred_element_type=F32)
        at, lanes = tok + HP * (i // 2), tok * (i % 2)
        out[at : at + HP, lanes : lanes + tok] = rows.astype(BF)


def qkv_kernel(geo, here, *refs):
    groups, nsh, rows, tok, lw, gw, hpg, fg = (
        geo[k] for k in ("groups", "nsh", "rows", "tok", "lw", "gw", "hpg", "fg")
    )
    pieces, parts = refs[:groups], refs[groups : groups + nsh]
    qbias, vbias, upb = refs[groups + nsh : groups + nsh + 3]
    vectors = refs[groups + nsh + 3 : -5]
    q, kv, w, vecs, ups = refs[-5:]
    group = here[0]
    for k in range(nsh):
        w[pl.ds(pl.multiple_of((here[2] ^ k) * rows, 16), rows), :] = parts[k][...]
    for i, ref in enumerate(vectors):
        vecs[i : i + 1, :] = row(ref)
    wide, each, mine = row(upb), fg // nsh, []
    for z in range(nsh):
        value = jnp.zeros((1, each), F32)
        for k in range(groups):
            at = (z * groups + k) * each
            value = jnp.where(group == k, wide[:, at : at + each], value)
        mine.append(value)
    ups[...] = jnp.broadcast_to(jnp.concatenate(mine, axis=1), ups.shape)
    head = row_iota(HP, lw) - group * hpg
    place = jnp.where((head >= 0) & (head < hpg) & (lane_iota(HP, lw) == gw + head), 1.0, 0.0)
    place = place.astype(BF)
    lane = lane_iota(1, lw)
    ones = jnp.where((lane >= gw) & (lane < gw + hpg), 1.0, 0.0)
    biases = []
    for ref in (qbias, vbias):
        wide = row(ref)
        mine = jnp.zeros((1, gw), F32)
        for g in range(groups):
            mine = jnp.where(group == g, wide[:, g * gw : (g + 1) * gw], mine)
        biases.append(jnp.concatenate([mine, jnp.zeros((1, lw - gw), F32)], axis=1))
    bias = jnp.concatenate([biases[0], jnp.zeros((1, lw), F32), biases[1] + ones], axis=1)
    for k in range(groups):
        rows = slice(k * tok, (k + 1) * tok)
        out = mm(pieces[k][0:tok, :], w[...]) + bias
        q[rows, :] = out[:, :lw].astype(BF)
        coef = mm(pieces[k][tok : tok + HP, 0:tok], place, TN)
        kv[rows, 0:lw] = (out[:, lw : 2 * lw] + coef).astype(BF)
        kv[rows, lw : 2 * lw] = out[:, 2 * lw :].astype(BF)


def attn_fwd_kernel(geo, deal, starts, place, *refs):
    splits, groups = geo["splits"], geo["groups"]
    q_s, kv, others, srow = refs[0], refs[1], refs[2 : splits + 1], refs[splits + 1]
    comb, att = refs[splits + 2 : splits + 4]
    k_s, v_s, c_s, comb_s, acc, mac, sems = refs[splits + 4 :]
    blk, lw, gw, hpg, own, pad = (geo[k] for k in ("blk", "lw", "gw", "hpg", "own", "pad"))
    for copy in load_blocks(geo, deal, place, kv, others, k_s, v_s, sems):
        copy.wait()
    group = place[0] // splits
    spread = coef_spread(lw, gw, hpg)
    zero = jnp.zeros((), BF)

    @pl.loop(0, (geo["seq"] + pad) // KT)
    def _(i):
        rows = pl.ds(pl.multiple_of(i * KT, KT), KT)
        c_s[rows, :] = (mm(k_s[rows, :], spread) * v_s[rows, :].astype(F32)).astype(BF)

    @pl.loop(0, own)
    def _(n):
        p = block_at(geo, deal, place, n)
        end = (p + 1) * blk
        mine = pl.ds(pl.multiple_of(n * blk, blk), blk)
        qb = q_s[mine, :].astype(F32) * (HD**-0.5)
        qm = [jnp.where(head_mask(blk, lw, h), qb, 0.0).astype(BF) for h in range(hpg)]
        qstart = jnp.broadcast_to(starts_of(srow, p, blk), (KT, blk)).T
        qpos = p * blk + row_iota(blk, KT)
        qlim = qpos - ((qpos - qstart) & (SEGL - 1))
        acc[...] = jnp.zeros_like(acc)
        mac[...] = jnp.zeros_like(mac)

        @pl.loop(0, (end - starts[0, p * blk] + KT - 1) // KT)
        def _(t):
            base = end - (t + 1) * KT
            rows = pl.ds(pl.multiple_of(pad + base, 64), KT)
            kt, vt, ct = k_s[rows, :], v_s[rows, :], c_s[rows, :]
            kpos = base + lane_iota(blk, KT)
            inside = kpos >= qstart
            visible = inside & (kpos <= qpos)
            earlier = inside & (kpos < qlim)
            numer = jnp.zeros((blk, lw), F32)
            for h in range(hpg):
                scores = mm(qm[h], kt, NT)
                probs = jnp.where(visible, jnp.exp(scores), 0.0).astype(BF)
                mine = head_mask(KT, lw, h) | (lane_iota(KT, lw) == gw + h)
                numer += mm(probs, jnp.where(mine, vt, zero))
            acc[...] += numer
            mac[...] += mm(jnp.where(earlier, 1.0, 0.0).astype(BF), ct)

        attended = acc[...]
        scale = jnp.ones((blk, lw), F32)
        for h in range(hpg):
            recip = 1.0 / acc[:, gw + h : gw + h + 1]
            scale = jnp.where(head_mask(blk, lw, h), recip, scale)
        attended = attended * scale
        att[mine, :] = attended
        comb_s[mine, :] = (attended + mac[...]).astype(BF)

    for k in range(groups):
        comb[group ^ k] = pack(comb_s[2 * k * blk : 2 * (k + 1) * blk, :gw])


def attn_bwd_kernel(geo, deal, starts, place, *refs):
    splits, groups, nblk = geo["splits"], geo["groups"], geo["nblk"]
    q_h, kv, others, srow = refs[0], refs[1], refs[2 : splits + 1], refs[splits + 1]
    dcombs = refs[splits + 2 : splits + 2 + groups]
    att_h, dq_h = refs[splits + 2 + groups : splits + 4 + groups]
    dkvs_h = refs[splits + 4 + groups : 2 * splits + 4 + groups]
    k_s, v_s, g_s, dq_a, dk_t, dv_t, r_t, q_s, att, dc_s, dq, dkv = refs[
        2 * splits + 4 + groups : -4
    ]
    qm, augs, sems, out_sems = refs[-4:]
    copies = [(q_h, q_s), (att_h, att)] + [(dcombs[k], dc_s.at[k]) for k in range(groups)]
    copies = fetch(copies, sems, 2 * nblk)
    blk, lw, gw, hpg, own, pad = (geo[k] for k in ("blk", "lw", "gw", "hpg", "own", "pad"))
    copies += load_blocks(geo, deal, place, kv, others, k_s, v_s, sems)
    scale = HD**-0.5

    @pl.loop(0, geo["seq"] // KT)
    def _(i):
        cols = pl.ds(pl.multiple_of(i * KT, KT), KT)
        for ref in (dk_t, dv_t, r_t):
            ref[:, cols] = jnp.zeros((gw, KT), F32)

    for copy in copies:
        copy.wait()
    for k in range(groups):
        rows = slice(2 * k * blk, 2 * (k + 1) * blk)
        g_s[rows, :] = jnp.concatenate(
            [unpack(dc_s[k]), jnp.zeros((2 * blk, lw - gw), BF)], axis=1
        )

    @pl.loop(0, own)
    def _(n):
        p = block_at(geo, deal, place, n)
        end = (p + 1) * blk
        mine = pl.ds(pl.multiple_of(n * blk, blk), blk)
        qb = q_s[mine, :].astype(F32) * scale
        wide = g_s[mine, :].astype(F32)
        saved = att[mine, :]
        prod = wide * saved
        lane = lane_iota(blk, lw)
        low = jnp.zeros((blk, lw), F32)
        for h in range(hpg):
            recip = 1.0 / saved[:, gw + h : gw + h + 1]
            only = head_mask(blk, lw, h)
            dtot = -jnp.sum(jnp.where(only, prod, 0.0), axis=1, keepdims=True) * recip
            high = dtot.astype(BF).astype(F32)
            dnum = jnp.where(only, wide * recip, 0.0)
            low += dnum
            aug = jnp.where(lane == gw, high, dnum)
            aug = jnp.where(lane == gw + 1, dtot - high, aug)
            stack = slice(h * blk, (h + 1) * blk)
            augs[stack, :] = aug.astype(BF)
            qm[stack, :] = jnp.where(only, qb, 0.0).astype(BF)
        q_t, dn_t, g_t = qb.astype(BF).T, low.astype(BF).T, g_s[mine, :].T
        qstart = jnp.broadcast_to(starts_of(srow, p, blk), (KT, blk)).T
        qpos = p * blk + row_iota(blk, KT)
        qlim = qpos - ((qpos - qstart) & (SEGL - 1))
        dq_a[...] = jnp.zeros_like(dq_a)

        lead = starts[0, p * blk] // 128 * 128
        count = (end - lead + KT - 1) // KT
        lead = jnp.minimum(lead, geo["seq"] - count * KT)

        @pl.loop(0, count)
        def _(t):
            base = lead + t * KT
            rows = pl.ds(pl.multiple_of(pad + base, 128), KT)
            cols = pl.ds(pl.multiple_of(base, 128), KT)
            kt, vt = k_s[rows, :], v_s[rows, :]
            kpos = base + lane_iota(blk, KT)
            inside = kpos >= qstart
            visible = inside & (kpos <= qpos)
            earlier = inside & (kpos < qlim)
            scores = mm(qm[...], kt, NT)
            dprobs = mm(augs[...], vt, NT)
            dscores = []
            for h in range(hpg):
                part, stack = slice(h * HD, (h + 1) * HD), slice(h * blk, (h + 1) * blk)
                probs = jnp.where(visible, jnp.exp(scores[stack]), 0.0)
                dscores.append((probs * dprobs[stack]).astype(BF))
                dv_t[part, cols] += mm(dn_t[part, :], probs.astype(BF))
                dk_t[part, cols] += mm(q_t[part, :], dscores[h])
            dque = mm(jnp.concatenate(dscores, axis=0), kt)
            dq_a[...] += own_lanes(dque, blk, lw, hpg)
            r_t[:, cols] += mm(g_t[:gw, :], jnp.where(earlier, 1.0, 0.0).astype(BF))

        dq[mine, :] = (dq_a[...] * scale).astype(BF)

    copies = fetch([(dq, dq_h)], out_sems, nblk)
    spread = coef_spread(lw, gw, hpg)

    @pl.loop(0, geo["seq"] // KT)
    def _(t):
        rows = pl.ds(pl.multiple_of(pad + t * KT, KT), KT)
        cols = pl.ds(pl.multiple_of(t * KT, KT), KT)
        fill = jnp.zeros((KT, lw - gw), F32)
        upright = lambda ref: jnp.concatenate([ref[:, cols].T, fill], axis=1)
        reach = upright(r_t)
        lane = lane_iota(KT, lw)
        dval = upright(dv_t) + reach * mm(k_s[rows, :], spread)
        prod = reach * v_s[rows, :].astype(F32)
        for h in range(hpg):
            part = jnp.where(head_mask(KT, lw, h), prod, 0.0)
            dval = jnp.where(lane == gw + h, jnp.sum(part, axis=1, keepdims=True), dval)
        narrow = dk_t[:, cols].astype(BF).T
        dkv[cols, 0:lw] = jnp.concatenate([narrow, fill.astype(BF)], axis=1)
        dkv[cols, lw : 2 * lw] = dval.astype(BF)

    for m in reversed(range(splits)):
        for n in range(m * own, (m + 1) * own):
            at = pl.ds(pl.multiple_of(block_at(geo, deal, place, n) * blk, 64), blk)
            to = pl.ds((n % own) * blk, blk)
            copies += fetch([(dkv.at[at], dkvs_h[m].at[to])], out_sems, n)
    for copy in copies:
        copy.wait()


def assemble_kernel(geo, split, *refs):
    splits, nsh = geo["splits"], geo["nsh"]
    for m in range(splits):
        for i in range(3):
            for z in range(nsh):
                refs[splits + i][z, split[0] ^ m] = refs[m][i, z]


def proj_kernel(geo, comb, wout, x, vecs, resid, n2):
    total = x[...].astype(F32) + vecs[0:1, :]
    for g in range(geo["groups"]):
        total += mm(unpack(comb[g]), wout[g])
    resid[...] = total
    unit, _ = norm_stats(total)
    n2[...] = (unit * vecs[1:2, :] + vecs[2:3, :]).astype(BF)


def ffn_kernel(geo, n2, g, wup, wdn, bias, y, dn2, act, dhid, ysum, dsum):
    fg = geo["fg"]
    ysum[...] = jnp.zeros_like(ysum)
    dsum[...] = jnp.zeros_like(dsum)

    @pl.loop(0, fg // FB)
    def _(b):
        cols = pl.ds(pl.multiple_of(b * FB, FB), FB)
        u = mm(n2[...], wup[:, cols]) + bias[0:1, cols]
        sq = u * u
        th = jnp.tanh(0.7978845608028654 * (u + 0.044715 * sq * u))
        half = 0.5 * (1.0 + th)
        a = (u * half).astype(BF)
        slope = half + 0.5 * u * (1.0 - th * th) * (0.7978845608028654 * (1.0 + 0.134145 * sq))
        d = (slope * mm(g[...], wdn[cols, :], NT)).astype(BF)
        act[:, cols] = a
        dhid[:, cols] = d
        ysum[...] += mm(a, wdn[cols, :])
        dsum[...] += mm(d, wup[:, cols], NT)

    y[...] = ysum[...].astype(BF)
    dn2[...] = dsum[...].astype(BF)


def ffn_grad_kernel(geo, split, *refs):
    groups, splits, nsh, part, parta, tok, fg = (
        geo[k] for k in ("groups", "splits", "nsh", "part", "parta", "tok", "fg")
    )
    n2s, dhids, acts, gs = (refs[i * groups : (i + 1) * groups] for i in range(4))
    outs, dupb, acc = refs[4 * groups : 4 * groups + splits], refs[-2], refs[-1]
    total = jnp.zeros((1, fg), F32)
    for ref in dhids:
        total += jnp.sum(ref[...].astype(F32), axis=0, keepdims=True)
    dupb[...] = jnp.broadcast_to(total, dupb.shape)
    for at, left, right in ((0, n2s, dhids), (parta, acts, gs)):
        flip = jnp.concatenate([ref[...].T for ref in left], axis=1)
        for b in range(0, fg, FB):
            side = jnp.concatenate([ref[:, b : b + FB] for ref in right])
            acc[:, b : b + FB] = mm(flip, side)
        for m in range(splits):
            for z in range(nsh):
                rows = (z * splits + (split[0] ^ m)) * part
                rows = pl.ds(pl.multiple_of(rows, 8), part)
                outs[m][z, at : at + part, :] = acc[rows, :].astype(BF)


def post_kernel(geo, group, *refs):
    groups = geo["groups"]
    dn2s, (wout, resid, g, vecs) = refs[:groups], refs[groups : groups + 4]
    dresid, dproj, small = refs[groups + 4 : groups + 7]
    dcombs = refs[groups + 7 :]
    unit, recip = norm_stats(resid[...])
    dn2 = dn2s[0][...].astype(F32)
    for ref in dn2s[1:]:
        dn2 += ref[...].astype(F32)
    wide = g[...].astype(F32)
    dres = wide + norm_back(dn2, unit, recip, vecs[1:2, :])
    dresid[...] = dres
    low = dres.astype(BF)
    dproj[...] = low
    for k in range(groups):
        dcombs[k][...] = pack(mm(low, wout[group[0] ^ k], NT).astype(BF))
    small[0:1, :] = jnp.sum(low.astype(F32), axis=0, keepdims=True)
    small[1:2, :] = jnp.sum(dn2 * unit, axis=0, keepdims=True)
    small[2:3, :] = jnp.sum(dn2, axis=0, keepdims=True)
    small[3:4, :] = jnp.sum(wide, axis=0, keepdims=True)
    small[4:8, :] = jnp.zeros((4, D), F32)


def out_grad_kernel(geo, here, comb, dproj, out):
    splits, nsh, gw = geo["splits"], geo["nsh"], geo["gw"]
    rows, sub = D // nsh, D // nsh // geo["nctx"]
    for g in range(geo["groups"]):
        value = mm(unpack(comb[g]), dproj[...], TN)
        for r in range(0, gw, sub):
            z, i = (g * gw + r) // rows, (g * gw + r) % rows // sub
            piece = value[r : r + sub, :].astype(BF)
            out[(i % splits) ^ here[1], (i // splits) ^ here[0], z] = piece


def extend_kernel(geo, *refs):
    groups, splits, nsh, tok = (geo[k] for k in ("groups", "splits", "nsh", "tok"))
    ys, grads, outs = refs[: groups - 1], refs[groups - 1 : groups - 1 + splits], refs[-groups:]
    for k in range(groups):
        total = grads[0][0, k].astype(F32)
        for ref in grads[1:]:
            total += ref[k].astype(F32)
        total = total.reshape(nsh * total.shape[1], D).astype(BF)
        if k == 0:
            outs[0][...] = total
        else:
            outs[k][0:tok, :] = ys[k - 1][...]
            outs[k][tok:, :] = total


def sum_kernel(geo, *refs):
    total = refs[0][...].astype(F32)
    for ref in refs[1:-1]:
        total += ref[...].astype(F32)
    refs[-1][...] = total.astype(BF)


def stack_kernel(geo, *refs):
    for k, ref in enumerate(refs[:-1]):
        refs[-1][k] = ref[...]


def late_kernel(geo, here, *refs):
    splits, groups, nsh, fg = (geo[k] for k in ("splits", "groups", "nsh", "fg"))
    sub = D // nsh // geo["nctx"]
    wgs, exts = refs[:splits], refs[splits : splits + groups]
    vec1, small2, dupb = refs[splits + groups : splits + groups + 3]
    outs, (dwout, vec) = refs[splits + groups + 3 : -2], refs[-2:]
    total = exts[0][...].astype(F32)
    for ref in exts[1:]:
        total += ref[geo["tok"] :, :].astype(F32)
    for z in range(nsh):
        dwout[z] = total[z * sub : (z + 1) * sub, :]
    vec[0:6, :] = vec1[0:6, :]
    vec[6:10, :] = small2[0:4, :]
    each, spans = fg // nsh, []
    for z in range(nsh):
        for g in range(groups):
            value = dupb[0:1, z * each : (z + 1) * each]
            spans.append(jnp.where(here[0] == g, value, 0.0))
    per = D // each
    for i in range(len(spans) // per):
        vec[10 + i : 11 + i, :] = jnp.concatenate(spans[i * per : (i + 1) * per], axis=1)
    vec[14:16, :] = jnp.zeros((2, D), F32)
    for k in range(nsh):
        z = here[2] ^ k
        total = wgs[0][z].astype(F32)
        for ref in wgs[1:]:
            total += ref[z].astype(F32)
        outs[k][...] = jnp.concatenate([vec[...], total, dwout[z]], axis=0).astype(BF)


def result_kernel(geo, *refs):
    groups = geo["groups"]
    ys, (resid, vecs, out) = refs[:groups], refs[groups:]
    total = resid[...] + vecs[3:4, :]
    for ref in ys:
        total += ref[0 : geo["tok"], :].astype(F32)
    out[...] = total


def dn1_kernel(geo, dq, *refs):
    splits, groups, tok, lw = (geo[k] for k in ("splits", "groups", "tok", "lw"))
    dkvs, (w, dqkv), parts = refs[:splits], refs[splits : splits + 2], refs[splits + 2 :]
    for k in range(groups):
        rows = slice(k * tok, (k + 1) * tok)
        both = dkvs[0][rows, :].astype(F32)
        for ref in dkvs[1:]:
            both += ref[rows, :].astype(F32)
        dqkv[rows, 0:lw] = dq[rows, :]
        dqkv[rows, lw : 3 * lw] = both.astype(BF)
        parts[k][...] = mm(dqkv[rows, :], w[...], NT).astype(BF)


def wgrad_kernel(geo, group, split, *refs):
    groups, splits, nsh, part, tok, lw, gw, hpg = (
        geo[k] for k in ("groups", "splits", "nsh", "part", "tok", "lw", "gw", "hpg")
    )
    pieces, parts, dqkv = refs[:groups], refs[groups : 2 * groups], refs[2 * groups]
    outs, (vec, acc) = refs[2 * groups + 1 : -2], refs[-2:]
    flip = jnp.concatenate([ref[0:tok, :].T for ref in pieces], axis=1)
    for b in range(0, 3 * lw, lw):
        acc[:, b : b + lw] = mm(flip, dqkv[:, b : b + lw])
    for m in range(splits):
        for z in range(nsh):
            rows = pl.ds(pl.multiple_of((z * splits + (split[0] ^ m)) * part, 8), part)
            for t in range(3):
                value = pack(acc[rows, t * lw : t * lw + gw])
                outs[m][z, :, t * lw : (t + 1) * lw] = value.astype(BF)
    plain = jnp.zeros((1, D), F32)
    cross = jnp.zeros((1, D), F32)
    means = jnp.zeros((HP, 128), F32)
    spreads = jnp.zeros((HP, 128), F32)
    for k in range(groups):
        dn1 = parts[k][...].astype(F32)
        plain += jnp.sum(dn1, axis=0, keepdims=True)
        cross += jnp.sum(dn1 * pieces[k][0:tok, :].astype(F32), axis=0, keepdims=True)
        dcoef = dqkv[k * tok : (k + 1) * tok, 3 * lw - 128 :]
        means += mm(pieces[k][tok : tok + HP, tok : 2 * tok], dcoef)
        spreads += mm(pieces[k][tok + HP : tok + 2 * HP, 0:tok], dcoef)
    total = jnp.sum(dqkv[...].astype(F32), axis=0, keepdims=True)
    vec[0:1, :] = cross
    vec[1:2, :] = plain
    head = row_iota(HP, 128) - group[0] * hpg
    hit = (head >= 0) & (head < hpg) & (lane_iota(HP, 128) == 128 - (lw - gw) + head)
    across = row_iota(HP, D) == lane_iota(HP, D)
    for i, value in enumerate((means, spreads)):
        value = jnp.sum(jnp.where(hit, value, 0.0), axis=1, keepdims=True)
        value = jnp.sum(jnp.where(across, value, 0.0), axis=0, keepdims=True)
        vec[4 + i : 5 + i, :] = value
    for i, t in enumerate((0, 2)):
        mine = total[:, t * lw : t * lw + gw]
        for g in range(groups):
            vec[2 + i : 3 + i, g * gw : (g + 1) * gw] = jnp.where(group[0] == g, mine, 0.0)
    vec[6:8, :] = jnp.zeros((2, D), F32)


def tail_kernel(geo, *refs):
    groups = geo["groups"]
    parts = refs[:groups]
    x, dresid, vecs, grad = refs[groups:]
    dn1 = parts[0][...].astype(F32)
    for ref in parts[1:]:
        dn1 += ref[...].astype(F32)
    unit, recip = norm_stats(x[...].astype(F32))
    grad[...] = dresid[...] + norm_back(dn1, unit, recip, vecs[4:5, :])


def finish_kernel(geo, ups, downs, up_g, down_g):
    groups, splits, nsh, part, fg, rows = (
        geo[k] for k in ("groups", "splits", "nsh", "part", "fg", "rows")
    )
    each = fg // nsh
    for i in range(groups * splits):
        g, c = i // splits, i % splits
        value = ups[i, 0:part, :].astype(F32)
        for z in range(nsh):
            at = z * groups * each + g * each
            up_g[c * part : (c + 1) * part, at : at + each] = value[:, z * each : (z + 1) * each]
        at = g * each + c * part
        down_g[at : at + part, :] = downs[i, 0:part, :].astype(F32)


def finish_in_kernel(geo, place, *refs):
    groups, splits, part, gw, lw = (geo[k] for k in ("groups", "splits", "part", "gw", "lw"))
    near, far, vecs = refs[:groups], refs[groups : groups + splits - 1], refs[-14]
    outs = refs[-13:]
    in_g, out_g = outs[:2]
    group, split = place[0] // splits, place[0] % splits
    prow = part * 3 // 4
    total = jnp.zeros((HP, D), F32)
    for k in range(groups):
        for m in range(splits):
            value = (near[k][...] if m == 0 else far[m - 1][k]).astype(F32)
            total += value[0:HP, :]
            out_g[place[0] ^ (k * splits + m)] = value[HP + prow :, :]
            rows = pl.ds(pl.multiple_of((split ^ m) * part, 8), part)
            wide = [unpack(value[HP : HP + prow, t * lw : (t + 1) * lw]) for t in range(3)]
            for g in range(groups):

                @pl.when((group ^ k) == g)
                def _():
                    for t in range(3):
                        in_g[rows, t * D + g * gw : t * D + (g + 1) * gw] = wide[t]

    flat = lambda i, n=D: total[i : i + 1, 0:n].reshape(n)
    outs[2][...] = ((total[0:1, :] - vecs[5:6, :] * total[1:2, :]) / vecs[4:5, :]).reshape(D)
    for ref, i in zip(outs[3:10], (1, 2, 3, 6, 7, 8, 9)):
        ref[...] = flat(i)
    outs[10][...] = flat(4, H)
    outs[11][...] = flat(5, H)
    for i in range(4):
        outs[12][i * D : (i + 1) * D] = flat(10 + i)


def full(shape):
    return pl.BlockSpec(shape, lambda *_: (0,) * len(shape))


ANY = pl.BlockSpec(memory_space=pl.ANY)
DMA = pltpu.SemaphoreType.DMA


def call(kernel, geo, scalars, grid, ins, in_specs, outs, out_specs, scratch, flops, moved, exps=0, limit=12):
    return pl.pallas_call(
        functools.partial(kernel, geo),
        grid_spec=pltpu.PrefetchScalarGridSpec(
            num_scalar_prefetch=len(scalars),
            grid=grid,
            in_specs=in_specs,
            out_specs=out_specs,
            scratch_shapes=scratch,
        ),
        out_shape=[jax.ShapeDtypeStruct(s, t) for s, t in outs],
        compiler_params=pltpu.CompilerParams(vmem_limit_bytes=limit << 20),
        cost_estimate=pl.CostEstimate(flops=1000, bytes_accessed=1000, transcendentals=0),
    )(*scalars, *ins)


def per_device(
    inputs,
    out_grad,
    segment_ids,
    doc_starts,
    deal_table,
    ridge_matrix,
    first_gain,
    first_shift,
    mixer_in,
    query_bias,
    value_bias,
    mixer_out,
    out_bias,
    second_gain,
    second_shift,
    up_weight,
    up_bias,
    down_weight,
    down_bias,
    memory_mean,
    memory_spread,
):
    tok = inputs.shape[1]
    blk = tok // 2
    nctx, nsh = lax.axis_size("ctx"), lax.axis_size("shard")
    place = lax.axis_index("ctx").astype(jnp.int32)
    seq, nblk = tok * nctx, 2 * nctx
    groups = math.gcd(H, nctx)
    splits = nctx // groups
    hpg = H // groups
    gw = hpg * HD
    lw = -(-(gw + hpg) // 128) * 128
    own = 2 * groups
    group, split = place // splits, place % splits
    ff = up_weight.shape[1]
    fg = ff // groups
    each = fg // nsh
    rows = D // nsh
    part = rows // splits
    parta = -(-part // 16) * 16
    sub = rows // nctx
    qrows = groups * tok
    geo = dict(
        tok=tok, blk=blk, seq=seq, nblk=nblk, groups=groups, splits=splits, hpg=hpg, gw=gw, lw=lw,
        own=own, pad=KT, nctx=nctx, nsh=nsh, fg=fg, rows=rows, part=part, parta=parta,
    )
    x = inputs[0]
    upstream = out_grad[0]
    peers = range(groups)
    across = lambda v, k: v if k == 0 else swap(v, "ctx", nctx, k * splits)
    inside = lambda v, m: swap(v, "ctx", nctx, m)
    gidx, sidx = group.reshape(1), split.reshape(1)
    vm = pltpu.VMEM
    zero = lambda n: jnp.zeros((n, D), F32)
    vrow = full((D,))
    tokd, square = full((tok, D)), full((D, D))

    prow = tok + 2 * HP
    (payload,) = call(
        prep_kernel, geo, (), (1,),
        (x, first_gain, first_shift, ridge_matrix, memory_mean, memory_spread),
        [tokd, vrow, vrow, full((tok, NB)), full((H,)), full((H,))],
        [((prow, D), BF)], [full((prow, D))], [], tok * D * 10, tok * D * 6,
    )
    pieces = [across(payload, k) for k in peers]

    w_mine = jnp.concatenate(
        [
            jnp.pad(
                lax.dynamic_slice_in_dim(mixer_in, t * D + group * gw, gw, 1),
                ((0, 0), (0, lw - gw)),
            )
            for t in range(3)
        ],
        axis=1,
    )
    w_mine, _ = lax.optimization_barrier((w_mine, payload))
    w_parts = swap_pieces(w_mine, "shard", nsh)

    up_rows = lax.dynamic_slice_in_dim(up_weight, split * part, part)
    up_mine = jnp.concatenate(
        [
            lax.dynamic_slice_in_dim(up_rows, z * (ff // nsh) + group * each, each, 1)
            for z in range(nsh)
        ],
        axis=1,
    )
    down_mine = lax.dynamic_slice_in_dim(down_weight, group * each + split * part, part)
    out_mine = lax.dynamic_slice_in_dim(mixer_out, split * part, part)
    trio = jnp.stack([up_mine, down_mine, out_mine])
    trio, _ = lax.optimization_barrier((trio, (w_parts, pieces)))
    trio = lax.all_gather(trio, "shard", axis=1)

    pidx = place.reshape(1)
    tables = (deal_table, doc_starts, pidx)

    vectors = (out_bias, second_gain, second_shift, down_bias, first_gain, first_shift)
    here = jnp.stack([group, split, lax.axis_index("shard").astype(jnp.int32)])
    vrows = full((8, D))
    q, kv, w_group, vecs, up_b = call(
        qkv_kernel, geo, (here,), (1,),
        (*pieces, *w_parts, query_bias, value_bias, up_bias, *vectors),
        [full((prow, D))] * groups + [full((rows, 3 * lw))] * nsh + [vrow] * 2 + [full((ff,))]
        + [vrow] * len(vectors),
        [((qrows, lw), BF), ((qrows, 2 * lw), BF), ((D, 3 * lw), BF), ((8, D), F32),
         ((8, fg), F32)],
        [full((qrows, lw)), full((qrows, 2 * lw)), full((D, 3 * lw)), vrows, full((8, fg))],
        [], qrows * D * 6 * lw, qrows * D * 4, 0, 16,
    )
    others = [inside(kv, m) for m in range(1, splits)]
    upstream_later, _ = lax.optimization_barrier((upstream, q))
    planes = [[g * splits + c for g in peers] for c in range(splits)]
    gs = [upstream if k == 0 else across(upstream_later, k) for k in peers]

    wide = (seq + KT, lw)
    sems = pltpu.SemaphoreType.DMA((2 * nblk,))
    tiles = qrows * seq // 2
    moved = (3 * qrows + 3 * seq) * lw * 2
    comb, att = call(
        attn_fwd_kernel, geo, tables, (1,),
        (q, kv, *others, doc_starts),
        [full((qrows, lw))] + [ANY] * splits + [full((1, seq))],
        [((groups, tok * 3 // 4, 256), BF), ((qrows, lw), F32)],
        [full((groups, tok * 3 // 4, 256)), full((qrows, lw))],
        [vm(wide, BF)] * 3
        + [vm((qrows, lw), BF), vm((blk, lw), F32), vm((blk, lw), F32), sems],
        tiles * lw * 2 * (2 * hpg + 1), moved, tiles * hpg, 6 + seq // 512,
    )
    comb, gs, trio = lax.optimization_barrier((comb, gs, trio))
    trios = [trio if m == 0 else inside(trio, m) for m in range(splits)]
    w_up, w_down, w_out = call(
        assemble_kernel, geo, (sidx,), (1,), trios, [full((3, nsh, part, D))] * splits,
        [((nsh, splits, part, D), BF)] * 3, [full((nsh, splits, part, D))] * 3,
        [], 1000, 1000, 0, 16,
    )
    w_up, w_down, w_out = (w.reshape(D, D) for w in (w_up, w_down, w_out))
    w_out = w_out.reshape(groups, gw, D)
    trade = lambda v: lax.all_to_all(v, "ctx", 0, 0, axis_index_groups=planes, tiled=True)
    comb = trade(comb)

    resid, n2 = call(
        proj_kernel, geo, (), (1,), (comb, w_out, x, vecs),
        [full((groups, tok * 3 // 4, 256)), full((groups, gw, D)), tokd, vrows],
        [((tok, D), F32), ((tok, D), BF)], [tokd, tokd],
        [], tok * D * D * 2, tok * D * 12,
    )
    ys, dn2s, acts, dhids = [], [], [], []
    n2s = [n2]
    for k in peers:
        if k == 1:
            n2s += [across(n2, m) for m in range(1, groups - 1)]
            n2_last, *n2s = lax.optimization_barrier((n2, *n2s, ys[0]))[:-1]
            n2s.append(across(n2_last, groups - 1))
        outs = call(
            ffn_kernel, geo, (), (1,), (n2s[k], gs[k], w_up, w_down, up_b),
            [tokd, tokd, square, square, full((8, fg))],
            [((tok, D), BF)] * 4, [tokd] * 4,
            [vm((tok, D), F32), vm((tok, D), F32)], tok * D * fg * 8, tok * D * 12 + D * fg * 4, tok * fg,
        )
        ys.append(outs[0])
        dn2s.append(across(outs[1], k))
        acts.append(outs[2])
        dhids.append(outs[3])
    dresid, dproj, small2, *dcombs = call(
        post_kernel, geo, (gidx,), (1,), (*dn2s, w_out, resid, upstream, vecs),
        [tokd] * groups + [full((groups, gw, D)), tokd, tokd, vrows],
        [((tok, D), F32), ((tok, D), BF), ((8, D), F32)]
        + [((tok * 3 // 4, 256), BF)] * groups,
        [tokd, tokd, full((8, D))] + [full((tok * 3 // 4, 256))] * groups,
        [], tok * D * D * 2, tok * D * 20,
    )
    dcombs = [across(dcombs[k], k) for k in peers]
    *dms, dupb = call(
        ffn_grad_kernel, geo, (sidx,), (1,), (*n2s, *dhids, *acts, *gs),
        [tokd] * (4 * groups),
        [((nsh, 2 * parta, D), BF)] * splits + [((8, fg), F32)],
        [full((nsh, 2 * parta, D))] * splits + [full((8, fg))],
        [vm((D, D), F32)], qrows * D * fg * 4, qrows * D * 8,
    )
    (dwout,) = call(
        out_grad_kernel, geo, (here,), (1,), (comb, dproj),
        [full((groups, tok * 3 // 4, 256)), tokd],
        [((splits, groups, nsh, sub, D), BF)], [full((splits, groups, nsh, sub, D))],
        [], tok * D * D * 2, tok * D * 6,
    )
    dwouts = [dwout] + [inside(dwout[m], m) for m in range(1, splits)]
    dms = [dms[0]] + [inside(dms[m], m) for m in range(1, splits)]
    (dm,) = call(
        sum_kernel, geo, (), (1,), dms, [full((nsh, 2 * parta, D))] * splits,
        [((nsh, 2 * parta, D), BF)], [full((nsh, 2 * parta, D))], [], 1000, 1000,
    )
    dm, dwouts, dcombs = lax.optimization_barrier((dm, dwouts, dcombs))
    erow = tok + nsh * sub
    exts = call(
        extend_kernel, geo, (), (1,), (*ys[1:], *dwouts),
        [tokd] * (groups - 1)
        + [pl.BlockSpec((1, groups, nsh, sub, D), lambda *_: (0, 0, 0, 0, 0))]
        + [full((groups, nsh, sub, D))] * (splits - 1),
        [((nsh * sub, D), BF)] + [((erow, D), BF)] * (groups - 1),
        [full((nsh * sub, D))] + [full((erow, D))] * (groups - 1),
        [], 1000, 1000,
    )
    dms, _ = lax.optimization_barrier((dms, dproj))
    dm = lax.psum_scatter(dm, "shard", scatter_dimension=0, tiled=False)

    dq, *dkvs = call(
        attn_bwd_kernel, geo, tables, (1,),
        (q, kv, *others, doc_starts, *dcombs, att),
        [ANY] * (splits + 1) + [full((1, seq))] + [ANY] * (groups + 1),
        [((qrows, lw), BF)] + [((qrows, 2 * lw), BF)] * splits,
        [ANY] * (splits + 1),
        [vm(wide, BF)] * 2
        + [vm((qrows, lw), BF), vm((blk, lw), F32)] + [vm((gw, seq), F32)] * 3
        + [vm((qrows, lw), BF), vm((qrows, lw), F32), vm((groups, tok * 3 // 4, 256), BF),
           vm((qrows, lw), BF), vm((seq, 2 * lw), BF), vm((hpg * blk, lw), BF),
           vm((hpg * blk, lw), BF), DMA((2 * nblk + 2 + groups,)),
           DMA((nblk + 1,))],
        tiles * lw * 2 * (5 * hpg + 1), moved, tiles * hpg, 60,
    )
    later, _ = lax.optimization_barrier((exts, dcombs))
    exts = [across(later[k], k) for k in peers]
    dkvs, exts, dm = lax.optimization_barrier((dkvs, exts, dm))
    dkvs = [dkvs[0]] + [inside(dkvs[m], m) for m in range(1, splits)]
    m_g = lax.all_gather(dm, "ctx", axis=0)
    (result,) = call(
        result_kernel, geo, (), (1,), (ys[0], *exts[1:], resid, vecs),
        [tokd] + [full((erow, D))] * (groups - 1) + [tokd, vrows], [((tok, D), F32)], [tokd],
        [], tok * D * 8, tok * D * 16,
    )
    dqkv, *parts = call(
        dn1_kernel, geo, (), (1,), (dq, *dkvs, w_group),
        [full((qrows, lw))] + [full((qrows, 2 * lw))] * splits + [full((D, 3 * lw))],
        [((qrows, 3 * lw), BF)] + [((tok, D), BF)] * groups,
        [full((qrows, 3 * lw))] + [tokd] * groups,
        [], qrows * D * 6 * lw, qrows * D * 8, 0, 60,
    )
    mine = parts
    parts = [across(parts[k], k) for k in peers]

    prow = part * 3 // 4
    *wgs, vec1 = call(
        wgrad_kernel, geo, (gidx, sidx), (1,), (*pieces, *mine, dqkv),
        [full((tok + 2 * HP, D))] * groups + [tokd] * groups + [full((qrows, 3 * lw))],
        [((nsh, prow, 3 * lw), BF)] * splits + [((8, D), F32)],
        [full((nsh, prow, 3 * lw))] * splits + [full((8, D))],
        [vm((D, 3 * lw), F32)], qrows * D * 6 * lw, qrows * D * 4, 0, 60,
    )
    wgs = [wgs[0]] + [inside(wgs[m], m) for m in range(1, splits)]
    lrow = HP + prow + sub
    lates = call(
        late_kernel, geo, (here,), (1,), (*wgs, *exts, vec1, small2, dupb),
        [full((nsh, prow, 3 * lw))] * splits + [full((nsh * sub, D))]
        + [full((erow, D))] * (groups - 1) + [full((8, D)), full((8, D)), full((8, fg))],
        [((lrow, D), BF)] * nsh, [full((lrow, D))] * nsh,
        [vm((nsh, sub, D), F32), vm((HP, D), F32)], 1000, 1000,
    )
    zs = [lates[k] if k == 0 else swap(lates[k], "shard", nsh, k) for k in range(nsh)]
    (zsum,) = call(
        sum_kernel, geo, (), (1,), zs, [full((lrow, D))] * nsh,
        [((lrow, D), BF)], [full((lrow, D))], [], 1000, 1000,
    )
    zsum, parts, result = lax.optimization_barrier((zsum, parts, result))
    near = [across(zsum, k) for k in peers]
    (input_grad,) = call(
        tail_kernel, geo, (), (1,), (*parts, x, dresid, vecs),
        [tokd] * (groups + 2) + [vrows], [((tok, D), F32)], [tokd],
        [], tok * D * 20, tok * D * 20,
    )
    gblock = lambda r: pl.BlockSpec((nctx, parta, D), lambda j, *_: (0, r, 0))
    up_g, down_g = call(
        finish_kernel, geo, (), (1,), (m_g, m_g), [gblock(0), gblock(1)],
        [((rows, ff), F32), ((ff // nsh, D), F32)],
        [full((rows, ff)), full((ff // nsh, D))],
        [], 1000, rows * ff * 12,
    )
    near, input_grad = lax.optimization_barrier((near, input_grad))
    (stacked,) = call(
        stack_kernel, geo, (), (1,), near, [full((lrow, D))] * groups,
        [((groups, lrow, D), BF)], [full((groups, lrow, D))], [], 1000, 1000,
    )
    far = [inside(stacked, m) for m in range(1, splits)]
    in_g, out_g, gain_g, shift_g, qb_g, vb_g, ob_g, gain2_g, shift2_g, db_g, mean_g, spread_g, ub_g = call(
        finish_in_kernel, geo, (pidx,), (1,),
        (*near, *far, vecs),
        [full((lrow, D))] * groups + [full((groups, lrow, D))] * (splits - 1) + [vrows],
        [((rows, 3 * D), F32), ((nctx, sub, D), F32)] + [((D,), F32)] * 8
        + [((H,), F32)] * 2 + [((ff,), F32)],
        [full((rows, 3 * D)), full((nctx, sub, D))] + [vrow] * 8 + [full((H,))] * 2
        + [full((ff,))],
        [], 1000, rows * D * 20,
    )
    out_g = out_g.reshape(rows, D)
    small = (
        gain_g, shift_g, qb_g, vb_g, ob_g, gain2_g, shift2_g, ub_g, db_g, mean_g, spread_g
    )
    return (result[None], input_grad[None], in_g, out_g, up_g, down_g) + small


def solution(mesh):
    rows, split = P("shard", None), P("shard", "ctx", None)
    none = P()
    return jax.shard_map(
        per_device,
        mesh=mesh,
        in_specs=(
            split, split, rows, rows, none, P("ctx", None), none, none, rows, none, none, rows,
            none, none, none, rows, none, rows, none, none, none,
        ),
        out_specs=(split, split, rows, rows, rows, rows) + (none,) * 11,
        check_vma=False,
    )
```

```python
import functools
import math

import jax
import jax.numpy as jnp
from jax import lax
from jax.experimental import pallas as pl
from jax.experimental.pallas import tpu as pltpu
from jax.sharding import PartitionSpec as P

D = 768
H = 12
HD = 64
NB = 256
SEGL = 16

HIGH = lax.Precision.HIGHEST
EPS = 1e-05
BF = jnp.bfloat16
F32 = jnp.float32
KT = 256
FB = 256
NN = (((1,), (0,)), ((), ()))
NT = (((1,), (1,)), ((), ()))
TN = (((0,), (0,)), ((), ()))


def mm(a, b, dims=NN):
    return lax.dot_general(a, b, dims, preferred_element_type=F32)


def norm_stats(values):
    center = values - jnp.mean(values, axis=-1, keepdims=True)
    spread = jnp.mean(center * center, axis=-1, keepdims=True)
    recip = lax.rsqrt(spread + EPS)
    return center * recip, recip


def norm_back(upstream, unit, recip, gain):
    scaled = upstream * gain
    return recip * (
        scaled
        - jnp.mean(scaled, axis=-1, keepdims=True)
        - unit * jnp.mean(scaled * unit, axis=-1, keepdims=True)
    )


def swap(x, axis, count, k):
    return lax.ppermute(x, axis, [(i, i ^ k) for i in range(count)])


def swap_pieces(x, axis, count):
    out = [x]
    for k in range(1, count):
        if k > 2:
            x, _ = lax.optimization_barrier((x, out[-1]))
        out.append(swap(x, axis, count, k))
    return out


def lane_iota(rows, cols):
    return lax.broadcasted_iota(jnp.int32, (rows, cols), 1)


def row_iota(rows, cols):
    return lax.broadcasted_iota(jnp.int32, (rows, cols), 0)


def head_mask(rows, cols, head):
    lane = lane_iota(rows, cols)
    return (lane >= head * HD) & (lane < (head + 1) * HD)


HP = 16
VR = 32


def pack(value):
    cut = value.shape[0] * 3 // 4
    last = [value[cut:, h * HD : (h + 1) * HD] for h in range(3)]
    return jnp.concatenate([value[:cut, :], jnp.concatenate(last, axis=0)], axis=1)


def unpack(value):
    each, gw = value.shape[0] // 3, 3 * HD
    last = [value[h * each : (h + 1) * each, gw:] for h in range(3)]
    return jnp.concatenate([value[:, :gw], jnp.concatenate(last, axis=1)], axis=0)


def coef_spread(lw, gw, hpg):
    row, lane = row_iota(lw, lw), lane_iota(lw, lw)
    hit = (row >= gw) & (row < gw + hpg) & (lane < gw)
    hit = hit & (lane >= (row - gw) * HD) & (lane < (row - gw + 1) * HD)
    return jnp.where(hit, 1.0, 0.0).astype(BF)


def block_at(geo, deal, place, n):
    own, splits = geo["own"], geo["splits"]
    device = place[0] ^ (((n % own) // 2) * splits + n // own)
    return deal[2 * device + n % 2]


def starts_of(ref, p, blk):
    at = pl.multiple_of((p * blk) // 128 * 128, 128)
    window = ref[:, pl.ds(at, blk + 64)]
    return jnp.where((p * blk) % 128 == 0, window[:, :blk], window[:, 64:])


def own_lanes(stacked, blk, lw, hpg):
    out = jnp.zeros((blk, lw), F32)
    for h in range(hpg):
        out = jnp.where(head_mask(blk, lw, h), stacked[h * blk : (h + 1) * blk], out)
    return out


def fetch(pairs, sems, first=0):
    copies = [pltpu.make_async_copy(a, b, sems.at[first + i]) for i, (a, b) in enumerate(pairs)]
    for copy in copies:
        copy.start()
    return copies


def load_blocks(geo, deal, place, kv, others, k_s, v_s, sems):
    blk, lw, own, pad = geo["blk"], geo["lw"], geo["own"], KT
    for ref in (k_s, v_s):
        ref[0:pad, :] = jnp.zeros((pad, lw), BF)
    copies = []
    for n in range(geo["nblk"]):
        source = kv if n < own else others[n // own - 1]
        rows = pl.ds((n % own) * blk, blk)
        to = pl.ds(pl.multiple_of(pad + block_at(geo, deal, place, n) * blk, 64), blk)
        for j, ref in enumerate((k_s, v_s)):
            copies.append(
                pltpu.make_async_copy(
                    source.at[rows, pl.ds(j * lw, lw)], ref.at[to], sems.at[2 * n + j]
                )
            )
    for copy in copies:
        copy.start()
    return copies


def row(ref):
    return ref[...].reshape(1, ref.shape[0])


def column(values):
    at = row_iota(HP, H) == lane_iota(HP, H)
    return jnp.sum(jnp.where(at, values, 0.0), axis=1, keepdims=True)


def basis_rows(mean, spread):
    centers = (lane_iota(HP, NB).astype(F32) + 0.5) / NB
    widths = spread + 1.0 / (NB * NB)
    offset = mean - centers
    weights = jnp.exp(-0.5 * offset * offset / widths) * lax.rsqrt(2.0 * math.pi * widths) / NB
    ratio = offset / widths
    return weights, -weights * ratio, 0.5 * weights * (ratio * ratio - 1.0 / widths)


def prep_kernel(geo, x, gain, shift, ridge, mean, spread, out):
    tok = geo["tok"]
    unit, _ = norm_stats(x[...].astype(F32))
    out[0:tok, :] = (unit * row(gain) + row(shift)).astype(BF)
    out[tok : tok + 2 * HP, :] = jnp.zeros((2 * HP, D), BF)
    used = row_iota(HP, 1) < H
    spreads = jnp.where(used, column(row(spread)), 0.01)
    for i, basis in enumerate(basis_rows(column(row(mean)), spreads)):
        rows = lax.dot_general(basis, ridge[...], NT, precision=HIGH, preferred_element_type=F32)
        at, lanes = tok + HP * (i // 2), tok * (i % 2)
        out[at : at + HP, lanes : lanes + tok] = rows.astype(BF)


def qkv_kernel(geo, here, *refs):
    groups, nsh, rows, tok, lw, gw, hpg, fg = (
        geo[k] for k in ("groups", "nsh", "rows", "tok", "lw", "gw", "hpg", "fg")
    )
    pieces, parts = refs[:groups], refs[groups : groups + nsh]
    qbias, vbias, upb = refs[groups + nsh : groups + nsh + 3]
    vectors = refs[groups + nsh + 3 : -5]
    q, kv, w, vecs, ups = refs[-5:]
    group = here[0]
    for k in range(nsh):
        w[pl.ds(pl.multiple_of((here[2] ^ k) * rows, 16), rows), :] = parts[k][...]
    for i, ref in enumerate(vectors):
        vecs[i : i + 1, :] = row(ref)
    wide, each, mine = row(upb), fg // nsh, []
    for z in range(nsh):
        value = jnp.zeros((1, each), F32)
        for k in range(groups):
            at = (z * groups + k) * each
            value = jnp.where(group == k, wide[:, at : at + each], value)
        mine.append(value)
    ups[...] = jnp.broadcast_to(jnp.concatenate(mine, axis=1), ups.shape)
    head = row_iota(HP, lw) - group * hpg
    place = jnp.where((head >= 0) & (head < hpg) & (lane_iota(HP, lw) == gw + head), 1.0, 0.0)
    place = place.astype(BF)
    lane = lane_iota(1, lw)
    ones = jnp.where((lane >= gw) & (lane < gw + hpg), 1.0, 0.0)
    biases = []
    for ref in (qbias, vbias):
        wide = row(ref)
        mine = jnp.zeros((1, gw), F32)
        for g in range(groups):
            mine = jnp.where(group == g, wide[:, g * gw : (g + 1) * gw], mine)
        biases.append(jnp.concatenate([mine, jnp.zeros((1, lw - gw), F32)], axis=1))
    bias = jnp.concatenate([biases[0], jnp.zeros((1, lw), F32), biases[1] + ones], axis=1)
    for k in range(groups):
        rows = slice(k * tok, (k + 1) * tok)
        out = mm(pieces[k][0:tok, :], w[...]) + bias
        q[rows, :] = out[:, :lw].astype(BF)
        coef = mm(pieces[k][tok : tok + HP, 0:tok], place, TN)
        kv[rows, 0:lw] = (out[:, lw : 2 * lw] + coef).astype(BF)
        kv[rows, lw : 2 * lw] = out[:, 2 * lw :].astype(BF)


def attn_fwd_kernel(geo, deal, starts, place, *refs):
    splits, groups = geo["splits"], geo["groups"]
    q_s, kv, others, srow = refs[0], refs[1], refs[2 : splits + 1], refs[splits + 1]
    comb, att = refs[splits + 2 : splits + 4]
    k_s, v_s, c_s, comb_s, acc, mac, sems = refs[splits + 4 :]
    blk, lw, gw, hpg, own, pad = (geo[k] for k in ("blk", "lw", "gw", "hpg", "own", "pad"))
    for copy in load_blocks(geo, deal, place, kv, others, k_s, v_s, sems):
        copy.wait()
    group = place[0] // splits
    spread = coef_spread(lw, gw, hpg)
    zero = jnp.zeros((), BF)

    @pl.loop(0, (geo["seq"] + pad) // KT)
    def _(i):
        rows = pl.ds(pl.multiple_of(i * KT, KT), KT)
        c_s[rows, :] = (mm(k_s[rows, :], spread) * v_s[rows, :].astype(F32)).astype(BF)

    @pl.loop(0, own)
    def _(n):
        p = block_at(geo, deal, place, n)
        end = (p + 1) * blk
        mine = pl.ds(pl.multiple_of(n * blk, blk), blk)
        qb = q_s[mine, :].astype(F32) * (HD**-0.5)
        qm = [jnp.where(head_mask(blk, lw, h), qb, 0.0).astype(BF) for h in range(hpg)]
        qstart = jnp.broadcast_to(starts_of(srow, p, blk), (KT, blk)).T
        qpos = p * blk + row_iota(blk, KT)
        qlim = qpos - ((qpos - qstart) & (SEGL - 1))
        acc[...] = jnp.zeros_like(acc)
        mac[...] = jnp.zeros_like(mac)

        @pl.loop(0, (end - starts[0, p * blk] + KT - 1) // KT)
        def _(t):
            base = end - (t + 1) * KT
            rows = pl.ds(pl.multiple_of(pad + base, 64), KT)
            kt, vt, ct = k_s[rows, :], v_s[rows, :], c_s[rows, :]
            kpos = base + lane_iota(blk, KT)
            inside = kpos >= qstart
            visible = inside & (kpos <= qpos)
            earlier = inside & (kpos < qlim)
            numer = jnp.zeros((blk, lw), F32)
            for h in range(hpg):
                scores = mm(qm[h], kt, NT)
                probs = jnp.where(visible, jnp.exp(scores), 0.0).astype(BF)
                mine = head_mask(KT, lw, h) | (lane_iota(KT, lw) == gw + h)
                numer += mm(probs, jnp.where(mine, vt, zero))
            acc[...] += numer
            mac[...] += mm(jnp.where(earlier, 1.0, 0.0).astype(BF), ct)

        attended = acc[...]
        scale = jnp.ones((blk, lw), F32)
        for h in range(hpg):
            recip = 1.0 / acc[:, gw + h : gw + h + 1]
            scale = jnp.where(head_mask(blk, lw, h), recip, scale)
        attended = attended * scale
        att[mine, :] = attended
        comb_s[mine, :] = (attended + mac[...]).astype(BF)

    for k in range(groups):
        comb[group ^ k] = pack(comb_s[2 * k * blk : 2 * (k + 1) * blk, :gw])


def attn_bwd_kernel(geo, deal, starts, place, *refs):
    splits, groups, nblk = geo["splits"], geo["groups"], geo["nblk"]
    q_h, kv, others, srow = refs[0], refs[1], refs[2 : splits + 1], refs[splits + 1]
    dcombs = refs[splits + 2 : splits + 2 + groups]
    att_h, dq_h = refs[splits + 2 + groups : splits + 4 + groups]
    dkvs_h = refs[splits + 4 + groups : 2 * splits + 4 + groups]
    k_s, v_s, g_s, dq_a, dk_t, dv_t, r_t, q_s, att, dc_s, dq, dkv = refs[
        2 * splits + 4 + groups : -4
    ]
    qm, augs, sems, out_sems = refs[-4:]
    copies = [(q_h, q_s), (att_h, att)] + [(dcombs[k], dc_s.at[k]) for k in range(groups)]
    copies = fetch(copies, sems, 2 * nblk)
    blk, lw, gw, hpg, own, pad = (geo[k] for k in ("blk", "lw", "gw", "hpg", "own", "pad"))
    copies += load_blocks(geo, deal, place, kv, others, k_s, v_s, sems)
    scale = HD**-0.5

    @pl.loop(0, geo["seq"] // KT)
    def _(i):
        cols = pl.ds(pl.multiple_of(i * KT, KT), KT)
        for ref in (dk_t, dv_t, r_t):
            ref[:, cols] = jnp.zeros((gw, KT), F32)

    for copy in copies:
        copy.wait()
    for k in range(groups):
        rows = slice(2 * k * blk, 2 * (k + 1) * blk)
        g_s[rows, :] = jnp.concatenate(
            [unpack(dc_s[k]), jnp.zeros((2 * blk, lw - gw), BF)], axis=1
        )

    @pl.loop(0, own)
    def _(n):
        p = block_at(geo, deal, place, n)
        end = (p + 1) * blk
        mine = pl.ds(pl.multiple_of(n * blk, blk), blk)
        qb = q_s[mine, :].astype(F32) * scale
        wide = g_s[mine, :].astype(F32)
        saved = att[mine, :]
        prod = wide * saved
        lane = lane_iota(blk, lw)
        low = jnp.zeros((blk, lw), F32)
        for h in range(hpg):
            recip = 1.0 / saved[:, gw + h : gw + h + 1]
            only = head_mask(blk, lw, h)
            dtot = -jnp.sum(jnp.where(only, prod, 0.0), axis=1, keepdims=True) * recip
            high = dtot.astype(BF).astype(F32)
            dnum = jnp.where(only, wide * recip, 0.0)
            low += dnum
            aug = jnp.where(lane == gw, high, dnum)
            aug = jnp.where(lane == gw + 1, dtot - high, aug)
            stack = slice(h * blk, (h + 1) * blk)
            augs[stack, :] = aug.astype(BF)
            qm[stack, :] = jnp.where(only, qb, 0.0).astype(BF)
        q_t, dn_t, g_t = qb.astype(BF).T, low.astype(BF).T, g_s[mine, :].T
        qstart = jnp.broadcast_to(starts_of(srow, p, blk), (KT, blk)).T
        qpos = p * blk + row_iota(blk, KT)
        qlim = qpos - ((qpos - qstart) & (SEGL - 1))
        dq_a[...] = jnp.zeros_like(dq_a)

        lead = starts[0, p * blk] // 128 * 128
        count = (end - lead + KT - 1) // KT
        lead = jnp.minimum(lead, geo["seq"] - count * KT)

        @pl.loop(0, count)
        def _(t):
            base = lead + t * KT
            rows = pl.ds(pl.multiple_of(pad + base, 128), KT)
            cols = pl.ds(pl.multiple_of(base, 128), KT)
            kt, vt = k_s[rows, :], v_s[rows, :]
            kpos = base + lane_iota(blk, KT)
            inside = kpos >= qstart
            visible = inside & (kpos <= qpos)
            earlier = inside & (kpos < qlim)
            scores = mm(qm[...], kt, NT)
            dprobs = mm(augs[...], vt, NT)
            dscores = []
            for h in range(hpg):
                part, stack = slice(h * HD, (h + 1) * HD), slice(h * blk, (h + 1) * blk)
                probs = jnp.where(visible, jnp.exp(scores[stack]), 0.0)
                dscores.append((probs * dprobs[stack]).astype(BF))
                dv_t[part, cols] += mm(dn_t[part, :], probs.astype(BF))
                dk_t[part, cols] += mm(q_t[part, :], dscores[h])
            dque = mm(jnp.concatenate(dscores, axis=0), kt)
            dq_a[...] += own_lanes(dque, blk, lw, hpg)
            r_t[:, cols] += mm(g_t[:gw, :], jnp.where(earlier, 1.0, 0.0).astype(BF))

        dq[mine, :] = (dq_a[...] * scale).astype(BF)

    copies = fetch([(dq, dq_h)], out_sems, nblk)
    spread = coef_spread(lw, gw, hpg)

    @pl.loop(0, geo["seq"] // KT)
    def _(t):
        rows = pl.ds(pl.multiple_of(pad + t * KT, KT), KT)
        cols = pl.ds(pl.multiple_of(t * KT, KT), KT)
        fill = jnp.zeros((KT, lw - gw), F32)
        upright = lambda ref: jnp.concatenate([ref[:, cols].T, fill], axis=1)
        reach = upright(r_t)
        lane = lane_iota(KT, lw)
        dval = upright(dv_t) + reach * mm(k_s[rows, :], spread)
        prod = reach * v_s[rows, :].astype(F32)
        for h in range(hpg):
            part = jnp.where(head_mask(KT, lw, h), prod, 0.0)
            dval = jnp.where(lane == gw + h, jnp.sum(part, axis=1, keepdims=True), dval)
        narrow = dk_t[:, cols].astype(BF).T
        dkv[cols, 0:lw] = jnp.concatenate([narrow, fill.astype(BF)], axis=1)
        dkv[cols, lw : 2 * lw] = dval.astype(BF)

    for m in reversed(range(splits)):
        for n in range(m * own, (m + 1) * own):
            at = pl.ds(pl.multiple_of(block_at(geo, deal, place, n) * blk, 64), blk)
            to = pl.ds((n % own) * blk, blk)
            copies += fetch([(dkv.at[at], dkvs_h[m].at[to])], out_sems, n)
    for copy in copies:
        copy.wait()


def assemble_kernel(geo, split, *refs):
    splits, nsh = geo["splits"], geo["nsh"]
    for m in range(splits):
        for i in range(3):
            for z in range(nsh):
                refs[splits + i][z, split[0] ^ m] = refs[m][i, z]


def proj_kernel(geo, comb, wout, x, vecs, resid, n2):
    total = x[...].astype(F32) + vecs[0:1, :]
    for g in range(geo["groups"]):
        total += mm(unpack(comb[g]), wout[g])
    resid[...] = total
    unit, _ = norm_stats(total)
    n2[...] = (unit * vecs[1:2, :] + vecs[2:3, :]).astype(BF)


def ffn_kernel(geo, n2, g, wup, wdn, bias, y, dn2, act, dhid, ysum, dsum):
    fg = geo["fg"]
    ysum[...] = jnp.zeros_like(ysum)
    dsum[...] = jnp.zeros_like(dsum)

    @pl.loop(0, fg // FB)
    def _(b):
        cols = pl.ds(pl.multiple_of(b * FB, FB), FB)
        u = mm(n2[...], wup[:, cols]) + bias[0:1, cols]
        sq = u * u
        th = jnp.tanh(0.7978845608028654 * (u + 0.044715 * sq * u))
        half = 0.5 * (1.0 + th)
        a = (u * half).astype(BF)
        slope = half + 0.5 * u * (1.0 - th * th) * (0.7978845608028654 * (1.0 + 0.134145 * sq))
        d = (slope * mm(g[...], wdn[cols, :], NT)).astype(BF)
        act[:, cols] = a
        dhid[:, cols] = d
        ysum[...] += mm(a, wdn[cols, :])
        dsum[...] += mm(d, wup[:, cols], NT)

    y[...] = ysum[...].astype(BF)
    dn2[...] = dsum[...].astype(BF)


def ffn_grad_kernel(geo, split, *refs):
    groups, splits, nsh, part, parta, tok, fg = (
        geo[k] for k in ("groups", "splits", "nsh", "part", "parta", "tok", "fg")
    )
    n2s, dhids, acts, gs = (refs[i * groups : (i + 1) * groups] for i in range(4))
    outs, dupb, acc = refs[4 * groups : 4 * groups + splits], refs[-2], refs[-1]
    total = jnp.zeros((1, fg), F32)
    for ref in dhids:
        total += jnp.sum(ref[...].astype(F32), axis=0, keepdims=True)
    dupb[...] = jnp.broadcast_to(total, dupb.shape)
    for at, left, right in ((0, n2s, dhids), (parta, acts, gs)):
        flip = jnp.concatenate([ref[...].T for ref in left], axis=1)
        for b in range(0, fg, FB):
            side = jnp.concatenate([ref[:, b : b + FB] for ref in right])
            acc[:, b : b + FB] = mm(flip, side)
        for m in range(splits):
            for z in range(nsh):
                rows = (z * splits + (split[0] ^ m)) * part
                rows = pl.ds(pl.multiple_of(rows, 8), part)
                outs[m][z, at : at + part, :] = acc[rows, :].astype(BF)


def post_kernel(geo, group, *refs):
    groups = geo["groups"]
    dn2s, (wout, resid, g, vecs) = refs[:groups], refs[groups : groups + 4]
    dresid, dproj, small = refs[groups + 4 : groups + 7]
    dcombs = refs[groups + 7 :]
    unit, recip = norm_stats(resid[...])
    dn2 = dn2s[0][...].astype(F32)
    for ref in dn2s[1:]:
        dn2 += ref[...].astype(F32)
    wide = g[...].astype(F32)
    dres = wide + norm_back(dn2, unit, recip, vecs[1:2, :])
    dresid[...] = dres
    low = dres.astype(BF)
    dproj[...] = low
    for k in range(groups):
        dcombs[k][...] = pack(mm(low, wout[group[0] ^ k], NT).astype(BF))
    small[0:1, :] = jnp.sum(low.astype(F32), axis=0, keepdims=True)
    small[1:2, :] = jnp.sum(dn2 * unit, axis=0, keepdims=True)
    small[2:3, :] = jnp.sum(dn2, axis=0, keepdims=True)
    small[3:4, :] = jnp.sum(wide, axis=0, keepdims=True)
    small[4:8, :] = jnp.zeros((4, D), F32)


def out_grad_kernel(geo, here, comb, dproj, out):
    splits, nsh, gw = geo["splits"], geo["nsh"], geo["gw"]
    rows, sub = D // nsh, D // nsh // geo["nctx"]
    for g in range(geo["groups"]):
        value = mm(unpack(comb[g]), dproj[...], TN)
        for r in range(0, gw, sub):
            z, i = (g * gw + r) // rows, (g * gw + r) % rows // sub
            piece = value[r : r + sub, :].astype(BF)
            out[(i % splits) ^ here[1], (i // splits) ^ here[0], z] = piece


def extend_kernel(geo, *refs):
    groups, splits, nsh, tok = (geo[k] for k in ("groups", "splits", "nsh", "tok"))
    ys, grads, outs = refs[: groups - 1], refs[groups - 1 : groups - 1 + splits], refs[-groups:]
    for k in range(groups):
        total = grads[0][0, k].astype(F32)
        for ref in grads[1:]:
            total += ref[k].astype(F32)
        total = total.reshape(nsh * total.shape[1], D).astype(BF)
        if k == 0:
            outs[0][...] = total
        else:
            outs[k][0:tok, :] = ys[k - 1][...]
            outs[k][tok:, :] = total


def sum_kernel(geo, *refs):
    total = refs[0][...].astype(F32)
    for ref in refs[1:-1]:
        total += ref[...].astype(F32)
    refs[-1][...] = total.astype(BF)


def stack_kernel(geo, *refs):
    for k, ref in enumerate(refs[:-1]):
        refs[-1][k] = ref[...]


def late_kernel(geo, here, *refs):
    splits, groups, nsh, fg = (geo[k] for k in ("splits", "groups", "nsh", "fg"))
    sub = D // nsh // geo["nctx"]
    wgs, exts = refs[:splits], refs[splits : splits + groups]
    vec1, small2, dupb = refs[splits + groups : splits + groups + 3]
    outs, (dwout, vec) = refs[splits + groups + 3 : -2], refs[-2:]
    total = exts[0][...].astype(F32)
    for ref in exts[1:]:
        total += ref[geo["tok"] :, :].astype(F32)
    for z in range(nsh):
        dwout[z] = total[z * sub : (z + 1) * sub, :]
    vec[0:6, :] = vec1[0:6, :]
    vec[6:10, :] = small2[0:4, :]
    each, spans = fg // nsh, []
    for z in range(nsh):
        for g in range(groups):
            value = dupb[0:1, z * each : (z + 1) * each]
            spans.append(jnp.where(here[0] == g, value, 0.0))
    per = D // each
    for i in range(len(spans) // per):
        vec[10 + i : 11 + i, :] = jnp.concatenate(spans[i * per : (i + 1) * per], axis=1)
    vec[14:16, :] = jnp.zeros((2, D), F32)
    for k in range(nsh):
        z = here[2] ^ k
        total = wgs[0][z].astype(F32)
        for ref in wgs[1:]:
            total += ref[z].astype(F32)
        outs[k][...] = jnp.concatenate([vec[...], total, dwout[z]], axis=0).astype(BF)


def result_kernel(geo, *refs):
    groups = geo["groups"]
    ys, (resid, vecs, out) = refs[:groups], refs[groups:]
    total = resid[...] + vecs[3:4, :]
    for ref in ys:
        total += ref[0 : geo["tok"], :].astype(F32)
    out[...] = total


def dn1_kernel(geo, dq, *refs):
    splits, groups, tok, lw = (geo[k] for k in ("splits", "groups", "tok", "lw"))
    dkvs, (w, dqkv), parts = refs[:splits], refs[splits : splits + 2], refs[splits + 2 :]
    for k in range(groups):
        rows = slice(k * tok, (k + 1) * tok)
        both = dkvs[0][rows, :].astype(F32)
        for ref in dkvs[1:]:
            both += ref[rows, :].astype(F32)
        dqkv[rows, 0:lw] = dq[rows, :]
        dqkv[rows, lw : 3 * lw] = both.astype(BF)
        parts[k][...] = mm(dqkv[rows, :], w[...], NT).astype(BF)


def wgrad_kernel(geo, group, split, *refs):
    groups, splits, nsh, part, tok, lw, gw, hpg = (
        geo[k] for k in ("groups", "splits", "nsh", "part", "tok", "lw", "gw", "hpg")
    )
    pieces, parts, dqkv = refs[:groups], refs[groups : 2 * groups], refs[2 * groups]
    outs, (vec, acc) = refs[2 * groups + 1 : -2], refs[-2:]
    flip = jnp.concatenate([ref[0:tok, :].T for ref in pieces], axis=1)
    for b in range(0, 3 * lw, lw):
        acc[:, b : b + lw] = mm(flip, dqkv[:, b : b + lw])
    for m in range(splits):
        for z in range(nsh):
            rows = pl.ds(pl.multiple_of((z * splits + (split[0] ^ m)) * part, 8), part)
            for t in range(3):
                value = pack(acc[rows, t * lw : t * lw + gw])
                outs[m][z, :, t * lw : (t + 1) * lw] = value.astype(BF)
    plain = jnp.zeros((1, D), F32)
    cross = jnp.zeros((1, D), F32)
    means = jnp.zeros((HP, 128), F32)
    spreads = jnp.zeros((HP, 128), F32)
    for k in range(groups):
        dn1 = parts[k][...].astype(F32)
        plain += jnp.sum(dn1, axis=0, keepdims=True)
        cross += jnp.sum(dn1 * pieces[k][0:tok, :].astype(F32), axis=0, keepdims=True)
        dcoef = dqkv[k * tok : (k + 1) * tok, 3 * lw - 128 :]
        means += mm(pieces[k][tok : tok + HP, tok : 2 * tok], dcoef)
        spreads += mm(pieces[k][tok + HP : tok + 2 * HP, 0:tok], dcoef)
    total = jnp.sum(dqkv[...].astype(F32), axis=0, keepdims=True)
    vec[0:1, :] = cross
    vec[1:2, :] = plain
    head = row_iota(HP, 128) - group[0] * hpg
    hit = (head >= 0) & (head < hpg) & (lane_iota(HP, 128) == 128 - (lw - gw) + head)
    across = row_iota(HP, D) == lane_iota(HP, D)
    for i, value in enumerate((means, spreads)):
        value = jnp.sum(jnp.where(hit, value, 0.0), axis=1, keepdims=True)
        value = jnp.sum(jnp.where(across, value, 0.0), axis=0, keepdims=True)
        vec[4 + i : 5 + i, :] = value
    for i, t in enumerate((0, 2)):
        mine = total[:, t * lw : t * lw + gw]
        for g in range(groups):
            vec[2 + i : 3 + i, g * gw : (g + 1) * gw] = jnp.where(group[0] == g, mine, 0.0)
    vec[6:8, :] = jnp.zeros((2, D), F32)


def tail_kernel(geo, *refs):
    groups = geo["groups"]
    parts = refs[:groups]
    x, dresid, vecs, grad = refs[groups:]
    dn1 = parts[0][...].astype(F32)
    for ref in parts[1:]:
        dn1 += ref[...].astype(F32)
    unit, recip = norm_stats(x[...].astype(F32))
    grad[...] = dresid[...] + norm_back(dn1, unit, recip, vecs[4:5, :])


def finish_kernel(geo, ups, downs, up_g, down_g):
    groups, splits, nsh, part, fg, rows = (
        geo[k] for k in ("groups", "splits", "nsh", "part", "fg", "rows")
    )
    each = fg // nsh
    for i in range(groups * splits):
        g, c = i // splits, i % splits
        value = ups[i, 0:part, :].astype(F32)
        for z in range(nsh):
            at = z * groups * each + g * each
            up_g[c * part : (c + 1) * part, at : at + each] = value[:, z * each : (z + 1) * each]
        at = g * each + c * part
        down_g[at : at + part, :] = downs[i, 0:part, :].astype(F32)


def finish_in_kernel(geo, place, *refs):
    groups, splits, part, gw, lw = (geo[k] for k in ("groups", "splits", "part", "gw", "lw"))
    near, far, vecs = refs[:groups], refs[groups : groups + splits - 1], refs[-14]
    outs = refs[-13:]
    in_g, out_g = outs[:2]
    group, split = place[0] // splits, place[0] % splits
    prow = part * 3 // 4
    total = jnp.zeros((HP, D), F32)
    for k in range(groups):
        for m in range(splits):
            value = (near[k][...] if m == 0 else far[m - 1][k]).astype(F32)
            total += value[0:HP, :]
            out_g[place[0] ^ (k * splits + m)] = value[HP + prow :, :]
            rows = pl.ds(pl.multiple_of((split ^ m) * part, 8), part)
            wide = [unpack(value[HP : HP + prow, t * lw : (t + 1) * lw]) for t in range(3)]
            for g in range(groups):

                @pl.when((group ^ k) == g)
                def _():
                    for t in range(3):
                        in_g[rows, t * D + g * gw : t * D + (g + 1) * gw] = wide[t]

    flat = lambda i, n=D: total[i : i + 1, 0:n].reshape(n)
    outs[2][...] = ((total[0:1, :] - vecs[5:6, :] * total[1:2, :]) / vecs[4:5, :]).reshape(D)
    for ref, i in zip(outs[3:10], (1, 2, 3, 6, 7, 8, 9)):
        ref[...] = flat(i)
    outs[10][...] = flat(4, H)
    outs[11][...] = flat(5, H)
    for i in range(4):
        outs[12][i * D : (i + 1) * D] = flat(10 + i)


def full(shape):
    return pl.BlockSpec(shape, lambda *_: (0,) * len(shape))


ANY = pl.BlockSpec(memory_space=pl.ANY)
DMA = pltpu.SemaphoreType.DMA


def call(kernel, geo, scalars, grid, ins, in_specs, outs, out_specs, scratch, flops, moved, exps=0, limit=12):
    return pl.pallas_call(
        functools.partial(kernel, geo),
        grid_spec=pltpu.PrefetchScalarGridSpec(
            num_scalar_prefetch=len(scalars),
            grid=grid,
            in_specs=in_specs,
            out_specs=out_specs,
            scratch_shapes=scratch,
        ),
        out_shape=[jax.ShapeDtypeStruct(s, t) for s, t in outs],
        compiler_params=pltpu.CompilerParams(vmem_limit_bytes=limit << 20),
        cost_estimate=pl.CostEstimate(flops=1000, bytes_accessed=1000, transcendentals=0),
    )(*scalars, *ins)


def per_device(
    inputs,
    out_grad,
    segment_ids,
    doc_starts,
    deal_table,
    ridge_matrix,
    first_gain,
    first_shift,
    mixer_in,
    query_bias,
    value_bias,
    mixer_out,
    out_bias,
    second_gain,
    second_shift,
    up_weight,
    up_bias,
    down_weight,
    down_bias,
    memory_mean,
    memory_spread,
):
    tok = inputs.shape[1]
    blk = tok // 2
    nctx, nsh = lax.axis_size("ctx"), lax.axis_size("shard")
    place = lax.axis_index("ctx").astype(jnp.int32)
    seq, nblk = tok * nctx, 2 * nctx
    groups = math.gcd(H, nctx)
    splits = nctx // groups
    hpg = H // groups
    gw = hpg * HD
    lw = -(-(gw + hpg) // 128) * 128
    own = 2 * groups
    group, split = place // splits, place % splits
    ff = up_weight.shape[1]
    fg = ff // groups
    each = fg // nsh
    rows = D // nsh
    part = rows // splits
    parta = -(-part // 16) * 16
    sub = rows // nctx
    qrows = groups * tok
    geo = dict(
        tok=tok, blk=blk, seq=seq, nblk=nblk, groups=groups, splits=splits, hpg=hpg, gw=gw, lw=lw,
        own=own, pad=KT, nctx=nctx, nsh=nsh, fg=fg, rows=rows, part=part, parta=parta,
    )
    x = inputs[0]
    upstream = out_grad[0]
    peers = range(groups)
    across = lambda v, k: v if k == 0 else swap(v, "ctx", nctx, k * splits)
    inside = lambda v, m: swap(v, "ctx", nctx, m)
    gidx, sidx = group.reshape(1), split.reshape(1)
    vm = pltpu.VMEM
    zero = lambda n: jnp.zeros((n, D), F32)
    vrow = full((D,))
    tokd, square = full((tok, D)), full((D, D))

    prow = tok + 2 * HP
    (payload,) = call(
        prep_kernel, geo, (), (1,),
        (x, first_gain, first_shift, ridge_matrix, memory_mean, memory_spread),
        [tokd, vrow, vrow, full((tok, NB)), full((H,)), full((H,))],
        [((prow, D), BF)], [full((prow, D))], [], tok * D * 10, tok * D * 6,
    )
    pieces = [across(payload, k) for k in peers]

    w_mine = jnp.concatenate(
        [
            jnp.pad(
                lax.dynamic_slice_in_dim(mixer_in, t * D + group * gw, gw, 1),
                ((0, 0), (0, lw - gw)),
            )
            for t in range(3)
        ],
        axis=1,
    )
    w_mine, _ = lax.optimization_barrier((w_mine, payload))
    w_parts = swap_pieces(w_mine, "shard", nsh)

    up_rows = lax.dynamic_slice_in_dim(up_weight, split * part, part)
    up_mine = jnp.concatenate(
        [
            lax.dynamic_slice_in_dim(up_rows, z * (ff // nsh) + group * each, each, 1)
            for z in range(nsh)
        ],
        axis=1,
    )
    down_mine = lax.dynamic_slice_in_dim(down_weight, group * each + split * part, part)
    out_mine = lax.dynamic_slice_in_dim(mixer_out, split * part, part)
    trio = jnp.stack([up_mine, down_mine, out_mine])
    trio, _ = lax.optimization_barrier((trio, (w_parts, pieces)))
    trio = lax.all_gather(trio, "shard", axis=1)

    pidx = place.reshape(1)
    tables = (deal_table, doc_starts, pidx)

    vectors = (out_bias, second_gain, second_shift, down_bias, first_gain, first_shift)
    here = jnp.stack([group, split, lax.axis_index("shard").astype(jnp.int32)])
    vrows = full((8, D))
    q, kv, w_group, vecs, up_b = call(
        qkv_kernel, geo, (here,), (1,),
        (*pieces, *w_parts, query_bias, value_bias, up_bias, *vectors),
        [full((prow, D))] * groups + [full((rows, 3 * lw))] * nsh + [vrow] * 2 + [full((ff,))]
        + [vrow] * len(vectors),
        [((qrows, lw), BF), ((qrows, 2 * lw), BF), ((D, 3 * lw), BF), ((8, D), F32),
         ((8, fg), F32)],
        [full((qrows, lw)), full((qrows, 2 * lw)), full((D, 3 * lw)), vrows, full((8, fg))],
        [], qrows * D * 6 * lw, qrows * D * 4, 0, 16,
    )
    others = [inside(kv, m) for m in range(1, splits)]
    upstream_later, _ = lax.optimization_barrier((upstream, q))
    planes = [[g * splits + c for g in peers] for c in range(splits)]
    gs = [upstream if k == 0 else across(upstream_later, k) for k in peers]

    wide = (seq + KT, lw)
    sems = pltpu.SemaphoreType.DMA((2 * nblk,))
    tiles = qrows * seq // 2
    moved = (3 * qrows + 3 * seq) * lw * 2
    comb, att = call(
        attn_fwd_kernel, geo, tables, (1,),
        (q, kv, *others, doc_starts),
        [full((qrows, lw))] + [ANY] * splits + [full((1, seq))],
        [((groups, tok * 3 // 4, 256), BF), ((qrows, lw), F32)],
        [full((groups, tok * 3 // 4, 256)), full((qrows, lw))],
        [vm(wide, BF)] * 3
        + [vm((qrows, lw), BF), vm((blk, lw), F32), vm((blk, lw), F32), sems],
        tiles * lw * 2 * (2 * hpg + 1), moved, tiles * hpg, 6 + seq // 512,
    )
    comb, gs, trio = lax.optimization_barrier((comb, gs, trio))
    trios = [trio if m == 0 else inside(trio, m) for m in range(splits)]
    w_up, w_down, w_out = call(
        assemble_kernel, geo, (sidx,), (1,), trios, [full((3, nsh, part, D))] * splits,
        [((nsh, splits, part, D), BF)] * 3, [full((nsh, splits, part, D))] * 3,
        [], 1000, 1000, 0, 16,
    )
    w_up, w_down, w_out = (w.reshape(D, D) for w in (w_up, w_down, w_out))
    w_out = w_out.reshape(groups, gw, D)
    trade = lambda v: lax.all_to_all(v, "ctx", 0, 0, axis_index_groups=planes, tiled=True)
    comb = trade(comb)

    resid, n2 = call(
        proj_kernel, geo, (), (1,), (comb, w_out, x, vecs),
        [full((groups, tok * 3 // 4, 256)), full((groups, gw, D)), tokd, vrows],
        [((tok, D), F32), ((tok, D), BF)], [tokd, tokd],
        [], tok * D * D * 2, tok * D * 12,
    )
    ys, dn2s, acts, dhids = [], [], [], []
    n2s = [n2]
    for k in peers:
        if k == 1:
            n2s += [across(n2, m) for m in range(1, groups - 1)]
            n2_last, *n2s = lax.optimization_barrier((n2, *n2s, ys[0]))[:-1]
            n2s.append(across(n2_last, groups - 1))
        outs = call(
            ffn_kernel, geo, (), (1,), (n2s[k], gs[k], w_up, w_down, up_b),
            [tokd, tokd, square, square, full((8, fg))],
            [((tok, D), BF)] * 4, [tokd] * 4,
            [vm((tok, D), F32), vm((tok, D), F32)], tok * D * fg * 8, tok * D * 12 + D * fg * 4, tok * fg,
        )
        ys.append(outs[0])
        dn2s.append(across(outs[1], k))
        acts.append(outs[2])
        dhids.append(outs[3])
    dresid, dproj, small2, *dcombs = call(
        post_kernel, geo, (gidx,), (1,), (*dn2s, w_out, resid, upstream, vecs),
        [tokd] * groups + [full((groups, gw, D)), tokd, tokd, vrows],
        [((tok, D), F32), ((tok, D), BF), ((8, D), F32)]
        + [((tok * 3 // 4, 256), BF)] * groups,
        [tokd, tokd, full((8, D))] + [full((tok * 3 // 4, 256))] * groups,
        [], tok * D * D * 2, tok * D * 20,
    )
    dcombs = [across(dcombs[k], k) for k in peers]
    *dms, dupb = call(
        ffn_grad_kernel, geo, (sidx,), (1,), (*n2s, *dhids, *acts, *gs),
        [tokd] * (4 * groups),
        [((nsh, 2 * parta, D), BF)] * splits + [((8, fg), F32)],
        [full((nsh, 2 * parta, D))] * splits + [full((8, fg))],
        [vm((D, D), F32)], qrows * D * fg * 4, qrows * D * 8,
    )
    (dwout,) = call(
        out_grad_kernel, geo, (here,), (1,), (comb, dproj),
        [full((groups, tok * 3 // 4, 256)), tokd],
        [((splits, groups, nsh, sub, D), BF)], [full((splits, groups, nsh, sub, D))],
        [], tok * D * D * 2, tok * D * 6,
    )
    dwouts = [dwout] + [inside(dwout[m], m) for m in range(1, splits)]
    dms = [dms[0]] + [inside(dms[m], m) for m in range(1, splits)]
    (dm,) = call(
        sum_kernel, geo, (), (1,), dms, [full((nsh, 2 * parta, D))] * splits,
        [((nsh, 2 * parta, D), BF)], [full((nsh, 2 * parta, D))], [], 1000, 1000,
    )
    dm, dwouts, dcombs = lax.optimization_barrier((dm, dwouts, dcombs))
    erow = tok + nsh * sub
    exts = call(
        extend_kernel, geo, (), (1,), (*ys[1:], *dwouts),
        [tokd] * (groups - 1)
        + [pl.BlockSpec((1, groups, nsh, sub, D), lambda *_: (0, 0, 0, 0, 0))]
        + [full((groups, nsh, sub, D))] * (splits - 1),
        [((nsh * sub, D), BF)] + [((erow, D), BF)] * (groups - 1),
        [full((nsh * sub, D))] + [full((erow, D))] * (groups - 1),
        [], 1000, 1000,
    )
    dms, _ = lax.optimization_barrier((dms, dproj))
    dm = lax.psum_scatter(dm, "shard", scatter_dimension=0, tiled=False)

    dq, *dkvs = call(
        attn_bwd_kernel, geo, tables, (1,),
        (q, kv, *others, doc_starts, *dcombs, att),
        [ANY] * (splits + 1) + [full((1, seq))] + [ANY] * (groups + 1),
        [((qrows, lw), BF)] + [((qrows, 2 * lw), BF)] * splits,
        [ANY] * (splits + 1),
        [vm(wide, BF)] * 2
        + [vm((qrows, lw), BF), vm((blk, lw), F32)] + [vm((gw, seq), F32)] * 3
        + [vm((qrows, lw), BF), vm((qrows, lw), F32), vm((groups, tok * 3 // 4, 256), BF),
           vm((qrows, lw), BF), vm((seq, 2 * lw), BF), vm((hpg * blk, lw), BF),
           vm((hpg * blk, lw), BF), DMA((2 * nblk + 2 + groups,)),
           DMA((nblk + 1,))],
        tiles * lw * 2 * (5 * hpg + 1), moved, tiles * hpg, 60,
    )
    later, _ = lax.optimization_barrier((exts, dcombs))
    exts = [across(later[k], k) for k in peers]
    dkvs, exts, dm = lax.optimization_barrier((dkvs, exts, dm))
    dkvs = [dkvs[0]] + [inside(dkvs[m], m) for m in range(1, splits)]
    m_g = lax.all_gather(dm, "ctx", axis=0)
    (result,) = call(
        result_kernel, geo, (), (1,), (ys[0], *exts[1:], resid, vecs),
        [tokd] + [full((erow, D))] * (groups - 1) + [tokd, vrows], [((tok, D), F32)], [tokd],
        [], tok * D * 8, tok * D * 16,
    )
    dqkv, *parts = call(
        dn1_kernel, geo, (), (1,), (dq, *dkvs, w_group),
        [full((qrows, lw))] + [full((qrows, 2 * lw))] * splits + [full((D, 3 * lw))],
        [((qrows, 3 * lw), BF)] + [((tok, D), BF)] * groups,
        [full((qrows, 3 * lw))] + [tokd] * groups,
        [], qrows * D * 6 * lw, qrows * D * 8, 0, 60,
    )
    mine = parts
    parts = [across(parts[k], k) for k in peers]

    prow = part * 3 // 4
    *wgs, vec1 = call(
        wgrad_kernel, geo, (gidx, sidx), (1,), (*pieces, *mine, dqkv),
        [full((tok + 2 * HP, D))] * groups + [tokd] * groups + [full((qrows, 3 * lw))],
        [((nsh, prow, 3 * lw), BF)] * splits + [((8, D), F32)],
        [full((nsh, prow, 3 * lw))] * splits + [full((8, D))],
        [vm((D, 3 * lw), F32)], qrows * D * 6 * lw, qrows * D * 4, 0, 60,
    )
    wgs = [wgs[0]] + [inside(wgs[m], m) for m in range(1, splits)]
    lrow = HP + prow + sub
    lates = call(
        late_kernel, geo, (here,), (1,), (*wgs, *exts, vec1, small2, dupb),
        [full((nsh, prow, 3 * lw))] * splits + [full((nsh * sub, D))]
        + [full((erow, D))] * (groups - 1) + [full((8, D)), full((8, D)), full((8, fg))],
        [((lrow, D), BF)] * nsh, [full((lrow, D))] * nsh,
        [vm((nsh, sub, D), F32), vm((HP, D), F32)], 1000, 1000,
    )
    zs = [lates[k] if k == 0 else swap(lates[k], "shard", nsh, k) for k in range(nsh)]
    (zsum,) = call(
        sum_kernel, geo, (), (1,), zs, [full((lrow, D))] * nsh,
        [((lrow, D), BF)], [full((lrow, D))], [], 1000, 1000,
    )
    zsum, parts, result = lax.optimization_barrier((zsum, parts, result))
    near = [across(zsum, k) for k in peers]
    (input_grad,) = call(
        tail_kernel, geo, (), (1,), (*parts, x, dresid, vecs),
        [tokd] * (groups + 2) + [vrows], [((tok, D), F32)], [tokd],
        [], tok * D * 20, tok * D * 20,
    )
    gblock = lambda r: pl.BlockSpec((nctx, parta, D), lambda j, *_: (0, r, 0))
    up_g, down_g = call(
        finish_kernel, geo, (), (1,), (m_g, m_g), [gblock(0), gblock(1)],
        [((rows, ff), F32), ((ff // nsh, D), F32)],
        [full((rows, ff)), full((ff // nsh, D))],
        [], 1000, rows * ff * 12,
    )
    near, input_grad, up_g = lax.optimization_barrier((near, input_grad, up_g))
    (stacked,) = call(
        stack_kernel, geo, (), (1,), near, [full((lrow, D))] * groups,
        [((groups, lrow, D), BF)], [full((groups, lrow, D))], [], 1000, 1000,
    )
    far = [inside(stacked, m) for m in range(1, splits)]
    in_g, out_g, gain_g, shift_g, qb_g, vb_g, ob_g, gain2_g, shift2_g, db_g, mean_g, spread_g, ub_g = call(
        finish_in_kernel, geo, (pidx,), (1,),
        (*near, *far, vecs),
        [full((lrow, D))] * groups + [full((groups, lrow, D))] * (splits - 1) + [vrows],
        [((rows, 3 * D), F32), ((nctx, sub, D), F32)] + [((D,), F32)] * 8
        + [((H,), F32)] * 2 + [((ff,), F32)],
        [full((rows, 3 * D)), full((nctx, sub, D))] + [vrow] * 8 + [full((H,))] * 2
        + [full((ff,))],
        [], 1000, rows * D * 20,
    )
    out_g = out_g.reshape(rows, D)
    small = (
        gain_g, shift_g, qb_g, vb_g, ob_g, gain2_g, shift2_g, ub_g, db_g, mean_g, spread_g
    )
    return (result[None], input_grad[None], in_g, out_g, up_g, down_g) + small


def solution(mesh):
    rows, split = P("shard", None), P("shard", "ctx", None)
    none = P()
    return jax.shard_map(
        per_device,
        mesh=mesh,
        in_specs=(
            split, split, rows, rows, none, P("ctx", None), none, none, rows, none, none, rows,
            none, none, none, rows, none, rows, none, none, none,
        ),
        out_specs=(split, split, rows, rows, rows, rows) + (none,) * 11,
        check_vma=False,
    )
```

```python
import functools
import math

import jax
import jax.numpy as jnp
from jax import lax
from jax.experimental import pallas as pl
from jax.experimental.pallas import tpu as pltpu
from jax.sharding import PartitionSpec as P

D = 768
H = 12
HD = 64
NB = 256
SEGL = 16

HIGH = lax.Precision.HIGHEST
EPS = 1e-05
BF = jnp.bfloat16
F32 = jnp.float32
KT = 256
FB = 256
UB = 768
NN = (((1,), (0,)), ((), ()))
NT = (((1,), (1,)), ((), ()))
TN = (((0,), (0,)), ((), ()))


def mm(a, b, dims=NN):
    return lax.dot_general(a, b, dims, preferred_element_type=F32)


def norm_stats(values):
    center = values - jnp.mean(values, axis=-1, keepdims=True)
    spread = jnp.mean(center * center, axis=-1, keepdims=True)
    recip = lax.rsqrt(spread + EPS)
    return center * recip, recip


def norm_back(upstream, unit, recip, gain):
    scaled = upstream * gain
    return recip * (
        scaled
        - jnp.mean(scaled, axis=-1, keepdims=True)
        - unit * jnp.mean(scaled * unit, axis=-1, keepdims=True)
    )


def swap(x, axis, count, k):
    return lax.ppermute(x, axis, [(i, i ^ k) for i in range(count)])


def swap_pieces(x, axis, count):
    out = [x]
    for k in range(1, count):
        if k > 2:
            x, _ = lax.optimization_barrier((x, out[-1]))
        out.append(swap(x, axis, count, k))
    return out


def lane_iota(rows, cols):
    return lax.broadcasted_iota(jnp.int32, (rows, cols), 1)


def row_iota(rows, cols):
    return lax.broadcasted_iota(jnp.int32, (rows, cols), 0)


def head_mask(rows, cols, head):
    lane = lane_iota(rows, cols)
    return (lane >= head * HD) & (lane < (head + 1) * HD)


HP = 16
VR = 32


def pack(value):
    cut = value.shape[0] * 3 // 4
    last = [value[cut:, h * HD : (h + 1) * HD] for h in range(3)]
    return jnp.concatenate([value[:cut, :], jnp.concatenate(last, axis=0)], axis=1)


def unpack(value):
    each, gw = value.shape[0] // 3, 3 * HD
    last = [value[h * each : (h + 1) * each, gw:] for h in range(3)]
    return jnp.concatenate([value[:, :gw], jnp.concatenate(last, axis=1)], axis=0)


def coef_spread(lw, gw, hpg):
    row, lane = row_iota(lw, lw), lane_iota(lw, lw)
    hit = (row >= gw) & (row < gw + hpg) & (lane < gw)
    hit = hit & (lane >= (row - gw) * HD) & (lane < (row - gw + 1) * HD)
    return jnp.where(hit, 1.0, 0.0).astype(BF)


def block_at(geo, deal, place, n):
    own, splits = geo["own"], geo["splits"]
    device = place[0] ^ (((n % own) // 2) * splits + n // own)
    return deal[2 * device + n % 2]


def starts_of(ref, p, blk):
    at = pl.multiple_of((p * blk) // 128 * 128, 128)
    window = ref[:, pl.ds(at, blk + 64)]
    return jnp.where((p * blk) % 128 == 0, window[:, :blk], window[:, 64:])


def own_lanes(stacked, blk, lw, hpg):
    out = jnp.zeros((blk, lw), F32)
    for h in range(hpg):
        out = jnp.where(head_mask(blk, lw, h), stacked[h * blk : (h + 1) * blk], out)
    return out


def fetch(pairs, sems, first=0):
    copies = [pltpu.make_async_copy(a, b, sems.at[first + i]) for i, (a, b) in enumerate(pairs)]
    for copy in copies:
        copy.start()
    return copies


def load_blocks(geo, deal, place, kv, others, k_s, v_s, sems):
    blk, lw, own, pad = geo["blk"], geo["lw"], geo["own"], KT
    for ref in (k_s, v_s):
        ref[0:pad, :] = jnp.zeros((pad, lw), BF)
    copies = []
    for n in range(geo["nblk"]):
        source = kv if n < own else others[n // own - 1]
        rows = pl.ds((n % own) * blk, blk)
        to = pl.ds(pl.multiple_of(pad + block_at(geo, deal, place, n) * blk, 64), blk)
        for j, ref in enumerate((k_s, v_s)):
            copies.append(
                pltpu.make_async_copy(
                    source.at[rows, pl.ds(j * lw, lw)], ref.at[to], sems.at[2 * n + j]
                )
            )
    for copy in copies:
        copy.start()
    return copies


def row(ref):
    return ref[...].reshape(1, ref.shape[0])


def column(values):
    at = row_iota(HP, H) == lane_iota(HP, H)
    return jnp.sum(jnp.where(at, values, 0.0), axis=1, keepdims=True)


def basis_rows(mean, spread):
    centers = (lane_iota(HP, NB).astype(F32) + 0.5) / NB
    widths = spread + 1.0 / (NB * NB)
    offset = mean - centers
    weights = jnp.exp(-0.5 * offset * offset / widths) * lax.rsqrt(2.0 * math.pi * widths) / NB
    ratio = offset / widths
    return weights, -weights * ratio, 0.5 * weights * (ratio * ratio - 1.0 / widths)


def prep_kernel(geo, x, gain, shift, ridge, mean, spread, out):
    tok = geo["tok"]
    unit, _ = norm_stats(x[...].astype(F32))
    out[0:tok, :] = (unit * row(gain) + row(shift)).astype(BF)
    out[tok : tok + 2 * HP, :] = jnp.zeros((2 * HP, D), BF)
    used = row_iota(HP, 1) < H
    spreads = jnp.where(used, column(row(spread)), 0.01)
    for i, basis in enumerate(basis_rows(column(row(mean)), spreads)):
        rows = lax.dot_general(basis, ridge[...], NT, precision=HIGH, preferred_element_type=F32)
        at, lanes = tok + HP * (i // 2), tok * (i % 2)
        out[at : at + HP, lanes : lanes + tok] = rows.astype(BF)


def qkv_kernel(geo, here, *refs):
    groups, nsh, rows, tok, lw, gw, hpg, fg = (
        geo[k] for k in ("groups", "nsh", "rows", "tok", "lw", "gw", "hpg", "fg")
    )
    pieces, parts = refs[:groups], refs[groups : groups + nsh]
    qbias, vbias, upb = refs[groups + nsh : groups + nsh + 3]
    vectors = refs[groups + nsh + 3 : -5]
    q, kv, w, vecs, ups = refs[-5:]
    group = here[0]
    for k in range(nsh):
        w[pl.ds(pl.multiple_of((here[2] ^ k) * rows, 16), rows), :] = parts[k][...]
    for i, ref in enumerate(vectors):
        vecs[i : i + 1, :] = row(ref)
    wide, each, mine = row(upb), fg // nsh, []
    for z in range(nsh):
        value = jnp.zeros((1, each), F32)
        for k in range(groups):
            at = (z * groups + k) * each
            value = jnp.where(group == k, wide[:, at : at + each], value)
        mine.append(value)
    ups[...] = jnp.broadcast_to(jnp.concatenate(mine, axis=1), ups.shape)
    head = row_iota(HP, lw) - group * hpg
    place = jnp.where((head >= 0) & (head < hpg) & (lane_iota(HP, lw) == gw + head), 1.0, 0.0)
    place = place.astype(BF)
    lane = lane_iota(1, lw)
    ones = jnp.where((lane >= gw) & (lane < gw + hpg), 1.0, 0.0)
    biases = []
    for ref in (qbias, vbias):
        wide = row(ref)
        mine = jnp.zeros((1, gw), F32)
        for g in range(groups):
            mine = jnp.where(group == g, wide[:, g * gw : (g + 1) * gw], mine)
        biases.append(jnp.concatenate([mine, jnp.zeros((1, lw - gw), F32)], axis=1))
    bias = jnp.concatenate([biases[0], jnp.zeros((1, lw), F32), biases[1] + ones], axis=1)
    for k in range(groups):
        rows = slice(k * tok, (k + 1) * tok)
        out = mm(pieces[k][0:tok, :], w[...]) + bias
        q[rows, :] = out[:, :lw].astype(BF)
        coef = mm(pieces[k][tok : tok + HP, 0:tok], place, TN)
        kv[rows, 0:lw] = (out[:, lw : 2 * lw] + coef).astype(BF)
        kv[rows, lw : 2 * lw] = out[:, 2 * lw :].astype(BF)


def attn_fwd_kernel(geo, deal, starts, place, *refs):
    splits, groups = geo["splits"], geo["groups"]
    q_s, kv, others, srow = refs[0], refs[1], refs[2 : splits + 1], refs[splits + 1]
    comb, att = refs[splits + 2 : splits + 4]
    k_s, v_s, c_s, comb_s, acc, mac, sems = refs[splits + 4 :]
    blk, lw, gw, hpg, own, pad = (geo[k] for k in ("blk", "lw", "gw", "hpg", "own", "pad"))
    for copy in load_blocks(geo, deal, place, kv, others, k_s, v_s, sems):
        copy.wait()
    group = place[0] // splits
    spread = coef_spread(lw, gw, hpg)
    zero = jnp.zeros((), BF)

    @pl.loop(0, (geo["seq"] + pad) // KT)
    def _(i):
        rows = pl.ds(pl.multiple_of(i * KT, KT), KT)
        c_s[rows, :] = (mm(k_s[rows, :], spread) * v_s[rows, :].astype(F32)).astype(BF)

    @pl.loop(0, own)
    def _(n):
        p = block_at(geo, deal, place, n)
        end = (p + 1) * blk
        mine = pl.ds(pl.multiple_of(n * blk, blk), blk)
        qb = q_s[mine, :].astype(F32) * (HD**-0.5)
        qm = [jnp.where(head_mask(blk, lw, h), qb, 0.0).astype(BF) for h in range(hpg)]
        qstart = jnp.broadcast_to(starts_of(srow, p, blk), (KT, blk)).T
        qpos = p * blk + row_iota(blk, KT)
        qlim = qpos - ((qpos - qstart) & (SEGL - 1))
        acc[...] = jnp.zeros_like(acc)
        mac[...] = jnp.zeros_like(mac)

        @pl.loop(0, (end - starts[0, p * blk] + KT - 1) // KT)
        def _(t):
            base = end - (t + 1) * KT
            rows = pl.ds(pl.multiple_of(pad + base, 64), KT)
            kt, vt, ct = k_s[rows, :], v_s[rows, :], c_s[rows, :]
            kpos = base + lane_iota(blk, KT)
            inside = kpos >= qstart
            visible = inside & (kpos <= qpos)
            earlier = inside & (kpos < qlim)
            numer = jnp.zeros((blk, lw), F32)
            for h in range(hpg):
                scores = mm(qm[h], kt, NT)
                probs = jnp.where(visible, jnp.exp(scores), 0.0).astype(BF)
                mine = head_mask(KT, lw, h) | (lane_iota(KT, lw) == gw + h)
                numer += mm(probs, jnp.where(mine, vt, zero))
            acc[...] += numer
            mac[...] += mm(jnp.where(earlier, 1.0, 0.0).astype(BF), ct)

        attended = acc[...]
        scale = jnp.ones((blk, lw), F32)
        for h in range(hpg):
            recip = 1.0 / acc[:, gw + h : gw + h + 1]
            scale = jnp.where(head_mask(blk, lw, h), recip, scale)
        attended = attended * scale
        att[mine, :] = attended
        comb_s[mine, :] = (attended + mac[...]).astype(BF)

    for k in range(groups):
        comb[group ^ k] = pack(comb_s[2 * k * blk : 2 * (k + 1) * blk, :gw])


def attn_bwd_kernel(geo, deal, starts, place, *refs):
    splits, groups, nblk = geo["splits"], geo["groups"], geo["nblk"]
    q_h, kv, others, srow = refs[0], refs[1], refs[2 : splits + 1], refs[splits + 1]
    dcombs = refs[splits + 2 : splits + 2 + groups]
    att_h, dq_h = refs[splits + 2 + groups : splits + 4 + groups]
    dkvs_h = refs[splits + 4 + groups : 2 * splits + 4 + groups]
    k_s, v_s, g_s, dq_a, dk_t, dv_t, r_t, q_s, att, dc_s, dq, dkv = refs[
        2 * splits + 4 + groups : -4
    ]
    qm, augs, sems, out_sems = refs[-4:]
    copies = [(q_h, q_s), (att_h, att)] + [(dcombs[k], dc_s.at[k]) for k in range(groups)]
    copies = fetch(copies, sems, 2 * nblk)
    blk, lw, gw, hpg, own, pad = (geo[k] for k in ("blk", "lw", "gw", "hpg", "own", "pad"))
    copies += load_blocks(geo, deal, place, kv, others, k_s, v_s, sems)
    scale = HD**-0.5

    @pl.loop(0, geo["seq"] // KT)
    def _(i):
        cols = pl.ds(pl.multiple_of(i * KT, KT), KT)
        for ref in (dk_t, dv_t, r_t):
            ref[:, cols] = jnp.zeros((gw, KT), F32)

    for copy in copies:
        copy.wait()
    for k in range(groups):
        rows = slice(2 * k * blk, 2 * (k + 1) * blk)
        g_s[rows, :] = jnp.concatenate(
            [unpack(dc_s[k]), jnp.zeros((2 * blk, lw - gw), BF)], axis=1
        )

    @pl.loop(0, own)
    def _(n):
        p = block_at(geo, deal, place, n)
        end = (p + 1) * blk
        mine = pl.ds(pl.multiple_of(n * blk, blk), blk)
        qb = q_s[mine, :].astype(F32) * scale
        wide = g_s[mine, :].astype(F32)
        saved = att[mine, :]
        prod = wide * saved
        lane = lane_iota(blk, lw)
        low = jnp.zeros((blk, lw), F32)
        for h in range(hpg):
            recip = 1.0 / saved[:, gw + h : gw + h + 1]
            only = head_mask(blk, lw, h)
            dtot = -jnp.sum(jnp.where(only, prod, 0.0), axis=1, keepdims=True) * recip
            high = dtot.astype(BF).astype(F32)
            dnum = jnp.where(only, wide * recip, 0.0)
            low += dnum
            aug = jnp.where(lane == gw, high, dnum)
            aug = jnp.where(lane == gw + 1, dtot - high, aug)
            stack = slice(h * blk, (h + 1) * blk)
            augs[stack, :] = aug.astype(BF)
            qm[stack, :] = jnp.where(only, qb, 0.0).astype(BF)
        q_t, dn_t, g_t = qb.astype(BF).T, low.astype(BF).T, g_s[mine, :].T
        qstart = jnp.broadcast_to(starts_of(srow, p, blk), (KT, blk)).T
        qpos = p * blk + row_iota(blk, KT)
        qlim = qpos - ((qpos - qstart) & (SEGL - 1))
        dq_a[...] = jnp.zeros_like(dq_a)

        lead = starts[0, p * blk] // 128 * 128
        count = (end - lead + KT - 1) // KT
        lead = jnp.minimum(lead, geo["seq"] - count * KT)

        @pl.loop(0, count)
        def _(t):
            base = lead + t * KT
            rows = pl.ds(pl.multiple_of(pad + base, 128), KT)
            cols = pl.ds(pl.multiple_of(base, 128), KT)
            kt, vt = k_s[rows, :], v_s[rows, :]
            kpos = base + lane_iota(blk, KT)
            inside = kpos >= qstart
            visible = inside & (kpos <= qpos)
            earlier = inside & (kpos < qlim)
            scores = mm(qm[...], kt, NT)
            dprobs = mm(augs[...], vt, NT)
            dscores = []
            for h in range(hpg):
                part, stack = slice(h * HD, (h + 1) * HD), slice(h * blk, (h + 1) * blk)
                probs = jnp.where(visible, jnp.exp(scores[stack]), 0.0)
                dscores.append((probs * dprobs[stack]).astype(BF))
                dv_t[part, cols] += mm(dn_t[part, :], probs.astype(BF))
                dk_t[part, cols] += mm(q_t[part, :], dscores[h])
            dque = mm(jnp.concatenate(dscores, axis=0), kt)
            dq_a[...] += own_lanes(dque, blk, lw, hpg)
            r_t[:, cols] += mm(g_t[:gw, :], jnp.where(earlier, 1.0, 0.0).astype(BF))

        dq[mine, :] = (dq_a[...] * scale).astype(BF)

    copies = fetch([(dq, dq_h)], out_sems, nblk)
    spread = coef_spread(lw, gw, hpg)

    @pl.loop(0, geo["seq"] // KT)
    def _(t):
        rows = pl.ds(pl.multiple_of(pad + t * KT, KT), KT)
        cols = pl.ds(pl.multiple_of(t * KT, KT), KT)
        fill = jnp.zeros((KT, lw - gw), F32)
        upright = lambda ref: jnp.concatenate([ref[:, cols].T, fill], axis=1)
        reach = upright(r_t)
        lane = lane_iota(KT, lw)
        dval = upright(dv_t) + reach * mm(k_s[rows, :], spread)
        prod = reach * v_s[rows, :].astype(F32)
        for h in range(hpg):
            part = jnp.where(head_mask(KT, lw, h), prod, 0.0)
            dval = jnp.where(lane == gw + h, jnp.sum(part, axis=1, keepdims=True), dval)
        narrow = dk_t[:, cols].astype(BF).T
        dkv[cols, 0:lw] = jnp.concatenate([narrow, fill.astype(BF)], axis=1)
        dkv[cols, lw : 2 * lw] = dval.astype(BF)

    for m in reversed(range(splits)):
        for n in range(m * own, (m + 1) * own):
            at = pl.ds(pl.multiple_of(block_at(geo, deal, place, n) * blk, 64), blk)
            to = pl.ds((n % own) * blk, blk)
            copies += fetch([(dkv.at[at], dkvs_h[m].at[to])], out_sems, n)
    for copy in copies:
        copy.wait()


def assemble_kernel(geo, split, *refs):
    splits, nsh = geo["splits"], geo["nsh"]
    for m in range(splits):
        for i in range(3):
            for z in range(nsh):
                refs[splits + i][z, split[0] ^ m] = refs[m][i, z]


def proj_kernel(geo, comb, wout, x, vecs, resid, n2):
    total = x[...].astype(F32) + vecs[0:1, :]
    for g in range(geo["groups"]):
        total += mm(unpack(comb[g]), wout[g])
    resid[...] = total
    unit, _ = norm_stats(total)
    n2[...] = (unit * vecs[1:2, :] + vecs[2:3, :]).astype(BF)


def ffn_kernel(geo, n2, g, wup, wdn, bias, y, dn2, act, dhid, ysum, dsum):
    fg = geo["fg"]
    ysum[...] = jnp.zeros_like(ysum)
    dsum[...] = jnp.zeros_like(dsum)

    @pl.loop(0, fg // UB)
    def _(b):
        cols = pl.ds(pl.multiple_of(b * UB, UB), UB)
        u = mm(n2[...], wup[:, cols]) + bias[0:1, cols]
        sq = u * u
        th = jnp.tanh(0.7978845608028654 * (u + 0.044715 * sq * u))
        half = 0.5 * (1.0 + th)
        a = (u * half).astype(BF)
        slope = half + 0.5 * u * (1.0 - th * th) * (0.7978845608028654 * (1.0 + 0.134145 * sq))
        d = (slope * mm(g[...], wdn[cols, :], NT)).astype(BF)
        act[:, cols] = a
        dhid[:, cols] = d
        ysum[...] += mm(a, wdn[cols, :])
        dsum[...] += mm(d, wup[:, cols], NT)

    y[...] = ysum[...].astype(BF)
    dn2[...] = dsum[...].astype(BF)


def ffn_grad_kernel(geo, split, *refs):
    groups, splits, nsh, part, parta, tok, fg = (
        geo[k] for k in ("groups", "splits", "nsh", "part", "parta", "tok", "fg")
    )
    n2s, dhids, acts, gs = (refs[i * groups : (i + 1) * groups] for i in range(4))
    outs, dupb, acc = refs[4 * groups : 4 * groups + splits], refs[-2], refs[-1]
    total = jnp.zeros((1, fg), F32)
    for ref in dhids:
        total += jnp.sum(ref[...].astype(F32), axis=0, keepdims=True)
    dupb[...] = jnp.broadcast_to(total, dupb.shape)
    for at, left, right in ((0, n2s, dhids), (parta, acts, gs)):
        flip = jnp.concatenate([ref[...].T for ref in left], axis=1)
        for b in range(0, fg, FB):
            side = jnp.concatenate([ref[:, b : b + FB] for ref in right])
            acc[:, b : b + FB] = mm(flip, side)
        for m in range(splits):
            for z in range(nsh):
                rows = (z * splits + (split[0] ^ m)) * part
                rows = pl.ds(pl.multiple_of(rows, 8), part)
                outs[m][z, at : at + part, :] = acc[rows, :].astype(BF)


def post_kernel(geo, group, *refs):
    groups = geo["groups"]
    dn2s, (wout, resid, g, vecs) = refs[:groups], refs[groups : groups + 4]
    dresid, dproj, small = refs[groups + 4 : groups + 7]
    dcombs = refs[groups + 7 :]
    unit, recip = norm_stats(resid[...])
    dn2 = dn2s[0][...].astype(F32)
    for ref in dn2s[1:]:
        dn2 += ref[...].astype(F32)
    wide = g[...].astype(F32)
    dres = wide + norm_back(dn2, unit, recip, vecs[1:2, :])
    dresid[...] = dres
    low = dres.astype(BF)
    dproj[...] = low
    for k in range(groups):
        dcombs[k][...] = pack(mm(low, wout[group[0] ^ k], NT).astype(BF))
    small[0:1, :] = jnp.sum(low.astype(F32), axis=0, keepdims=True)
    small[1:2, :] = jnp.sum(dn2 * unit, axis=0, keepdims=True)
    small[2:3, :] = jnp.sum(dn2, axis=0, keepdims=True)
    small[3:4, :] = jnp.sum(wide, axis=0, keepdims=True)
    small[4:8, :] = jnp.zeros((4, D), F32)


def out_grad_kernel(geo, here, comb, dproj, out):
    splits, nsh, gw = geo["splits"], geo["nsh"], geo["gw"]
    rows, sub = D // nsh, D // nsh // geo["nctx"]
    for g in range(geo["groups"]):
        value = mm(unpack(comb[g]), dproj[...], TN)
        for r in range(0, gw, sub):
            z, i = (g * gw + r) // rows, (g * gw + r) % rows // sub
            piece = value[r : r + sub, :].astype(BF)
            out[(i % splits) ^ here[1], (i // splits) ^ here[0], z] = piece


def extend_kernel(geo, *refs):
    groups, splits, nsh, tok = (geo[k] for k in ("groups", "splits", "nsh", "tok"))
    ys, grads, outs = refs[: groups - 1], refs[groups - 1 : groups - 1 + splits], refs[-groups:]
    for k in range(groups):
        total = grads[0][0, k].astype(F32)
        for ref in grads[1:]:
            total += ref[k].astype(F32)
        total = total.reshape(nsh * total.shape[1], D).astype(BF)
        if k == 0:
            outs[0][...] = total
        else:
            outs[k][0:tok, :] = ys[k - 1][...]
            outs[k][tok:, :] = total


def sum_kernel(geo, *refs):
    total = refs[0][...].astype(F32)
    for ref in refs[1:-1]:
        total += ref[...].astype(F32)
    refs[-1][...] = total.astype(BF)


def stack_kernel(geo, *refs):
    for k, ref in enumerate(refs[:-1]):
        refs[-1][k] = ref[...]


def late_kernel(geo, here, *refs):
    splits, groups, nsh, fg = (geo[k] for k in ("splits", "groups", "nsh", "fg"))
    sub = D // nsh // geo["nctx"]
    wgs, exts = refs[:splits], refs[splits : splits + groups]
    vec1, small2, dupb = refs[splits + groups : splits + groups + 3]
    outs, (dwout, vec) = refs[splits + groups + 3 : -2], refs[-2:]
    total = exts[0][...].astype(F32)
    for ref in exts[1:]:
        total += ref[geo["tok"] :, :].astype(F32)
    for z in range(nsh):
        dwout[z] = total[z * sub : (z + 1) * sub, :]
    vec[0:6, :] = vec1[0:6, :]
    vec[6:10, :] = small2[0:4, :]
    each, spans = fg // nsh, []
    for z in range(nsh):
        for g in range(groups):
            value = dupb[0:1, z * each : (z + 1) * each]
            spans.append(jnp.where(here[0] == g, value, 0.0))
    per = D // each
    for i in range(len(spans) // per):
        vec[10 + i : 11 + i, :] = jnp.concatenate(spans[i * per : (i + 1) * per], axis=1)
    vec[14:16, :] = jnp.zeros((2, D), F32)
    for k in range(nsh):
        z = here[2] ^ k
        total = wgs[0][z].astype(F32)
        for ref in wgs[1:]:
            total += ref[z].astype(F32)
        outs[k][...] = jnp.concatenate([vec[...], total, dwout[z]], axis=0).astype(BF)


def result_kernel(geo, *refs):
    groups = geo["groups"]
    ys, (resid, vecs, out) = refs[:groups], refs[groups:]
    total = resid[...] + vecs[3:4, :]
    for ref in ys:
        total += ref[0 : geo["tok"], :].astype(F32)
    out[...] = total


def dn1_kernel(geo, dq, *refs):
    splits, groups, tok, lw = (geo[k] for k in ("splits", "groups", "tok", "lw"))
    dkvs, (w, dqkv), parts = refs[:splits], refs[splits : splits + 2], refs[splits + 2 :]
    for k in range(groups):
        rows = slice(k * tok, (k + 1) * tok)
        both = dkvs[0][rows, :].astype(F32)
        for ref in dkvs[1:]:
            both += ref[rows, :].astype(F32)
        dqkv[rows, 0:lw] = dq[rows, :]
        dqkv[rows, lw : 3 * lw] = both.astype(BF)
        parts[k][...] = mm(dqkv[rows, :], w[...], NT).astype(BF)


def wgrad_kernel(geo, group, split, *refs):
    groups, splits, nsh, part, tok, lw, gw, hpg = (
        geo[k] for k in ("groups", "splits", "nsh", "part", "tok", "lw", "gw", "hpg")
    )
    pieces, parts, dqkv = refs[:groups], refs[groups : 2 * groups], refs[2 * groups]
    outs, (vec, acc) = refs[2 * groups + 1 : -2], refs[-2:]
    flip = jnp.concatenate([ref[0:tok, :].T for ref in pieces], axis=1)
    for b in range(0, 3 * lw, lw):
        acc[:, b : b + lw] = mm(flip, dqkv[:, b : b + lw])
    for m in range(splits):
        for z in range(nsh):
            rows = pl.ds(pl.multiple_of((z * splits + (split[0] ^ m)) * part, 8), part)
            for t in range(3):
                value = pack(acc[rows, t * lw : t * lw + gw])
                outs[m][z, :, t * lw : (t + 1) * lw] = value.astype(BF)
    plain = jnp.zeros((1, D), F32)
    cross = jnp.zeros((1, D), F32)
    means = jnp.zeros((HP, 128), F32)
    spreads = jnp.zeros((HP, 128), F32)
    for k in range(groups):
        dn1 = parts[k][...].astype(F32)
        plain += jnp.sum(dn1, axis=0, keepdims=True)
        cross += jnp.sum(dn1 * pieces[k][0:tok, :].astype(F32), axis=0, keepdims=True)
        dcoef = dqkv[k * tok : (k + 1) * tok, 3 * lw - 128 :]
        means += mm(pieces[k][tok : tok + HP, tok : 2 * tok], dcoef)
        spreads += mm(pieces[k][tok + HP : tok + 2 * HP, 0:tok], dcoef)
    total = jnp.sum(dqkv[...].astype(F32), axis=0, keepdims=True)
    vec[0:1, :] = cross
    vec[1:2, :] = plain
    head = row_iota(HP, 128) - group[0] * hpg
    hit = (head >= 0) & (head < hpg) & (lane_iota(HP, 128) == 128 - (lw - gw) + head)
    across = row_iota(HP, D) == lane_iota(HP, D)
    for i, value in enumerate((means, spreads)):
        value = jnp.sum(jnp.where(hit, value, 0.0), axis=1, keepdims=True)
        value = jnp.sum(jnp.where(across, value, 0.0), axis=0, keepdims=True)
        vec[4 + i : 5 + i, :] = value
    for i, t in enumerate((0, 2)):
        mine = total[:, t * lw : t * lw + gw]
        for g in range(groups):
            vec[2 + i : 3 + i, g * gw : (g + 1) * gw] = jnp.where(group[0] == g, mine, 0.0)
    vec[6:8, :] = jnp.zeros((2, D), F32)


def tail_kernel(geo, *refs):
    groups = geo["groups"]
    parts = refs[:groups]
    x, dresid, vecs, grad = refs[groups:]
    dn1 = parts[0][...].astype(F32)
    for ref in parts[1:]:
        dn1 += ref[...].astype(F32)
    unit, recip = norm_stats(x[...].astype(F32))
    grad[...] = dresid[...] + norm_back(dn1, unit, recip, vecs[4:5, :])


def finish_kernel(geo, ups, downs, up_g, down_g):
    groups, splits, nsh, part, fg, rows = (
        geo[k] for k in ("groups", "splits", "nsh", "part", "fg", "rows")
    )
    each = fg // nsh
    for i in range(groups * splits):
        g, c = i // splits, i % splits
        value = ups[i, 0:part, :].astype(F32)
        for z in range(nsh):
            at = z * groups * each + g * each
            up_g[c * part : (c + 1) * part, at : at + each] = value[:, z * each : (z + 1) * each]
        at = g * each + c * part
        down_g[at : at + part, :] = downs[i, 0:part, :].astype(F32)


def finish_in_kernel(geo, place, *refs):
    groups, splits, part, gw, lw = (geo[k] for k in ("groups", "splits", "part", "gw", "lw"))
    near, far, vecs = refs[:groups], refs[groups : groups + splits - 1], refs[-14]
    outs = refs[-13:]
    in_g, out_g = outs[:2]
    group, split = place[0] // splits, place[0] % splits
    prow = part * 3 // 4
    total = jnp.zeros((HP, D), F32)
    for k in range(groups):
        for m in range(splits):
            value = (near[k][...] if m == 0 else far[m - 1][k]).astype(F32)
            total += value[0:HP, :]
            out_g[place[0] ^ (k * splits + m)] = value[HP + prow :, :]
            rows = pl.ds(pl.multiple_of((split ^ m) * part, 8), part)
            wide = [unpack(value[HP : HP + prow, t * lw : (t + 1) * lw]) for t in range(3)]
            for g in range(groups):

                @pl.when((group ^ k) == g)
                def _():
                    for t in range(3):
                        in_g[rows, t * D + g * gw : t * D + (g + 1) * gw] = wide[t]

    flat = lambda i, n=D: total[i : i + 1, 0:n].reshape(n)
    outs[2][...] = ((total[0:1, :] - vecs[5:6, :] * total[1:2, :]) / vecs[4:5, :]).reshape(D)
    for ref, i in zip(outs[3:10], (1, 2, 3, 6, 7, 8, 9)):
        ref[...] = flat(i)
    outs[10][...] = flat(4, H)
    outs[11][...] = flat(5, H)
    for i in range(4):
        outs[12][i * D : (i + 1) * D] = flat(10 + i)


def full(shape):
    return pl.BlockSpec(shape, lambda *_: (0,) * len(shape))


ANY = pl.BlockSpec(memory_space=pl.ANY)
DMA = pltpu.SemaphoreType.DMA


def call(kernel, geo, scalars, grid, ins, in_specs, outs, out_specs, scratch, flops, moved, exps=0, limit=12):
    return pl.pallas_call(
        functools.partial(kernel, geo),
        grid_spec=pltpu.PrefetchScalarGridSpec(
            num_scalar_prefetch=len(scalars),
            grid=grid,
            in_specs=in_specs,
            out_specs=out_specs,
            scratch_shapes=scratch,
        ),
        out_shape=[jax.ShapeDtypeStruct(s, t) for s, t in outs],
        compiler_params=pltpu.CompilerParams(vmem_limit_bytes=limit << 20),
        cost_estimate=pl.CostEstimate(flops=1000, bytes_accessed=1000, transcendentals=0),
    )(*scalars, *ins)


def per_device(
    inputs,
    out_grad,
    segment_ids,
    doc_starts,
    deal_table,
    ridge_matrix,
    first_gain,
    first_shift,
    mixer_in,
    query_bias,
    value_bias,
    mixer_out,
    out_bias,
    second_gain,
    second_shift,
    up_weight,
    up_bias,
    down_weight,
    down_bias,
    memory_mean,
    memory_spread,
):
    tok = inputs.shape[1]
    blk = tok // 2
    nctx, nsh = lax.axis_size("ctx"), lax.axis_size("shard")
    place = lax.axis_index("ctx").astype(jnp.int32)
    seq, nblk = tok * nctx, 2 * nctx
    groups = math.gcd(H, nctx)
    splits = nctx // groups
    hpg = H // groups
    gw = hpg * HD
    lw = -(-(gw + hpg) // 128) * 128
    own = 2 * groups
    group, split = place // splits, place % splits
    ff = up_weight.shape[1]
    fg = ff // groups
    each = fg // nsh
    rows = D // nsh
    part = rows // splits
    parta = -(-part // 16) * 16
    sub = rows // nctx
    qrows = groups * tok
    geo = dict(
        tok=tok, blk=blk, seq=seq, nblk=nblk, groups=groups, splits=splits, hpg=hpg, gw=gw, lw=lw,
        own=own, pad=KT, nctx=nctx, nsh=nsh, fg=fg, rows=rows, part=part, parta=parta,
    )
    x = inputs[0]
    upstream = out_grad[0]
    peers = range(groups)
    across = lambda v, k: v if k == 0 else swap(v, "ctx", nctx, k * splits)
    inside = lambda v, m: swap(v, "ctx", nctx, m)
    gidx, sidx = group.reshape(1), split.reshape(1)
    vm = pltpu.VMEM
    zero = lambda n: jnp.zeros((n, D), F32)
    vrow = full((D,))
    tokd, square = full((tok, D)), full((D, D))

    prow = tok + 2 * HP
    (payload,) = call(
        prep_kernel, geo, (), (1,),
        (x, first_gain, first_shift, ridge_matrix, memory_mean, memory_spread),
        [tokd, vrow, vrow, full((tok, NB)), full((H,)), full((H,))],
        [((prow, D), BF)], [full((prow, D))], [], tok * D * 10, tok * D * 6,
    )
    pieces = [across(payload, k) for k in peers]

    w_mine = jnp.concatenate(
        [
            jnp.pad(
                lax.dynamic_slice_in_dim(mixer_in, t * D + group * gw, gw, 1),
                ((0, 0), (0, lw - gw)),
            )
            for t in range(3)
        ],
        axis=1,
    )
    w_mine, _ = lax.optimization_barrier((w_mine, payload))
    w_parts = swap_pieces(w_mine, "shard", nsh)

    up_rows = lax.dynamic_slice_in_dim(up_weight, split * part, part)
    up_mine = jnp.concatenate(
        [
            lax.dynamic_slice_in_dim(up_rows, z * (ff // nsh) + group * each, each, 1)
            for z in range(nsh)
        ],
        axis=1,
    )
    down_mine = lax.dynamic_slice_in_dim(down_weight, group * each + split * part, part)
    out_mine = lax.dynamic_slice_in_dim(mixer_out, split * part, part)
    trio = jnp.stack([up_mine, down_mine, out_mine])
    trio, _ = lax.optimization_barrier((trio, (w_parts, pieces)))
    trio = lax.all_gather(trio, "shard", axis=1)

    pidx = place.reshape(1)
    tables = (deal_table, doc_starts, pidx)

    vectors = (out_bias, second_gain, second_shift, down_bias, first_gain, first_shift)
    here = jnp.stack([group, split, lax.axis_index("shard").astype(jnp.int32)])
    vrows = full((8, D))
    q, kv, w_group, vecs, up_b = call(
        qkv_kernel, geo, (here,), (1,),
        (*pieces, *w_parts, query_bias, value_bias, up_bias, *vectors),
        [full((prow, D))] * groups + [full((rows, 3 * lw))] * nsh + [vrow] * 2 + [full((ff,))]
        + [vrow] * len(vectors),
        [((qrows, lw), BF), ((qrows, 2 * lw), BF), ((D, 3 * lw), BF), ((8, D), F32),
         ((8, fg), F32)],
        [full((qrows, lw)), full((qrows, 2 * lw)), full((D, 3 * lw)), vrows, full((8, fg))],
        [], qrows * D * 6 * lw, qrows * D * 4, 0, 16,
    )
    others = [inside(kv, m) for m in range(1, splits)]
    upstream_later, _ = lax.optimization_barrier((upstream, q))
    planes = [[g * splits + c for g in peers] for c in range(splits)]
    gs = [upstream if k == 0 else across(upstream_later, k) for k in peers]

    wide = (seq + KT, lw)
    sems = pltpu.SemaphoreType.DMA((2 * nblk,))
    tiles = qrows * seq // 2
    moved = (3 * qrows + 3 * seq) * lw * 2
    comb, att = call(
        attn_fwd_kernel, geo, tables, (1,),
        (q, kv, *others, doc_starts),
        [full((qrows, lw))] + [ANY] * splits + [full((1, seq))],
        [((groups, tok * 3 // 4, 256), BF), ((qrows, lw), F32)],
        [full((groups, tok * 3 // 4, 256)), full((qrows, lw))],
        [vm(wide, BF)] * 3
        + [vm((qrows, lw), BF), vm((blk, lw), F32), vm((blk, lw), F32), sems],
        tiles * lw * 2 * (2 * hpg + 1), moved, tiles * hpg, 6 + seq // 512,
    )
    comb, gs, trio = lax.optimization_barrier((comb, gs, trio))
    trios = [trio if m == 0 else inside(trio, m) for m in range(splits)]
    w_up, w_down, w_out = call(
        assemble_kernel, geo, (sidx,), (1,), trios, [full((3, nsh, part, D))] * splits,
        [((nsh, splits, part, D), BF)] * 3, [full((nsh, splits, part, D))] * 3,
        [], 1000, 1000, 0, 16,
    )
    w_up, w_down, w_out = (w.reshape(D, D) for w in (w_up, w_down, w_out))
    w_out = w_out.reshape(groups, gw, D)
    trade = lambda v: lax.all_to_all(v, "ctx", 0, 0, axis_index_groups=planes, tiled=True)
    comb = trade(comb)

    resid, n2 = call(
        proj_kernel, geo, (), (1,), (comb, w_out, x, vecs),
        [full((groups, tok * 3 // 4, 256)), full((groups, gw, D)), tokd, vrows],
        [((tok, D), F32), ((tok, D), BF)], [tokd, tokd],
        [], tok * D * D * 2, tok * D * 12,
    )
    ys, dn2s, acts, dhids = [], [], [], []
    n2s = [n2]
    for k in peers:
        if k == 1:
            n2s += [across(n2, m) for m in range(1, groups - 1)]
            n2s = list(lax.optimization_barrier((*n2s, ys[0]))[:-1])
            n2s.append(across(n2, groups - 1))
        outs = call(
            ffn_kernel, geo, (), (1,), (n2s[k], gs[k], w_up, w_down, up_b),
            [tokd, tokd, square, square, full((8, fg))],
            [((tok, D), BF)] * 4, [tokd] * 4,
            [vm((tok, D), F32), vm((tok, D), F32)], tok * D * fg * 8, tok * D * 12 + D * fg * 4, tok * fg,
        )
        ys.append(outs[0])
        dn2s.append(across(outs[1], k))
        acts.append(outs[2])
        dhids.append(outs[3])
    dresid, dproj, small2, *dcombs = call(
        post_kernel, geo, (gidx,), (1,), (*dn2s, w_out, resid, upstream, vecs),
        [tokd] * groups + [full((groups, gw, D)), tokd, tokd, vrows],
        [((tok, D), F32), ((tok, D), BF), ((8, D), F32)]
        + [((tok * 3 // 4, 256), BF)] * groups,
        [tokd, tokd, full((8, D))] + [full((tok * 3 // 4, 256))] * groups,
        [], tok * D * D * 2, tok * D * 20,
    )
    dcombs = [across(dcombs[k], k) for k in peers]
    *dms, dupb = call(
        ffn_grad_kernel, geo, (sidx,), (1,), (*n2s, *dhids, *acts, *gs),
        [tokd] * (4 * groups),
        [((nsh, 2 * parta, D), BF)] * splits + [((8, fg), F32)],
        [full((nsh, 2 * parta, D))] * splits + [full((8, fg))],
        [vm((D, D), F32)], qrows * D * fg * 4, qrows * D * 8,
    )
    (dwout,) = call(
        out_grad_kernel, geo, (here,), (1,), (comb, dproj),
        [full((groups, tok * 3 // 4, 256)), tokd],
        [((splits, groups, nsh, sub, D), BF)], [full((splits, groups, nsh, sub, D))],
        [], tok * D * D * 2, tok * D * 6,
    )
    dwouts = [dwout] + [inside(dwout[m], m) for m in range(1, splits)]
    dms = [dms[0]] + [inside(dms[m], m) for m in range(1, splits)]
    (dm,) = call(
        sum_kernel, geo, (), (1,), dms, [full((nsh, 2 * parta, D))] * splits,
        [((nsh, 2 * parta, D), BF)], [full((nsh, 2 * parta, D))], [], 1000, 1000,
    )
    dm, dwouts, dcombs = lax.optimization_barrier((dm, dwouts, dcombs))
    erow = tok + nsh * sub
    exts = call(
        extend_kernel, geo, (), (1,), (*ys[1:], *dwouts),
        [tokd] * (groups - 1)
        + [pl.BlockSpec((1, groups, nsh, sub, D), lambda *_: (0, 0, 0, 0, 0))]
        + [full((groups, nsh, sub, D))] * (splits - 1),
        [((nsh * sub, D), BF)] + [((erow, D), BF)] * (groups - 1),
        [full((nsh * sub, D))] + [full((erow, D))] * (groups - 1),
        [], 1000, 1000,
    )
    dms, _ = lax.optimization_barrier((dms, dproj))
    dm = lax.psum_scatter(dm, "shard", scatter_dimension=0, tiled=False)

    dq, *dkvs = call(
        attn_bwd_kernel, geo, tables, (1,),
        (q, kv, *others, doc_starts, *dcombs, att),
        [ANY] * (splits + 1) + [full((1, seq))] + [ANY] * (groups + 1),
        [((qrows, lw), BF)] + [((qrows, 2 * lw), BF)] * splits,
        [ANY] * (splits + 1),
        [vm(wide, BF)] * 2
        + [vm((qrows, lw), BF), vm((blk, lw), F32)] + [vm((gw, seq), F32)] * 3
        + [vm((qrows, lw), BF), vm((qrows, lw), F32), vm((groups, tok * 3 // 4, 256), BF),
           vm((qrows, lw), BF), vm((seq, 2 * lw), BF), vm((hpg * blk, lw), BF),
           vm((hpg * blk, lw), BF), DMA((2 * nblk + 2 + groups,)),
           DMA((nblk + 1,))],
        tiles * lw * 2 * (5 * hpg + 1), moved, tiles * hpg, 60,
    )
    later, _ = lax.optimization_barrier((exts, dcombs))
    exts = [across(later[k], k) for k in peers]
    dkvs, exts, dm = lax.optimization_barrier((dkvs, exts, dm))
    dkvs = [dkvs[0]] + [inside(dkvs[m], m) for m in range(1, splits)]
    m_g = lax.all_gather(dm, "ctx", axis=0)
    (result,) = call(
        result_kernel, geo, (), (1,), (ys[0], *exts[1:], resid, vecs),
        [tokd] + [full((erow, D))] * (groups - 1) + [tokd, vrows], [((tok, D), F32)], [tokd],
        [], tok * D * 8, tok * D * 16,
    )
    dqkv, *parts = call(
        dn1_kernel, geo, (), (1,), (dq, *dkvs, w_group),
        [full((qrows, lw))] + [full((qrows, 2 * lw))] * splits + [full((D, 3 * lw))],
        [((qrows, 3 * lw), BF)] + [((tok, D), BF)] * groups,
        [full((qrows, 3 * lw))] + [tokd] * groups,
        [], qrows * D * 6 * lw, qrows * D * 8, 0, 60,
    )
    mine = parts
    parts = [across(parts[k], k) for k in peers]

    prow = part * 3 // 4
    *wgs, vec1 = call(
        wgrad_kernel, geo, (gidx, sidx), (1,), (*pieces, *mine, dqkv),
        [full((tok + 2 * HP, D))] * groups + [tokd] * groups + [full((qrows, 3 * lw))],
        [((nsh, prow, 3 * lw), BF)] * splits + [((8, D), F32)],
        [full((nsh, prow, 3 * lw))] * splits + [full((8, D))],
        [vm((D, 3 * lw), F32)], qrows * D * 6 * lw, qrows * D * 4, 0, 60,
    )
    wgs = [wgs[0]] + [inside(wgs[m], m) for m in range(1, splits)]
    lrow = HP + prow + sub
    lates = call(
        late_kernel, geo, (here,), (1,), (*wgs, *exts, vec1, small2, dupb),
        [full((nsh, prow, 3 * lw))] * splits + [full((nsh * sub, D))]
        + [full((erow, D))] * (groups - 1) + [full((8, D)), full((8, D)), full((8, fg))],
        [((lrow, D), BF)] * nsh, [full((lrow, D))] * nsh,
        [vm((nsh, sub, D), F32), vm((HP, D), F32)], 1000, 1000,
    )
    zs = [lates[k] if k == 0 else swap(lates[k], "shard", nsh, k) for k in range(nsh)]
    (zsum,) = call(
        sum_kernel, geo, (), (1,), zs, [full((lrow, D))] * nsh,
        [((lrow, D), BF)], [full((lrow, D))], [], 1000, 1000,
    )
    zsum, parts, result = lax.optimization_barrier((zsum, parts, result))
    near = [across(zsum, k) for k in peers]
    (input_grad,) = call(
        tail_kernel, geo, (), (1,), (*parts, x, dresid, vecs),
        [tokd] * (groups + 2) + [vrows], [((tok, D), F32)], [tokd],
        [], tok * D * 20, tok * D * 20,
    )
    gblock = lambda r: pl.BlockSpec((nctx, parta, D), lambda j, *_: (0, r, 0))
    up_g, down_g = call(
        finish_kernel, geo, (), (1,), (m_g, m_g), [gblock(0), gblock(1)],
        [((rows, ff), F32), ((ff // nsh, D), F32)],
        [full((rows, ff)), full((ff // nsh, D))],
        [], 1000, rows * ff * 12,
    )
    near, input_grad, up_g = lax.optimization_barrier((near, input_grad, up_g))
    (stacked,) = call(
        stack_kernel, geo, (), (1,), near, [full((lrow, D))] * groups,
        [((groups, lrow, D), BF)], [full((groups, lrow, D))], [], 1000, 1000,
    )
    far = [inside(stacked, m) for m in range(1, splits)]
    in_g, out_g, gain_g, shift_g, qb_g, vb_g, ob_g, gain2_g, shift2_g, db_g, mean_g, spread_g, ub_g = call(
        finish_in_kernel, geo, (pidx,), (1,),
        (*near, *far, vecs),
        [full((lrow, D))] * groups + [full((groups, lrow, D))] * (splits - 1) + [vrows],
        [((rows, 3 * D), F32), ((nctx, sub, D), F32)] + [((D,), F32)] * 8
        + [((H,), F32)] * 2 + [((ff,), F32)],
        [full((rows, 3 * D)), full((nctx, sub, D))] + [vrow] * 8 + [full((H,))] * 2
        + [full((ff,))],
        [], 1000, rows * D * 20,
    )
    out_g = out_g.reshape(rows, D)
    small = (
        gain_g, shift_g, qb_g, vb_g, ob_g, gain2_g, shift2_g, ub_g, db_g, mean_g, spread_g
    )
    return (result[None], input_grad[None], in_g, out_g, up_g, down_g) + small


def solution(mesh):
    rows, split = P("shard", None), P("shard", "ctx", None)
    none = P()
    return jax.shard_map(
        per_device,
        mesh=mesh,
        in_specs=(
            split, split, rows, rows, none, P("ctx", None), none, none, rows, none, none, rows,
            none, none, none, rows, none, rows, none, none, none,
        ),
        out_specs=(split, split, rows, rows, rows, rows) + (none,) * 11,
        check_vma=False,
    )
```
